32 devices in a mesh: rep: 4 (over y, core), shard: 8 (over z, x).
Axes of the slice: x: 2, y: 2, z: 4, core: 2. Of those that a mesh axis runs over, the one named last changes fastest.
Arguments:
- layer_input: bfloat16 [32, 197, 768], P(('rep', 'shard')), may hold values from -6 to 6
- cotangent: bfloat16 [32, 197, 768], P(('rep', 'shard')), may hold values from -6 to 6
- live: int32 [32], P(('rep', 'shard')), may hold values 0 or 1
- first_gain: bfloat16 [768], P('shard'), may hold values from 0.099609375 to 1.8984375
- first_bias: bfloat16 [768], P('shard'), may hold values from -3 to 3
- qkv_weight: bfloat16 [768, 2304], P('shard'), may hold values from -0.21875 to 0.21875
- query_bias: bfloat16 [768], P('shard'), may hold values from -3 to 3
- value_bias: bfloat16 [768], P('shard'), may hold values from -3 to 3
- out_weight: bfloat16 [768, 768], P('shard'), may hold values from -1.5 to 1.5
- out_bias: bfloat16 [768], P('shard'), may hold values from -3 to 3
- second_gain: bfloat16 [768], P('shard'), may hold values from 0.099609375 to 1.8984375
- second_bias: bfloat16 [768], P('shard'), may hold values from -3 to 3
- up_weight: bfloat16 [768, 3072], P('shard'), may hold values from -0.21875 to 0.21875
- up_bias: bfloat16 [3072], P('shard'), may hold values from -3 to 3
- down_weight: bfloat16 [3072, 768], P('shard'), may hold values from -0.109375 to 0.109375
- down_bias: bfloat16 [768], P('shard'), may hold values from -3 to 3
Outputs:
- output: bfloat16 [32, 197, 768], P(('rep', 'shard'))
- input_grad: bfloat16 [32, 197, 768], P(('rep', 'shard'))
- first_gain_grad: float32 [768], P('shard')
- first_bias_grad: float32 [768], P('shard')
- qkv_weight_grad: float32 [768, 2304], P('shard')
- query_bias_grad: float32 [768], P('shard')
- value_bias_grad: float32 [768], P('shard')
- out_weight_grad: float32 [768, 768], P('shard')
- out_bias_grad: float32 [768], P('shard')
- second_gain_grad: float32 [768], P('shard')
- second_bias_grad: float32 [768], P('shard')
- up_weight_grad: float32 [768, 3072], P('shard')
- up_bias_grad: float32 [3072], P('shard')
- down_weight_grad: float32 [3072, 768], P('shard')
- down_bias_grad: float32 [768], P('shard')
The draws below stay inside these ranges and needn't reach their ends.
All inputs are finite; a program needn't handle non-finite values. No bound on the sum of `live` on one device may be relied on, other than what follows from the above.
Results may differ from the reference program's by a relative error of at most 0.014.
Values may be sent and summed in bfloat16 or wider, within the bound.
A program may use at most 128 MiB of HBM per device.

```python
import jax
import jax.numpy as jnp
from jax import lax

D = 768
FF = 3072
HEAD_DIM = 64
SEQ = 197
IMAGES = 32


def set_ends(values, own_key, smallest, top_value):
    extent = values.shape
    place = [jax.random.randint(jax.random.fold_in(own_key, axis), (), 0, extent[axis]) for axis in range(len(extent))]
    values = values.at[tuple(place)].set(smallest)
    longest = extent.index(max(extent))
    place[longest] = (place[longest] + 1) % extent[longest]
    return values.at[tuple(place)].set(top_value)


def level_of(own_key, dims, pieces, low, largest):
    gain = 1.0
    for dim, parts in pieces:
        draws = jax.random.uniform(jax.random.fold_in(jax.random.fold_in(own_key, 6), dim), (parts,), jnp.float32, low / len(pieces), largest / len(pieces))
        gain = gain * jnp.repeat(jnp.exp(draws), dims[dim] // parts).reshape((-1,) + (1,) * (len(dims) - 1 - dim))
    return gain


def gaussian(key, extent, scale, bound, shards=(), held_as=jnp.bfloat16):
    entries = scale * jax.random.normal(key, extent, jnp.float32)
    if shards:
        entries = entries * level_of(key, extent, shards, -0.22, 0.18)
    return jnp.clip(entries, -bound, bound).astype(held_as)


def setup_inputs(seed: int = 0) -> dict:
    key_of = jax.random.split(jax.random.key(seed), 17)
    return {
        "layer_input": gaussian(key_of[0], (IMAGES, SEQ, D), 1.0, 6.0, ((0, 32),)),
        "cotangent": gaussian(key_of[1], (IMAGES, SEQ, D), 1.0, 6.0, ((0, 32),)),
        "live": set_ends((jax.random.randint(key_of[2], (IMAGES,), 0, 4) < 3).astype(jnp.int32), jax.random.fold_in(key_of[2], 1), 0, 1),
        "first_gain": jnp.clip(1.0 + 0.18 * jax.random.normal(key_of[3], (D,), jnp.float32), 0.099609375, 1.8984375).astype(jnp.bfloat16),
        "first_bias": gaussian(key_of[4], (D,), 0.5, 3.0, ((0, 8),)),
        "qkv_weight": gaussian(key_of[5], (D, 3 * D), D ** -0.5, 0.21875, ((0, 8),)),
        "query_bias": gaussian(key_of[6], (D,), 0.5, 3.0, ((0, 8),)),
        "value_bias": gaussian(key_of[7], (D,), 0.5, 3.0, ((0, 8),)),
        "out_weight": gaussian(key_of[8], (D, D), (D // 48) ** -0.5, 1.5, ((0, 8),)),
        "out_bias": gaussian(key_of[9], (D,), 0.5, 3.0, ((0, 8),)),
        "second_gain": jnp.clip(1.0 + 0.18 * jax.random.normal(key_of[10], (D,), jnp.float32), 0.099609375, 1.8984375).astype(jnp.bfloat16),
        "second_bias": gaussian(key_of[11], (D,), 0.5, 3.0, ((0, 8),)),
        "up_weight": gaussian(key_of[12], (D, FF), D ** -0.5, 0.21875, ((0, 8),)),
        "up_bias": gaussian(key_of[13], (FF,), 0.5, 3.0, ((0, 8),)),
        "down_weight": gaussian(key_of[14], (FF, D), FF ** -0.5, 0.109375, ((0, 8),)),
        "down_bias": gaussian(key_of[15], (D,), 0.5, 3.0, ((0, 8),)),
    }


norm_eps = 1e-06
root_half = 0.7071067811865476
density_coef = 0.3989422804014327

def matmul(operand, factor):
    flat = operand.reshape(-1, operand.shape[-1])
    product = jnp.dot(flat, factor, preferred_element_type=jnp.float32)
    return product.reshape(operand.shape[:-1] + (factor.shape[-1],))

def outer_product(operand, factor):
    return jnp.dot(operand.reshape(-1, operand.shape[-1]).T, factor.reshape(-1, factor.shape[-1]), preferred_element_type=jnp.float32)

def batched(form, operand, factor):
    return jnp.einsum(form, operand.astype(jnp.float32), factor.astype(jnp.float32))

def layer_norm(values, norm_gain, norm_bias):
    average = lax.optimization_barrier(jnp.mean(values, axis=-1, keepdims=True))
    centred = values - average
    spread = lax.optimization_barrier(jnp.mean(centred * centred, axis=-1, keepdims=True))
    inv_std = lax.rsqrt(spread + norm_eps)
    hat_vals = centred * inv_std
    return (hat_vals * norm_gain.astype(jnp.float32) + norm_bias.astype(jnp.float32), hat_vals, inv_std)

def norm_back(incoming, hat_vals, inv_std, norm_gain):
    scaled = incoming * norm_gain.astype(jnp.float32)
    return inv_std * (scaled - lax.optimization_barrier(jnp.mean(scaled, axis=-1, keepdims=True)) - hat_vals * lax.optimization_barrier(jnp.mean(scaled * hat_vals, axis=-1, keepdims=True)))

def block_pass(params, layer_input, cotangent, live):
    first_gain, first_bias, qkv_weight, query_bias, value_bias, out_weight, out_bias, second_gain, second_bias, up_weight, up_bias, down_weight, down_bias = params
    images, length, model_width = layer_input.shape
    head_count = model_width // HEAD_DIM
    score_scale = HEAD_DIM ** (-0.5)
    stream = layer_input.astype(jnp.float32)
    normed, first_hat, first_inv = layer_norm(stream, first_gain, first_bias)
    normed = normed.astype(jnp.bfloat16)
    projected = matmul(normed, qkv_weight)
    shape_heads = (images, length, head_count, HEAD_DIM)
    queries = (projected[..., :model_width] + query_bias.astype(jnp.float32)).astype(jnp.bfloat16).reshape(shape_heads)
    key_rows = projected[..., model_width:2 * model_width].astype(jnp.bfloat16).reshape(shape_heads)
    values = (projected[..., 2 * model_width:] + value_bias.astype(jnp.float32)).astype(jnp.bfloat16).reshape(shape_heads)
    scores = batched('bqhd,bkhd->bhqk', queries, key_rows) * score_scale
    log_total = jnp.log(lax.optimization_barrier(jnp.sum(jnp.exp(scores), axis=-1, keepdims=True)))
    weights = jnp.exp(scores - log_total).astype(jnp.bfloat16)
    attended = batched('bhqk,bkhd->bqhd', weights, values).reshape(images, length, model_width).astype(jnp.bfloat16)
    middle = stream + matmul(attended, out_weight) + out_bias.astype(jnp.float32)
    second_normed, second_hat, second_inv = layer_norm(middle, second_gain, second_bias)
    second_normed = second_normed.astype(jnp.bfloat16)
    hidden_pre = matmul(second_normed, up_weight) + up_bias.astype(jnp.float32)
    normal_cdf = 0.5 * (1.0 + lax.erf(hidden_pre * root_half))
    hidden = (hidden_pre * normal_cdf).astype(jnp.bfloat16)
    result = middle + matmul(hidden, down_weight) + down_bias.astype(jnp.float32)
    image_mask = live.astype(jnp.float32)[:, None, None]
    output = (result * image_mask).astype(jnp.bfloat16)
    upstream = cotangent.astype(jnp.float32) * image_mask
    upstream_low = upstream.astype(jnp.bfloat16)
    down_weight_grad = outer_product(hidden, upstream_low)
    down_bias_grad = lax.optimization_barrier(jnp.sum(upstream, axis=(0, 1)))
    hidden_grad = matmul(upstream_low, down_weight.T)
    density = jnp.exp(-0.5 * hidden_pre * hidden_pre) * density_coef
    pre_grad = hidden_grad * (normal_cdf + hidden_pre * density)
    pre_low = pre_grad.astype(jnp.bfloat16)
    up_weight_grad = outer_product(second_normed, pre_low)
    up_bias_grad = lax.optimization_barrier(jnp.sum(pre_grad, axis=(0, 1)))
    second_in = matmul(pre_low, up_weight.T)
    second_gain_grad = lax.optimization_barrier(jnp.sum(second_in * second_hat, axis=(0, 1)))
    second_bias_grad = lax.optimization_barrier(jnp.sum(second_in, axis=(0, 1)))
    middle_grad = upstream + norm_back(second_in, second_hat, second_inv, second_gain)
    middle_low = middle_grad.astype(jnp.bfloat16)
    out_weight_grad = outer_product(attended, middle_low)
    out_bias_grad = lax.optimization_barrier(jnp.sum(middle_grad, axis=(0, 1)))
    attended_grad = matmul(middle_low, out_weight.T).astype(jnp.bfloat16).reshape(shape_heads)
    again_scores = batched('bqhd,bkhd->bhqk', queries, key_rows) * score_scale
    probs = jnp.exp(again_scores - log_total)
    probs_low = probs.astype(jnp.bfloat16)
    value_grad = batched('bhqk,bqhd->bkhd', probs_low, attended_grad)
    prob_grad = batched('bqhd,bkhd->bhqk', attended_grad, values)
    score_grad = (probs * (prob_grad - lax.optimization_barrier(jnp.sum(probs * prob_grad, axis=-1, keepdims=True))) * score_scale).astype(jnp.bfloat16)
    query_grad = batched('bhqk,bkhd->bqhd', score_grad, key_rows)
    key_grad = batched('bhqk,bqhd->bkhd', score_grad, queries)
    flat_shape = (images, length, model_width)
    query_grad = query_grad.reshape(flat_shape)
    value_grad = value_grad.reshape(flat_shape)
    joined = jnp.concatenate([query_grad, key_grad.reshape(flat_shape), value_grad], axis=-1).astype(jnp.bfloat16)
    qkv_weight_grad = outer_product(normed, joined)
    query_bias_grad = lax.optimization_barrier(jnp.sum(query_grad, axis=(0, 1)))
    value_bias_grad = lax.optimization_barrier(jnp.sum(value_grad, axis=(0, 1)))
    first_in = matmul(joined, qkv_weight.T)
    first_gain_grad = lax.optimization_barrier(jnp.sum(first_in * first_hat, axis=(0, 1)))
    first_bias_grad = lax.optimization_barrier(jnp.sum(first_in, axis=(0, 1)))
    input_grad = (middle_grad + norm_back(first_in, first_hat, first_inv, first_gain)).astype(jnp.bfloat16)
    grads = (first_gain_grad, first_bias_grad, qkv_weight_grad, query_bias_grad, value_bias_grad, out_weight_grad, out_bias_grad, second_gain_grad, second_bias_grad, up_weight_grad, up_bias_grad, down_weight_grad, down_bias_grad)
    return (output, input_grad, grads)

def reference(layer_input, cotangent, live, first_gain, first_bias, qkv_weight, query_bias, value_bias, out_weight, out_bias, second_gain, second_bias, up_weight, up_bias, down_weight, down_bias):
    params = (first_gain, first_bias, qkv_weight, query_bias, value_bias, out_weight, out_bias, second_gain, second_bias, up_weight, up_bias, down_weight, down_bias)
    blocks = IMAGES // 16
    inputs_blocked = layer_input.reshape(blocks, 16, SEQ, D)
    cot_blocked = cotangent.reshape(blocks, 16, SEQ, D)
    live_blocked = live.reshape(blocks, 16)

    def advance(totals, item):
        output, input_grad, grads = block_pass(params, item[0], item[1], item[2])
        return (tuple((total + grad for total, grad in zip(totals, grads))), (output, input_grad))
    zeros = tuple((jnp.zeros(param.shape, jnp.float32) for param in params))
    totals, (outputs, input_grads) = lax.scan(advance, zeros, (inputs_blocked, cot_blocked, live_blocked))
    return (outputs.reshape(IMAGES, SEQ, D), input_grads.reshape(IMAGES, SEQ, D), totals[0], totals[1], totals[2], totals[3], totals[4], totals[5], totals[6], totals[7], totals[8], totals[9], totals[10], totals[11], totals[12])
```

```python
import functools

import jax
import jax.numpy as jnp
from jax import lax
from jax.experimental import pallas as pl
from jax.experimental.pallas import tpu as pltpu
from jax.sharding import PartitionSpec as P

HEAD_DIM = 64
LANES = 128
NORM_EPS = 1e-06
ROOT_HALF = 0.7071067811865476
DENSITY_COEF = 0.3989422804014327
MESH = pl.DeviceIdType.MESH
F32 = jnp.float32
LOW = jnp.bfloat16

QKV, OUT, UP, DOWN = range(4)
SHARED, MINE, YOURS = range(3)


def ring_index(position, n):
    half = position // (n // 2)
    return (1 - half) * 2 * position + half * (2 * (n - 1 - position) + 1)


def ring_position(index, n):
    odd = index % 2
    step = index // 2
    return (1 - odd) * step + odd * (n - 1 - step)


def remote(source, target, send, recv, device):
    return pltpu.make_async_remote_copy(
        src_ref=source,
        dst_ref=target,
        send_sem=send,
        recv_sem=recv,
        device_id=device,
        device_id_type=MESH,
    )


def dot_nn(a, b):
    return jnp.dot(a, b, preferred_element_type=F32)


def dot_nt(a, b):
    return lax.dot_general(a, b, (((1,), (1,)), ((), ())), preferred_element_type=F32)


def dot_tn(a, b):
    return lax.dot_general(a, b, (((0,), (0,)), ((), ())), preferred_element_type=F32)


def split(refs, counts):
    at = 0
    for count in counts:
        yield refs[at : at + count]
        at += count


def layer_kernel(n, length, padded, model, *refs):
    ins, outs, weights, acts, halves, given, over, arrive_a, arrive_b, extra, sems = split(
        refs, (8, 7, 4, 23, 4, 4, 4, 4, 4, 4 + 6, 25)
    )
    x_in, cot_in, live_in, qkv_in, out_in, up_in, down_in, line_in = ins
    output_ref, input_grad_ref, *sums, line_out = outs
    (
        x_low,
        cot_low,
        upstream,
        hat1,
        inv1,
        normed,
        normed_t,
        qkv,
        probs,
        attended,
        attended_t,
        middle,
        hat2,
        inv2,
        second,
        second_t,
        hidden,
        hidden_t,
        pre_low,
        slope,
        incoming,
        middle_low,
        vec_grad,
    ) = acts
    joined, middle_grad, head_grad = qkv, middle, normed
    exchange, (lines, vec, up_bias, line_grad, line_a, line_b) = extra[:4], extra[4:]
    (
        in_sem,
        own_sem,
        ring_s,
        ring_r,
        row_s,
        row_r,
        core_s,
        core_r,
        line_s,
        line_r,
        give_s,
        give_r,
        over_s,
        over_r,
        sum_s,
        sum_r,
        end_s,
        end_r,
        tail_s,
        tail_r,
        pair_s,
        pair_r,
    ) = sems[:22]
    line_pair = sems[22]
    pre_bias, score_rows = sems[23], sems[24]

    rows = qkv_in.shape[0]
    height = [ref.shape[0] for ref in (qkv_in, out_in, up_in, down_in)]
    sixth = [ref.shape[1] // 6 for ref in (qkv_in, out_in, up_in, down_in)]
    matrix_in = (qkv_in, out_in, up_in, down_in)
    hidden_units = up_in.shape[1]
    reach = (n // 2, n // 2 - 1)

    rep = lax.axis_index("rep")
    me = lax.axis_index("shard")
    core = rep % 2
    row = rep // 2
    position = ring_position(me, n)
    sign = 1 - 2 * core

    def at(k):
        return ring_index((position + sign * k + n) % n, n)

    peers = ((rep, at(1)), (rep, at(-1)))
    partner = (row * 2 + 1 - core, me)
    across = ((1 - row) * 2 + core, me)
    third = (2, row, 1 - row)

    def block(m, b):
        return pl.ds(pl.multiple_of(b * height[m], height[m]), height[m])

    def columns(m, slot, whose):
        width = sixth[m]
        return pl.ds(pl.multiple_of((2 * third[slot] + whose) * width, width), width)

    def piece(m, b, slot):
        return weights[m].at[block(m, b), columns(m, slot, core)]

    def came(d, h):
        return at(-1 - h) if d == 0 else at(1 + h)

    def own_copy(m, slot):
        return pltpu.make_async_copy(
            matrix_in[m].at[:, columns(m, slot, core)], piece(m, me, slot), own_sem.at[m, slot]
        )

    def gather_send(m, slot, d, h):
        view = piece(m, at(-h) if d == 0 else at(h), slot)
        return remote(view, view, ring_s.at[m, slot, d, h], ring_r.at[m, slot, d, h], peers[d])

    def gather_row(m, d, h, slot):
        view = piece(m, came(d, h), slot)
        k = d * reach[0] + h
        return remote(view, view, row_s.at[m, k], row_r.at[m, k], across)

    def gather_core(m, slot, whose):
        view = weights[m].at[:, columns(m, slot, whose)]
        return remote(view, view, core_s.at[m, slot], core_r.at[m, slot], partner)

    def gather_start(m):
        for slot in (MINE, SHARED):
            for d in (0, 1):
                gather_send(m, slot, d, 0).start()

    def gather_hop(m, h, slots=(MINE, SHARED)):
        for slot in slots:
            for d in (0, 1):
                if h < reach[d]:
                    view = piece(m, came(d, h), slot)
                    remote(
                        view, view, ring_s.at[m, slot, d, h], ring_r.at[m, slot, d, h], peers[d]
                    ).wait_recv()
                    if h + 1 < reach[d]:
                        gather_send(m, slot, d, h + 1).start()
                    if slot == MINE:
                        gather_row(m, d, h, MINE).start()

    def gather_relay(m):
        for slot in (MINE, SHARED):
            gather_core(m, slot, core).start()

    def gather_end(m):
        for d in (0, 1):
            for h in range(reach[d]):
                gather_row(m, d, h, YOURS).wait_recv()
        gather_core(m, YOURS, core).start()
        for slot in (MINE, SHARED, YOURS):
            gather_core(m, slot, 1 - core).wait_recv()

    def line_send(d, h):
        view = lines.at[at(-h) if d == 0 else at(h)]
        return remote(view, view, line_s.at[d, h], line_r.at[d, h], peers[d])

    def line_hop(h):
        for d in (0, 1):
            if h < reach[d]:
                view = lines.at[came(d, h)]
                remote(view, view, line_s.at[d, h], line_r.at[d, h], peers[d]).wait_recv()
                if h + 1 < reach[d]:
                    line_send(d, h + 1).start()

    def give(m, slot):
        return remote(
            halves[m].at[1, slot],
            given[m].at[slot],
            give_s.at[m, slot],
            give_r.at[m, slot],
            partner,
        )

    def send_over(m):
        return remote(halves[m].at[0, YOURS], over[m], over_s.at[m], over_r.at[m], across)

    def local(m, slot, b):
        total = halves[m][0, slot, block(m, b)].astype(F32) + given[m][slot, block(m, b)].astype(
            F32
        )
        if slot == MINE:
            total = total + over[m][block(m, b)].astype(F32)
        return total

    def ring_sum(m, slot, d, t):
        b = at(reach[0] - t) if d == 0 else at(t - reach[1])
        arrive = (arrive_a, arrive_b)[d]
        return remote(
            halves[m].at[0, slot, block(m, b)],
            arrive[m].at[slot, t],
            sum_s.at[m, slot, d, t],
            sum_r.at[m, slot, d, t],
            peers[d],
        )

    def reduce_give(m, slot):
        give(m, slot).start()

    def reduce_over(m):
        give(m, YOURS).wait_recv()

        def body(b, carry):
            halves[m][0, YOURS, block(m, b)] = local(m, YOURS, b).astype(LOW)
            return carry

        lax.fori_loop(0, n, body, 0)
        send_over(m).start()

    def reduce_step(m, slot, t):
        if t == 0:
            give(m, slot).wait_recv()
            if slot == MINE:
                send_over(m).wait_recv()
        for d in (0, 1):
            if t < reach[d]:
                b = at(reach[0] - t) if d == 0 else at(t - reach[1])
                total = local(m, slot, b)
                if t > 0:
                    ring_sum(m, slot, d, t - 1).wait_recv()
                    total = total + (arrive_a, arrive_b)[d][m][slot, t - 1].astype(F32)
                halves[m][0, slot, block(m, b)] = total.astype(LOW)
                ring_sum(m, slot, d, t).start()

    def end_view(m, slot, whose):
        return sums[m].at[:, columns(m, slot, whose)]

    def end_copy(m, k, source, target, peer):
        return remote(source, target, end_s.at[m, k], end_r.at[m, k], peer)

    def reduce_end(m, slot):
        total = local(m, slot, me)
        for d in (0, 1):
            if reach[d]:
                ring_sum(m, slot, d, reach[d] - 1).wait_recv()
                total = total + (arrive_a, arrive_b)[d][m][slot, reach[d] - 1].astype(F32)
        if slot == MINE:
            sums[m][:, columns(m, MINE, core)] = total.astype(LOW)
            view = end_view(m, MINE, core)
            end_copy(m, 0, view, view, across).start()
            end_copy(m, 1, view, view, partner).start()
        else:
            halves[m][0, SHARED, block(m, me)] = total.astype(LOW)
            end_copy(m, 2, halves[m].at[0, SHARED, block(m, me)], exchange[m], across).start()

    def reduce_exchange(m):
        end_copy(m, 2, halves[m].at[0, SHARED, block(m, me)], exchange[m], across).wait_recv()
        total = halves[m][0, SHARED, block(m, me)].astype(F32) + exchange[m][...].astype(F32)
        sums[m][:, columns(m, SHARED, core)] = total.astype(LOW)
        view = end_view(m, SHARED, core)
        end_copy(m, 3, view, view, partner).start()
        view = end_view(m, YOURS, core)
        end_copy(m, 0, view, view, across).wait_recv()
        end_copy(m, 4, view, view, partner).start()

    def reduce_finish(m):
        for k, slot in ((1, MINE), (3, SHARED), (4, YOURS)):
            view = end_view(m, slot, 1 - core)
            end_copy(m, k, view, view, partner).wait_recv()

    steps = padded // 16
    slices = [pl.ds(i * 16, 16) for i in range(steps)]
    gain = lambda i: vec[i : i + 1, :]
    live = live_in[0].astype(F32)
    row_id = lax.broadcasted_iota(jnp.int32, (padded, 1), 0)
    row_mask = (row_id < length).astype(F32)
    pair_width = 2 * HEAD_DIM
    pairs = model // pair_width

    def normalise(source, hat, inv):
        for s in slices:
            values = source[s, :]
            centred = values - jnp.mean(values, axis=-1, keepdims=True)
            spread = jnp.mean(centred * centred, axis=-1, keepdims=True)
            inv_std = lax.rsqrt(spread + NORM_EPS)
            hat[s, :] = centred * inv_std
            inv[s, :] = jnp.broadcast_to(inv_std, (16, LANES))

    def scale_shift(hat, low, g, b, mask):
        for i, s in enumerate(slices):
            value = hat[s, :] * gain(g) + gain(b)
            if mask and (i + 1) * 16 > length:
                value = value * row_mask[i * 16 : (i + 1) * 16]
            low[s, :] = value.astype(LOW)

    def transpose(source, target):
        def body(i, carry):
            cols = pl.ds(pl.multiple_of(i * 256, 256), 256)
            target[cols, :] = source[:, cols].T
            return carry

        lax.fori_loop(0, source.shape[1] // 256, body, 0)

    def begin():
        middle[...] = jnp.zeros_like(middle)
        middle[:length, :] = x_low[0].astype(F32)
        incoming[...] = jnp.zeros_like(incoming)
        incoming[:length, :] = cot_low[0].astype(F32) * live
        upstream[...] = incoming[...].astype(LOW)
        vec_grad[...] = jnp.zeros_like(vec_grad)
        vec_grad[7:8, :] = jnp.sum(incoming[...], axis=0, keepdims=True)
        normalise(middle, hat1, inv1)

    def vectors():
        for b in range(n):
            held = lines[b].astype(F32)
            vec[:, b * rows : (b + 1) * rows] = held[:, :rows]
            for e in range(4):
                first = (b * 4 + e) * rows
                up_bias[:, first : first + rows] = jnp.broadcast_to(
                    held[8 + e : 9 + e, :rows], (8, rows)
                )

    def first_norm():
        scale_shift(hat1, normed, 0, 1, True)
        transpose(normed, normed_t)
        zero = jnp.zeros((1, model), F32)
        for k, v in enumerate((vec[2:3, :], zero, vec[3:4, :])):
            pre_bias[:, k * model : (k + 1) * model] = jnp.broadcast_to(v, (8, model))

    def project(first, last):
        wide = 2 * sixth[QKV] // 2

        def body(c, carry):
            cols = pl.ds(pl.multiple_of(c * wide, wide), wide)
            value = (dot_nn(normed[...], weights[QKV][:, cols]) + pre_bias[0:1, cols]) * row_mask
            factor = jnp.where(c * wide < model, HEAD_DIM**-0.5, 1.0)
            qkv[:, cols] = (value.astype(LOW).astype(F32) * factor).astype(LOW)
            return carry

        lax.fori_loop(first, last, body, 0)

    lane = lax.broadcasted_iota(jnp.int32, (padded, pair_width), 1)
    low_lane = lane < HEAD_DIM
    key_mask = lax.broadcasted_iota(jnp.int32, (1, padded), 1) < length

    def heads(part, p):
        return qkv[:, pl.ds(pl.multiple_of(part * model + p * pair_width, LANES), pair_width)]

    def stacked(value, target):
        wide = value.astype(F32)
        target[:padded, :] = jnp.where(low_lane, wide, 0.0).astype(LOW)
        target[padded:, :] = jnp.where(low_lane, 0.0, wide).astype(LOW)

    def merged(value):
        return jnp.where(low_lane, value[:padded], value[padded:])

    def attend(first, last):
        def body(p, carry):
            stacked(heads(0, p), score_rows.at[0])
            scores = dot_nt(score_rows[0], heads(1, p))
            powers = jnp.where(key_mask, jnp.exp(scores), 0.0)
            total = jnp.sum(powers, axis=-1, keepdims=True)
            weight = (powers * (1.0 / total)).astype(LOW)
            probs[p] = weight
            cols = pl.ds(pl.multiple_of(p * pair_width, LANES), pair_width)
            attended[:, cols] = merged(dot_nn(weight, heads(2, p))).astype(LOW)
            return carry

        lax.fori_loop(first, last, body, 0)

    def mix():
        def body(c, carry):
            cols = pl.ds(pl.multiple_of(c * 256, 256), 256)
            middle[:, cols] = (
                middle[:, cols] + dot_nn(attended[...], weights[OUT][:, cols]) + vec[4:5, cols]
            )
            return carry

        lax.fori_loop(0, model // 256, body, 0)
        normalise(middle, hat2, inv2)
        scale_shift(hat2, second, 5, 6, False)

    def transposes():
        transpose(attended, attended_t)
        transpose(second, second_t)

    wide_hidden = 512

    def expand(first, last):
        def body(c, carry):
            cols = pl.ds(pl.multiple_of(c * wide_hidden, wide_hidden), wide_hidden)
            pre = dot_nn(second[...], weights[UP][:, cols]) + up_bias[0:1, cols]
            cdf = 0.5 * (1.0 + lax.erf(pre * ROOT_HALF))
            density = jnp.exp(-0.5 * pre * pre) * DENSITY_COEF
            value = (pre * cdf).astype(LOW)
            hidden[:, cols] = value
            slope[:, cols] = cdf + pre * density
            hidden_t[cols, :] = value.T
            return carry

        lax.fori_loop(first, last, body, 0)

    def contract():
        def body(c, carry):
            cols = pl.ds(pl.multiple_of(c * 256, 256), 256)
            value = dot_nn(hidden[...], weights[DOWN][:, cols]) + vec[7:8, cols]
            value = (middle[:, cols] + value) * live
            output_ref[0, :, cols] = value[:length].astype(LOW)
            return carry

        lax.fori_loop(0, model // 256, body, 0)

    def gradient(m, left, right, slot):
        width = sixth[m]
        base = third[slot] * 2 * width
        if width % 256 == 0:
            count, step = 2 * width // 256, 256
        elif (2 * width) % 256 == 0 and width < 256:
            count, step = 1, 2 * width
        else:
            count, step = 2, width
        tall = left.shape[0]
        high = min(tall, model)

        def body(i, carry):
            c, r = i % count, i // count
            cols = pl.ds(pl.multiple_of(base + c * step, LANES), step)
            down = pl.ds(pl.multiple_of(r * high, high), high)
            value = dot_nn(left[down, :], right[:, cols]).astype(LOW)
            if step > width:
                for whose in range(2):
                    halves[m][(whose + core) % 2, slot, down] = value[
                        :, whose * width : (whose + 1) * width
                    ]
            else:
                per = width // step
                start = pl.multiple_of((c % per) * step, LANES)
                halves[m][(c // per + core) % 2, slot, down, pl.ds(start, step)] = value
            return carry

        lax.fori_loop(0, count * (tall // high), body, 0)
        reduce_give(m, slot)

    def hidden_back(first, last):
        def body(c, carry):
            cols = pl.ds(pl.multiple_of(c * wide_hidden, wide_hidden), wide_hidden)
            value = dot_nt(upstream[...], weights[DOWN][cols, :]) * slope[:, cols]
            up_bias[:, cols] = jnp.broadcast_to(
                jnp.sum(value, axis=0, keepdims=True), (8, wide_hidden)
            )
            pre_low[:, cols] = value.astype(LOW)
            return carry

        lax.fori_loop(first, last, body, 0)

    def second_back():
        def body(c, carry):
            cols = pl.ds(pl.multiple_of(c * 256, 256), 256)
            incoming[:, cols] = dot_nt(pre_low[...], weights[UP][cols, :])
            return carry

        lax.fori_loop(0, model // 256, body, 0)

    def norm_back(hat, inv, g, add):
        gain_sum = jnp.zeros((1, model), F32)
        bias_sum = jnp.zeros((1, model), F32)
        add_sum = jnp.zeros((1, model), F32)
        for s in slices:
            came_in = incoming[s, :]
            hat_vals = hat[s, :]
            scaled = came_in * gain(g)
            average = jnp.mean(scaled, axis=-1, keepdims=True)
            along = jnp.mean(scaled * hat_vals, axis=-1, keepdims=True)
            value = add[s, :].astype(F32) + inv[s, 0:1] * (scaled - average - hat_vals * along)
            gain_sum += jnp.sum(came_in * hat_vals, axis=0, keepdims=True)
            bias_sum += jnp.sum(came_in, axis=0, keepdims=True)
            add_sum += jnp.sum(value, axis=0, keepdims=True)
            middle_grad[s, :] = value
            middle_low[s, :] = value.astype(LOW)
        vec_grad[g : g + 1, :] = gain_sum
        vec_grad[g + 1 : g + 2, :] = bias_sum
        return add_sum

    def attended_back():
        def body(c, carry):
            cols = pl.ds(pl.multiple_of(c * 256, 256), 256)
            head_grad[:, cols] = dot_nt(middle_low[...], weights[OUT][cols, :]).astype(LOW)
            return carry

        lax.fori_loop(0, model // 256, body, 0)

    def attend_back(first, last):
        def body(p, carry):
            start = pl.multiple_of(p * pair_width, LANES)
            cols = pl.ds(start, pair_width)
            stacked(head_grad[:, cols], score_rows.at[1])
            stacked(heads(0, p), score_rows.at[0])
            weight = probs[p]
            value_grad = dot_tn(weight, score_rows[1])
            prob_grad = dot_nt(score_rows[1], heads(2, p))
            wide = weight.astype(F32)
            along = jnp.sum(wide * prob_grad, axis=-1, keepdims=True)
            score_grad = (wide * (prob_grad - along)).astype(LOW)
            query_grad = merged(dot_nn(score_grad, heads(1, p))) * HEAD_DIM**-0.5
            key_grad = dot_tn(score_grad, score_rows[0])
            vec_grad[2:3, cols] = jnp.sum(query_grad, axis=0, keepdims=True)
            vec_grad[3:4, cols] = jnp.sum(value_grad, axis=0, keepdims=True)
            for k, value in enumerate((query_grad, key_grad, value_grad)):
                joined[:, pl.ds(pl.multiple_of(k * model + start, LANES), pair_width)] = (
                    value.astype(LOW)
                )
            return carry

        lax.fori_loop(first, last, body, 0)

    def first_back():
        def body(c, carry):
            cols = pl.ds(pl.multiple_of(c * 256, 256), 256)
            incoming[:, cols] = dot_nt(joined[...], weights[QKV][cols, :])
            return carry

        lax.fori_loop(0, model // 256, body, 0)

    def tail_local():
        line_grad[...] = jnp.zeros_like(line_grad)
        for b in range(n):
            line_grad[b, 0:8, 0:rows] = vec_grad[0:8, b * rows : (b + 1) * rows]
            for e in range(4):
                first = (b * 4 + e) * rows
                line_grad[b, 8 + e : 9 + e, 0:rows] = up_bias[0:1, first : first + rows]

    def tail_sum(d, t):
        b = at(reach[0] - t) if d == 0 else at(t - reach[1])
        arrive = (line_a, line_b)[d]
        return remote(line_grad.at[b], arrive.at[t], tail_s.at[d, t], tail_r.at[d, t], peers[d])

    def tail_step(t):
        for d in (0, 1):
            if t < reach[d]:
                b = at(reach[0] - t) if d == 0 else at(t - reach[1])
                if t > 0:
                    tail_sum(d, t - 1).wait_recv()
                    line_grad[b] = line_grad[b] + (line_a, line_b)[d][t - 1]
                tail_sum(d, t).start()

    def pair_copy(k, peer):
        return remote(
            line_pair.at[2 * k], line_pair.at[2 * k + 1], pair_s.at[k], pair_r.at[k], peer
        )

    def tail_end():
        total = line_grad[me]
        for d in (0, 1):
            if reach[d]:
                tail_sum(d, reach[d] - 1).wait_recv()
                total = total + (line_a, line_b)[d][reach[d] - 1]
        line_pair[0] = total
        pair_copy(0, across).start()

    def tail_pair():
        pair_copy(0, across).wait_recv()
        line_pair[2] = line_pair[0] + line_pair[1]
        pair_copy(1, partner).start()

    def tail_finish():
        pair_copy(1, partner).wait_recv()
        line_out[...] = line_pair[2] + line_pair[3]

    line_copy = pltpu.make_async_copy(line_in, lines.at[me], in_sem.at[0])
    x_copy = pltpu.make_async_copy(x_in, x_low, in_sem.at[1])
    cot_copy = pltpu.make_async_copy(cot_in, cot_low, in_sem.at[2])
    line_copy.start()
    for m in range(4):
        for slot in (MINE, SHARED, YOURS):
            own_copy(m, slot).start()
    x_copy.start()
    cot_copy.start()

    barrier = pltpu.get_barrier_semaphore()
    for peer in (*peers, partner, across):
        pl.semaphore_signal(barrier, inc=1, device_id=peer, device_id_type=MESH)
    pl.semaphore_wait(barrier, 4)

    line_copy.wait()
    for d in (0, 1):
        line_send(d, 0).start()
    for slot in (MINE, SHARED, YOURS):
        own_copy(QKV, slot).wait()
    gather_start(QKV)
    for m in (OUT, UP, DOWN):
        for slot in (MINE, SHARED, YOURS):
            own_copy(m, slot).wait()
    gather_start(OUT)
    x_copy.wait()
    cot_copy.wait()
    begin()
    for h in range(reach[0]):
        line_hop(h)
        gather_hop(QKV, h)
        gather_hop(OUT, h)
        if h == reach[0] - 2:
            gather_start(UP)
    gather_relay(QKV)
    gather_relay(OUT)
    vectors()
    first_norm()
    gather_end(QKV)

    def gather_part(m, part, parts):
        for h in range(reach[0] * part // parts, reach[0] * (part + 1) // parts):
            gather_hop(m, h)
            if m == UP and h == reach[0] - 2:
                gather_start(DOWN)

    project(0, 6)
    gather_part(UP, 0, 4)
    attend(0, 2)
    gather_part(UP, 1, 4)
    attend(2, 4)
    gather_part(UP, 2, 4)
    attend(4, pairs)
    gather_end(OUT)
    gather_part(UP, 3, 4)
    gather_relay(UP)
    mix()
    gather_end(UP)
    transposes()
    expand(0, 2)
    gather_part(DOWN, 0, 4)
    expand(2, 4)
    gather_part(DOWN, 1, 4)
    expand(4, 6)
    gather_part(DOWN, 2, 4)
    for slot in (YOURS, SHARED, MINE):
        gradient(DOWN, hidden_t, upstream, slot)
    gather_part(DOWN, 3, 4)
    gather_relay(DOWN)
    reduce_over(DOWN)
    gather_end(DOWN)

    def reduce_steps(m, first, last):
        for t in range(first, last):
            for slot in (SHARED, MINE):
                reduce_step(m, slot, t)

    def ring_part(m, part, parts):
        reduce_steps(m, reach[0] * part // parts, reach[0] * (part + 1) // parts)

    def reduce_last(m):
        for slot in (SHARED, MINE):
            reduce_end(m, slot)

    ring_part(DOWN, 0, 4)
    hidden_back(0, hidden_units // wide_hidden)
    contract()
    ring_part(DOWN, 1, 4)
    for slot in (YOURS, SHARED, MINE):
        gradient(UP, second_t, pre_low, slot)
    reduce_over(UP)
    ring_part(DOWN, 2, 4)
    ring_part(UP, 0, 4)
    second_back()
    ring_part(DOWN, 3, 4)
    vec_grad[4:5, :] = norm_back(hat2, inv2, 5, upstream)
    reduce_last(DOWN)
    for slot in (YOURS, SHARED, MINE):
        gradient(OUT, attended_t, middle_low, slot)
    reduce_over(OUT)
    ring_part(UP, 1, 4)
    attended_back()
    reduce_exchange(DOWN)
    ring_part(OUT, 0, 4)
    attend_back(0, 2)
    ring_part(UP, 2, 4)
    ring_part(OUT, 1, 4)
    attend_back(2, 4)
    ring_part(UP, 3, 4)
    ring_part(OUT, 2, 4)
    attend_back(4, pairs)
    ring_part(OUT, 3, 4)
    reduce_last(UP)
    for slot in (YOURS, SHARED, MINE):
        gradient(QKV, normed_t, joined, slot)
    reduce_over(QKV)
    reduce_last(OUT)
    reduce_exchange(UP)
    reduce_exchange(OUT)
    ring_part(QKV, 0, 4)
    first_back()
    norm_back(hat1, inv1, 0, middle_grad)
    input_grad_ref[0] = middle_grad[:length, :].astype(LOW)
    tail_local()
    ring_part(QKV, 1, 4)
    for part in range(4):
        for t in range(reach[0] * part // 4, reach[0] * (part + 1) // 4):
            tail_step(t)
        if part < 2:
            ring_part(QKV, 2 + part, 4)
    tail_end()
    reduce_last(QKV)
    tail_pair()
    reduce_exchange(QKV)
    tail_finish()
    for m in range(4):
        reduce_finish(m)

    for m in range(4):
        for slot in (SHARED, MINE, YOURS):
            gather_core(m, slot, core).wait_send()
            give(m, slot).wait_send()
        send_over(m).wait_send()
        for d in (0, 1):
            for h in range(reach[d]):
                gather_row(m, d, h, MINE).wait_send()
                for slot in (SHARED, MINE):
                    gather_send(m, slot, d, h).wait_send()
                    ring_sum(m, slot, d, h).wait_send()
        view = end_view(m, MINE, core)
        for k in (0, 1, 3, 4):
            end_copy(m, k, view, view, partner).wait_send()
        end_copy(m, 2, halves[m].at[0, SHARED, block(m, me)], exchange[m], across).wait_send()
    for d in (0, 1):
        for h in range(reach[d]):
            line_send(d, h).wait_send()
            tail_sum(d, h).wait_send()
    pair_copy(0, across).wait_send()
    pair_copy(1, partner).wait_send()


def run_layer(layer_input, cotangent, live, matrices, line, n):
    images, length, model = layer_input.shape
    padded = -(-length // 16) * 16
    hidden_units = matrices[UP].shape[1]
    vmem, dma = pltpu.VMEM, pltpu.SemaphoreType.DMA
    reach = (n // 2, n // 2 - 1)
    height = [a.shape[0] for a in matrices]
    sixth = [a.shape[1] // 6 for a in matrices]
    pairs = model // (2 * HEAD_DIM)
    wide = (padded, model)
    scratch = [vmem((n * a.shape[0], a.shape[1]), LOW) for a in matrices]
    scratch += [
        vmem((1, length, model), LOW),
        vmem((1, length, model), LOW),
        vmem(wide, LOW),
        vmem(wide, F32),
        vmem((padded, LANES), F32),
        vmem(wide, LOW),
        vmem((model, padded), LOW),
        vmem((padded, 3 * model), LOW),
        vmem((pairs, 2 * padded, padded), LOW),
        vmem(wide, LOW),
        vmem((model, padded), LOW),
        vmem(wide, F32),
        vmem(wide, F32),
        vmem((padded, LANES), F32),
        vmem(wide, LOW),
        vmem((model, padded), LOW),
        vmem((padded, hidden_units), LOW),
        vmem((hidden_units, padded), LOW),
        vmem((padded, hidden_units), LOW),
        vmem((padded, hidden_units), F32),
        vmem(wide, F32),
        vmem(wide, LOW),
        vmem((16, model), F32),
    ]
    scratch += [vmem((2, 3, n * r, w), LOW) for r, w in zip(height, sixth)]
    scratch += [vmem((3, n * r, w), LOW) for r, w in zip(height, sixth)]
    scratch += [vmem((n * r, w), LOW) for r, w in zip(height, sixth)]
    scratch += [vmem((2, reach[0], r, w), LOW) for r, w in zip(height, sixth)]
    scratch += [vmem((2, max(reach[1], 1), r, w), LOW) for r, w in zip(height, sixth)]
    scratch += [vmem((r, w), LOW) for r, w in zip(height, sixth)]
    scratch += [
        vmem((n,) + line.shape, LOW),
        vmem((16, model), F32),
        vmem((8, hidden_units), F32),
        vmem((n,) + line.shape, F32),
        vmem((reach[0],) + line.shape, F32),
        vmem((max(reach[1], 1),) + line.shape, F32),
    ]
    scratch += [
        dma((3,)),
        dma((4, 3)),
        dma((4, 2, 2, reach[0])),
        dma((4, 2, 2, reach[0])),
        dma((4, n - 1)),
        dma((4, n - 1)),
        dma((4, 3)),
        dma((4, 3)),
        dma((2, reach[0])),
        dma((2, reach[0])),
        dma((4, 3)),
        dma((4, 3)),
        dma((4,)),
        dma((4,)),
        dma((4, 2, 2, reach[0])),
        dma((4, 2, 2, reach[0])),
        dma((4, 5)),
        dma((4, 5)),
        dma((2, reach[0])),
        dma((2, reach[0])),
        dma((2,)),
        dma((2,)),
        vmem((4,) + line.shape, F32),
        vmem((8, 3 * model), F32),
        vmem((2, 2 * padded, 2 * HEAD_DIM), LOW),
    ]
    anywhere = pl.BlockSpec(memory_space=pl.ANY)
    near = pl.BlockSpec(memory_space=pltpu.VMEM)
    return pl.pallas_call(
        functools.partial(layer_kernel, n, length, padded, model),
        out_shape=[jax.ShapeDtypeStruct(layer_input.shape, LOW)] * 2
        + [jax.ShapeDtypeStruct(a.shape, LOW) for a in matrices]
        + [jax.ShapeDtypeStruct(line.shape, F32)],
        in_specs=[anywhere] * 2 + [pl.BlockSpec(memory_space=pltpu.SMEM)] + [anywhere] * 5,
        out_specs=[near] * 7,
        scratch_shapes=scratch,
        compiler_params=pltpu.CompilerParams(
            collective_id=0, has_side_effects=True, vmem_limit_bytes=60 * 1024 * 1024
        ),
        name="layer",
    )(layer_input, cotangent, live, *matrices, line)


norm_eps = 1e-06
root_half = 0.7071067811865476
density_coef = 0.3989422804014327


def matmul(operand, factor):
    flat = operand.reshape(-1, operand.shape[-1])
    product = jnp.dot(flat, factor, preferred_element_type=jnp.float32)
    return product.reshape(operand.shape[:-1] + (factor.shape[-1],))


def outer_product(operand, factor):
    return jnp.dot(
        operand.reshape(-1, operand.shape[-1]).T,
        factor.reshape(-1, factor.shape[-1]),
        preferred_element_type=jnp.float32,
    )


def batched(form, operand, factor):
    return jnp.einsum(form, operand, factor, preferred_element_type=jnp.float32)


def layer_norm(values, norm_gain, norm_bias):
    average = jnp.mean(values, axis=-1, keepdims=True)
    centred = values - average
    spread = jnp.mean(centred * centred, axis=-1, keepdims=True)
    inv_std = lax.rsqrt(spread + norm_eps)
    hat_vals = centred * inv_std
    return (
        hat_vals * norm_gain.astype(jnp.float32) + norm_bias.astype(jnp.float32),
        hat_vals,
        inv_std,
    )


def norm_back(incoming, hat_vals, inv_std, norm_gain):
    scaled = incoming * norm_gain.astype(jnp.float32)
    return inv_std * (
        scaled
        - jnp.mean(scaled, axis=-1, keepdims=True)
        - hat_vals * jnp.mean(scaled * hat_vals, axis=-1, keepdims=True)
    )


def forward_pass(params, layer_input, live):
    (
        first_gain,
        first_bias,
        qkv_weight,
        query_bias,
        value_bias,
        out_weight,
        out_bias,
        second_gain,
        second_bias,
        up_weight,
        up_bias,
        down_weight,
        down_bias,
    ) = params
    images, length, model_width = layer_input.shape
    head_count = model_width // HEAD_DIM
    score_scale = HEAD_DIM ** (-0.5)
    stream = layer_input.astype(jnp.float32)
    normed, first_hat, first_inv = layer_norm(stream, first_gain, first_bias)
    normed = normed.astype(jnp.bfloat16)
    projected = matmul(normed, qkv_weight)
    shape_heads = (images, length, head_count, HEAD_DIM)
    queries = (
        (projected[..., :model_width] + query_bias.astype(jnp.float32))
        .astype(jnp.bfloat16)
        .reshape(shape_heads)
    )
    key_rows = (
        projected[..., model_width : 2 * model_width].astype(jnp.bfloat16).reshape(shape_heads)
    )
    values = (
        (projected[..., 2 * model_width :] + value_bias.astype(jnp.float32))
        .astype(jnp.bfloat16)
        .reshape(shape_heads)
    )
    scores = batched("bqhd,bkhd->bhqk", queries, key_rows) * score_scale
    log_total = jnp.log(jnp.sum(jnp.exp(scores), axis=-1, keepdims=True))
    weights = jnp.exp(scores - log_total).astype(jnp.bfloat16)
    attended = (
        batched("bhqk,bkhd->bqhd", weights, values)
        .reshape(images, length, model_width)
        .astype(jnp.bfloat16)
    )
    middle = stream + matmul(attended, out_weight) + out_bias.astype(jnp.float32)
    second_normed, second_hat, second_inv = layer_norm(middle, second_gain, second_bias)
    second_normed = second_normed.astype(jnp.bfloat16)
    hidden_pre = matmul(second_normed, up_weight) + up_bias.astype(jnp.float32)
    normal_cdf = 0.5 * (1.0 + lax.erf(hidden_pre * root_half))
    hidden = (hidden_pre * normal_cdf).astype(jnp.bfloat16)
    result = middle + matmul(hidden, down_weight) + down_bias.astype(jnp.float32)
    image_mask = live.astype(jnp.float32)[:, None, None]
    output = (result * image_mask).astype(jnp.bfloat16)
    saved = (
        normed,
        first_hat,
        first_inv,
        queries,
        key_rows,
        values,
        log_total,
        attended,
        second_normed,
        second_hat,
        second_inv,
        hidden_pre,
        normal_cdf,
        hidden,
        image_mask,
    )
    return (output, saved)


def backward_pass(params, saved, cotangent):
    (
        first_gain,
        first_bias,
        qkv_weight,
        query_bias,
        value_bias,
        out_weight,
        out_bias,
        second_gain,
        second_bias,
        up_weight,
        up_bias,
        down_weight,
        down_bias,
    ) = params
    (
        normed,
        first_hat,
        first_inv,
        queries,
        key_rows,
        values,
        log_total,
        attended,
        second_normed,
        second_hat,
        second_inv,
        hidden_pre,
        normal_cdf,
        hidden,
        image_mask,
    ) = saved
    images, length, head_count, head_width = queries.shape
    flat_shape = (images, length, head_count * head_width)
    score_scale = HEAD_DIM ** (-0.5)
    upstream = cotangent.astype(jnp.float32) * image_mask
    upstream_low = upstream.astype(jnp.bfloat16)
    down_weight_grad = outer_product(hidden, upstream_low)
    down_bias_grad = jnp.sum(upstream, axis=(0, 1))
    hidden_grad = matmul(upstream_low, down_weight.T)
    density = jnp.exp(-0.5 * hidden_pre * hidden_pre) * density_coef
    pre_grad = hidden_grad * (normal_cdf + hidden_pre * density)
    pre_low = pre_grad.astype(jnp.bfloat16)
    up_weight_grad = outer_product(second_normed, pre_low)
    up_bias_grad = jnp.sum(pre_grad, axis=(0, 1))
    second_in = matmul(pre_low, up_weight.T)
    second_gain_grad = jnp.sum(second_in * second_hat, axis=(0, 1))
    second_bias_grad = jnp.sum(second_in, axis=(0, 1))
    middle_grad = upstream + norm_back(second_in, second_hat, second_inv, second_gain)
    middle_low = middle_grad.astype(jnp.bfloat16)
    out_weight_grad = outer_product(attended, middle_low)
    out_bias_grad = jnp.sum(middle_grad, axis=(0, 1))
    attended_grad = matmul(middle_low, out_weight.T).astype(jnp.bfloat16).reshape(queries.shape)
    again_scores = batched("bqhd,bkhd->bhqk", queries, key_rows) * score_scale
    probs = jnp.exp(again_scores - log_total)
    probs_low = probs.astype(jnp.bfloat16)
    value_grad = batched("bhqk,bqhd->bkhd", probs_low, attended_grad)
    prob_grad = batched("bqhd,bkhd->bhqk", attended_grad, values)
    score_grad = (
        probs * (prob_grad - jnp.sum(probs * prob_grad, axis=-1, keepdims=True)) * score_scale
    ).astype(jnp.bfloat16)
    query_grad = batched("bhqk,bkhd->bqhd", score_grad, key_rows).reshape(flat_shape)
    key_grad = batched("bhqk,bqhd->bkhd", score_grad, queries).reshape(flat_shape)
    value_grad = value_grad.reshape(flat_shape)
    joined = jnp.concatenate([query_grad, key_grad, value_grad], axis=-1).astype(jnp.bfloat16)
    qkv_weight_grad = outer_product(normed, joined)
    query_bias_grad = jnp.sum(query_grad, axis=(0, 1))
    value_bias_grad = jnp.sum(value_grad, axis=(0, 1))
    first_in = matmul(joined, qkv_weight.T)
    first_gain_grad = jnp.sum(first_in * first_hat, axis=(0, 1))
    first_bias_grad = jnp.sum(first_in, axis=(0, 1))
    middle_grad = middle_grad + norm_back(first_in, first_hat, first_inv, first_gain)
    input_grad = middle_grad.astype(jnp.bfloat16)
    grads = (
        first_gain_grad,
        first_bias_grad,
        qkv_weight_grad,
        query_bias_grad,
        value_bias_grad,
        out_weight_grad,
        out_bias_grad,
        second_gain_grad,
        second_bias_grad,
        up_weight_grad,
        up_bias_grad,
        down_weight_grad,
        down_bias_grad,
    )
    return (input_grad, grads)


def places(n):
    rep = lax.axis_index("rep")
    me = lax.axis_index("shard")
    core = rep % 2
    row = rep // 2
    position = ring_position(me, n)
    right = (rep, ring_index((position + 1) % n, n))
    left = (rep, ring_index((position + n - 1) % n, n))
    partner = (row * 2 + 1 - core, me)
    across = ((1 - row) * 2 + core, me)
    return me, core, row, position, right, left, partner, across


def greet(peers):
    barrier = pltpu.get_barrier_semaphore()
    for peer in peers:
        pl.semaphore_signal(barrier, inc=1, device_id=peer, device_id_type=MESH)
    pl.semaphore_wait(barrier, len(peers))


def remote(source, target, send, recv, device):
    return pltpu.make_async_remote_copy(
        src_ref=source,
        dst_ref=target,
        send_sem=send,
        recv_sem=recv,
        device_id=device,
        device_id_type=MESH,
    )


def window(refs, side, part, block, width):
    qkv, out, up, down = refs
    if side == 2:
        return [(None, down.at[block, part])]
    if side == 1:
        return [(None, up.at[block, :, pl.ds(pl.multiple_of(part * width, width), width)])]
    inner = part - part // 3
    return [
        (part < 3, qkv.at[block, :, pl.ds(pl.multiple_of(inner * width, width), width)]),
        (part == 3, out.at[block]),
    ]


def start_each(views, make):
    for condition, view in views:
        if condition is None:
            make(view).start()
        else:
            pl.when(condition)(make(view).start)


def gather_kernel(
    n,
    width,
    qkv_in,
    out_in,
    up_in,
    down_in,
    line_in,
    qkv_ref,
    out_ref,
    up_ref,
    down_ref,
    line_ref,
    local_sem,
    ring_s,
    ring_r,
    core_s,
    core_r,
    row_s,
    row_r,
    last_s,
    last_r,
    line_s,
    line_r,
):
    me, core, row, position, right, left, partner, across = places(n)
    refs = (qkv_ref, out_ref, up_ref, down_ref)
    pairs = zip((qkv_in, out_in, up_in, down_in, line_in), refs + (line_ref,))
    locals_ = [
        pltpu.make_async_copy(source, target.at[me], local_sem.at[i])
        for i, (source, target) in enumerate(pairs)
    ]
    for copy in locals_:
        copy.start()
    greet((right, left, partner, across))
    for copy in locals_:
        copy.wait()

    def block(way, r):
        return ring_index((position + (1 if way else n - 1) * r) % n, n)

    def views(i, r, whose):
        way, kind = i // 2, i % 2
        side, part = (2, 2 * whose + way) if kind else (way, 2 * whose + row)
        return window(refs, side, part, block(way, r), width)

    def over(way, r, whose):
        return window(refs, way, 2 * whose + 1 - row, block(way, r), width)

    def ring(i, r):
        peer = left if i // 2 else right
        return lambda v: remote(v, v, ring_s.at[i, r], ring_r.at[i, r], peer)

    def to_core(i, r):
        return lambda v: remote(v, v, core_s.at[i, r], core_r.at[i, r], partner)

    def to_row(way, r):
        return lambda v: remote(v, v, row_s.at[way, r], row_r.at[way, r], across)

    def to_last(way, r):
        return lambda v: remote(v, v, last_s.at[way, r], last_r.at[way, r], partner)

    def line(r):
        view = line_ref.at[block(0, r)]
        return remote(view, view, line_s.at[r], line_r.at[r], right)

    def one(vs):
        return vs[0][1]

    for i in range(4):
        start_each(views(i, 0, core), ring(i, 0))
    line(0).start()

    def relay(r):
        for way in range(2):
            to_row(way, r)(one(over(way, r + 1, core))).wait_recv()
            start_each(over(way, r + 1, core), to_last(way, r))

    def step(r, carry):
        for i in (0, 2, 1, 3):
            got = views(i, r + 1, core)
            ring(i, r)(one(got)).wait_recv()

            @pl.when(r < n - 2)
            def _():
                start_each(got, ring(i, r + 1))

            if i % 2 == 0:
                start_each(got, to_row(i // 2, r))
            start_each(got, to_core(i, r))
        line(r).wait_recv()

        @pl.when(r < n - 2)
        def _():
            line(r + 1).start()

        @pl.when(r > 0)
        def _():
            relay(r - 1)

        return carry

    lax.fori_loop(0, n - 1, step, 0)
    relay(n - 2)

    def finish(r, carry):
        for i in range(4):
            view = one(views(i, r, core))
            ring(i, r)(view).wait_send()
            to_core(i, r)(view).wait_send()
            to_core(i, r)(view).wait_recv()
        for way in range(2):
            view = one(views(2 * way, r, core))
            to_row(way, r)(view).wait_send()
            to_last(way, r)(view).wait_send()
            to_last(way, r)(view).wait_recv()
        line(r).wait_send()
        return carry

    lax.fori_loop(0, n - 1, finish, 0)


def gather_all(arrays, n, width):
    dma = pltpu.SemaphoreType.DMA
    return pl.pallas_call(
        functools.partial(gather_kernel, n, width),
        out_shape=[jax.ShapeDtypeStruct((n,) + a.shape, a.dtype) for a in arrays],
        in_specs=[pl.BlockSpec(memory_space=pltpu.VMEM)] * len(arrays),
        out_specs=[pl.BlockSpec(memory_space=pl.ANY)] * len(arrays),
        scratch_shapes=[dma((len(arrays),))]
        + [dma((4, n - 1))] * 4
        + [dma((2, n - 1))] * 4
        + [dma((n - 1,))] * 2,
        compiler_params=pltpu.CompilerParams(collective_id=0, has_side_effects=True),
        name="gather_all",
    )(*arrays)


def reduce_kernel(
    n,
    width,
    qkv_ref,
    out_ref,
    up_ref,
    down_ref,
    line_ref,
    sums,
    line_out,
    own,
    given,
    arrive,
    over,
    other,
    line_send,
    line_got,
    line_pair,
    own_sem,
    given_s,
    given_r,
    ring_s,
    ring_r,
    row_s,
    row_r,
    end_row_s,
    end_row_r,
    end_core_s,
    end_core_r,
    line_s,
    line_r,
    pair_s,
    pair_r,
):
    me, core, row, position, right, left, partner, across = places(n)
    refs = (qkv_ref, out_ref, up_ref, down_ref)
    f32 = jnp.float32

    def block(way, k):
        return ring_index((position + (1 if way else n - 1) * (k + 1)) % n, n)

    def source(i, k, whose):
        way, kind = i % 2, i // 2
        side, part = (
            (way, 2 * whose + row),
            (2, 2 * whose + way),
            (way, 2 * whose + 1 - row),
        )[kind]
        return window(refs, side, part, block(way, k), width)

    def load(i, k):
        return lambda v: pltpu.make_async_copy(v, own.at[i, k], own_sem.at[i, k])

    def give(i, k):
        return lambda v: remote(v, given.at[i, k], given_s.at[i, k], given_r.at[i, k], partner)

    def ring(i, k):
        peer = left if i % 2 else right
        return remote(own.at[i, k], arrive.at[i, k], ring_s.at[i, k], ring_r.at[i, k], peer)

    def to_row(way, k):
        return remote(
            own.at[4 + way, k], over.at[way, k], row_s.at[way, k], row_r.at[way, k], across
        )

    def line_ring(k):
        return remote(line_send.at[k], line_got.at[k], line_s.at[k], line_r.at[k], right)

    order = (4, 5, 2, 3, 0, 1)

    def loads(k, carry):
        for i in order:
            start_each(source(i, k, core), load(i, k))
        return carry

    lax.fori_loop(0, n, loads, 0)
    greet((right, left, partner, across))

    def gives(k, carry):
        for i in order:
            start_each(source(i, k, 1 - core), give(i, k))
        return carry

    lax.fori_loop(0, n, gives, 0)

    def take(i, k):
        view = source(i, k, core)[0][1]
        load(i, k)(view).wait()
        give(i, k)(view).wait_recv()
        return own[i, k].astype(f32) + given[i, k].astype(f32)

    def put(i, k, total):
        own[i, k] = total.astype(own.dtype)

    def ahead(k):
        for way in range(2):
            put(4 + way, k, take(4 + way, k))
            to_row(way, k).start()

    def partial(i, k, first):
        total = take(i, k)
        if i < 2:
            to_row(i, k).wait_recv()
            total = total + over[i, k].astype(f32)
        if not first:
            ring(i, k - 1).wait_recv()
            total = total + arrive[i, k - 1].astype(f32)
        return total

    ahead(0)
    line_send[0] = line_ref[block(0, 0)]
    line_ring(0).start()
    ahead(1)
    for i in (2, 3, 0, 1):
        put(i, 0, partial(i, 0, True))
        ring(i, 0).start()

    def step(k, carry):
        ahead(k + 1)
        for i in (2, 3, 0, 1):
            put(i, k, partial(i, k, False))
            ring(i, k).start()
        line_ring(k - 1).wait_recv()
        line_send[k] = line_ref[block(0, k)] + line_got[k - 1]
        line_ring(k).start()
        return carry

    lax.fori_loop(1, n - 1, step, 0)

    def end_row(i, k=None):
        if i < 2:
            view = sums.at[i, 2 * core + row]
            return remote(view, view, end_row_s.at[i], end_row_r.at[i], across)
        return remote(
            own.at[i, n - 1], other.at[i - 2], end_row_s.at[i], end_row_r.at[i], across
        )

    def end_core(j, side, part):
        view = sums.at[side, part]
        return remote(view, view, end_core_s.at[j], end_core_r.at[j], partner)

    for i in (2, 3):
        put(i, n - 1, partial(i, n - 1, False))
        end_row(i).start()
    line_ring(n - 2).wait_recv()
    line_pair[0] = line_ref[me] + line_got[n - 2]
    pair_row = remote(line_pair.at[0], line_pair.at[1], pair_s.at[0], pair_r.at[0], across)
    pair_row.start()
    for way in (0, 1):
        sums[way, 2 * core + row] = partial(way, n - 1, False).astype(sums.dtype)
        end_row(way).start()
        end_core(way, way, 2 * core + row).start()
    pair_row.wait()
    line_pair[2] = line_pair[0] + line_pair[1]
    pair_core = remote(line_pair.at[2], line_pair.at[3], pair_s.at[1], pair_r.at[1], partner)
    pair_core.start()
    for way in (0, 1):
        end_row(2 + way).wait_recv()
        total = own[2 + way, n - 1].astype(f32) + other[way].astype(f32)
        sums[2, 2 * core + way] = total.astype(sums.dtype)
        end_core(2 + way, 2, 2 * core + way).start()
    for way in (0, 1):
        end_row(way).wait_recv()
        end_core(4 + way, way, 2 * core + 1 - row).start()
    pair_core.wait()
    line_out[...] = line_pair[2] + line_pair[3]
    for i in range(4):
        end_row(i).wait_send()
    for j in range(6):
        copy = end_core(j, 0, 0)
        copy.wait_send()
        copy.wait_recv()

    def finish(k, carry):
        for i in range(6):
            give(i, k)(source(i, k, core)[0][1]).wait_send()
        for way in range(2):
            to_row(way, k).wait_send()
        return carry

    lax.fori_loop(0, n, finish, 0)

    def finish_ring(k, carry):
        for i in range(4):
            ring(i, k).wait_send()
        line_ring(k).wait_send()
        return carry

    lax.fori_loop(0, n - 1, finish_ring, 0)


def reduce_all(arrays, n, width):
    dma = pltpu.SemaphoreType.DMA
    vmem = pltpu.VMEM
    rows = arrays[0].shape[1]
    low = arrays[0].dtype
    line = arrays[-1].shape[1:]
    anywhere = pl.BlockSpec(memory_space=pl.ANY)
    near = pl.BlockSpec(memory_space=pltpu.VMEM)
    return pl.pallas_call(
        functools.partial(reduce_kernel, n, width),
        out_shape=[
            jax.ShapeDtypeStruct((3, 4, rows, width), low),
            jax.ShapeDtypeStruct(line, jnp.float32),
        ],
        in_specs=[anywhere] * 4 + [near],
        out_specs=[near, near],
        scratch_shapes=[
            vmem((6, n, rows, width), low),
            vmem((6, n, rows, width), low),
            vmem((4, n - 1, rows, width), low),
            vmem((2, n, rows, width), low),
            vmem((2, rows, width), low),
            vmem((n - 1,) + line, jnp.float32),
            vmem((n - 1,) + line, jnp.float32),
            vmem((4,) + line, jnp.float32),
            dma((6, n)),
            dma((6, n)),
            dma((6, n)),
            dma((4, n - 1)),
            dma((4, n - 1)),
            dma((2, n)),
            dma((2, n)),
            dma((4,)),
            dma((4,)),
            dma((6,)),
            dma((6,)),
            dma((n - 1,)),
            dma((n - 1,)),
            dma((2,)),
            dma((2,)),
        ],
        compiler_params=pltpu.CompilerParams(
            collective_id=1, has_side_effects=True, vmem_limit_bytes=56 * 1024 * 1024
        ),
        name="reduce_all",
    )(*arrays)


def per_device_in_parts(n, layer_input, cotangent, live, *params):
    width = params[0].shape[0] * n
    rows = params[0].shape[0]
    matrices = [i for i, p in enumerate(params) if p.ndim == 2]
    vectors = [i for i, p in enumerate(params) if p.ndim == 1]
    shapes = [params[i].shape for i in matrices]
    assert shapes == [(rows, 3 * width), (rows, width), (rows, 4 * width), (4 * rows, width)]
    lengths = [params[i].shape[0] for i in vectors]
    tall = -(-sum(lengths) // (16 * LANES)) * 16
    spare = tall * LANES - sum(lengths)

    line = jnp.concatenate([params[i] for i in vectors] + [jnp.zeros(spare, params[0].dtype)])
    sent = [params[i] for i in matrices]
    sent[3] = sent[3].reshape(4, rows, width)
    *full, lines = gather_all(sent + [line.reshape(tall, LANES)], n, width)
    gathered = [None] * len(params)
    for i, array in zip(matrices, full):
        gathered[i] = array.reshape(n * params[i].shape[0], params[i].shape[1])
    tail = lines.reshape(n, -1)
    at = 0
    for i, length in zip(vectors, lengths):
        gathered[i] = tail[:, at : at + length].reshape(-1)
        at += length

    output, saved = forward_pass(gathered, layer_input, live)
    input_grad, grads = backward_pass(gathered, saved, cotangent)

    low = jnp.bfloat16
    blocks = [grads[i].astype(low).reshape((n,) + a.shape) for i, a in zip(matrices, sent)]
    parts = [grads[i].reshape(n, -1) for i in vectors] + [jnp.zeros((n, spare), jnp.float32)]
    blocks.append(jnp.concatenate(parts, axis=1).reshape(n, tall, LANES))
    sums, tail = reduce_all(blocks, n, width)

    def joined(pieces):
        return jnp.swapaxes(pieces, 0, 1).reshape(rows, -1).astype(jnp.float32)

    results = [None] * len(params)
    whole = (
        joined(sums[0, :3]),
        sums[0, 3].astype(jnp.float32),
        joined(sums[1]),
        sums[2].reshape(4 * rows, width).astype(jnp.float32),
    )
    for i, array in zip(matrices, whole):
        results[i] = array
    tail = tail.reshape(-1)
    at = 0
    for i, length in zip(vectors, lengths):
        results[i] = tail[at : at + length]
        at += length
    return (output, input_grad, *results)


VECTORS = (0, 1, None, 2, 3, None, 4, 5, 6, None, 8, None, 7)


def per_device(n, layer_input, cotangent, live, *params):
    rows = params[0].shape[0]
    if rows % 16 or layer_input.shape[0] != 1:
        return per_device_in_parts(n, layer_input, cotangent, live, *params)
    matrices = [p for p in params if p.ndim == 2]
    order = sorted((place, i) for i, place in enumerate(VECTORS) if place is not None)
    stack = jnp.concatenate([params[i].reshape(-1, rows) for _, i in order])
    line = jnp.pad(stack, ((0, 16 - stack.shape[0]), (0, LANES - rows)))
    output, input_grad, *sums, tail = run_layer(layer_input, cotangent, live, matrices, line, n)
    results = []
    for i, p in enumerate(params):
        if p.ndim == 2:
            results.append(sums.pop(0).astype(F32))
        else:
            first = VECTORS[i]
            results.append(tail[first : first + p.shape[0] // rows, :rows].reshape(-1))
    return (output, input_grad, *results)


def solution(mesh):
    whole = P(("rep", "shard"), None, None)
    vector, matrix = P("shard"), P("shard", None)
    ranks = (1, 1, 2, 1, 1, 2, 1, 1, 1, 2, 1, 2, 1)
    params = tuple(matrix if rank == 2 else vector for rank in ranks)
    return jax.shard_map(
        functools.partial(per_device, mesh.shape["shard"]),
        mesh=mesh,
        in_specs=(whole, whole, P(("rep", "shard"))) + params,
        out_specs=(whole, whole) + params,
        check_vma=False,
    )
```

```python
import functools

import jax
import jax.numpy as jnp
from jax import lax
from jax.experimental import pallas as pl
from jax.experimental.pallas import tpu as pltpu
from jax.sharding import PartitionSpec as P

HEAD_DIM = 64
LANES = 128
NORM_EPS = 1e-06
ROOT_HALF = 0.7071067811865476
DENSITY_COEF = 0.3989422804014327
MESH = pl.DeviceIdType.MESH
F32 = jnp.float32
LOW = jnp.bfloat16

QKV, OUT, UP, DOWN = range(4)
SHARED, MINE, YOURS = range(3)


def ring_index(position, n):
    half = position // (n // 2)
    return (1 - half) * 2 * position + half * (2 * (n - 1 - position) + 1)


def ring_position(index, n):
    odd = index % 2
    step = index // 2
    return (1 - odd) * step + odd * (n - 1 - step)


def remote(source, target, send, recv, device):
    return pltpu.make_async_remote_copy(
        src_ref=source,
        dst_ref=target,
        send_sem=send,
        recv_sem=recv,
        device_id=device,
        device_id_type=MESH,
    )


def dot_nn(a, b):
    return jnp.dot(a, b, preferred_element_type=F32)


def dot_nt(a, b):
    return lax.dot_general(a, b, (((1,), (1,)), ((), ())), preferred_element_type=F32)


def dot_tn(a, b):
    return lax.dot_general(a, b, (((0,), (0,)), ((), ())), preferred_element_type=F32)


def split(refs, counts):
    at = 0
    for count in counts:
        yield refs[at : at + count]
        at += count

ORDER = (
    "GO", "GU", "gQ0", "gO0", "l0", "gU0", "gQ1", "gO1", "l1", "GD", "gU1", "gQ2", "gO2", "l2",
    "gU2", "gQ3", "gO3", "l3", "RQ", "RO", "gD0", "v", "EQ", "p", "gU3", "RU", "gD1", "a0", "EO",
    "a1", "gD2", "m", "t", "EU", "u0", "u1", "dDs", "dDy", "gD3", "RD", "dDm", "oD0", "Ds0", "oD1",
    "oD2", "oD3", "Dm0", "ED", "hb", "dUs", "dUy", "dUm", "Ds1", "Us0", "Dm1", "sb", "nb", "dOs",
    "dOm", "dOy", "oU0", "Ds2", "oU1", "oU2", "oU3", "ob", "Dm2", "Us1", "Os0", "Om0", "Oy0", "ab0",
    "Ds3", "Dm3", "ab1", "Um0", "dQs", "dQm", "dQy", "Us2", "Um1", "Qs0", "Qm0", "Qy0", "Os1",
    "Om1", "Oy1", "Ds", "Dm", "Us3", "Um2", "Qs1", "Qm1", "Qy1", "fb", "fn", "t0", "XD", "Um3",
    "Us", "Os2", "Om2", "Oy2", "Qs2", "Qm2", "Qy2", "t1", "c", "Um", "Os3", "Om3", "Oy3", "Qs3",
    "Qm3", "Qy3", "t2", "XU", "Os", "Om", "Oy", "t3", "Qs", "Qm", "Qy", "te", "XO", "tp", "XQ",
    "tf", "FQ", "FO", "FU", "FD",
)


def layer_kernel(n, length, padded, model, *refs):
    ins, outs, weights, acts, halves, given, over, arrive_a, arrive_b, extra, sems = split(
        refs, (8, 7, 4, 23, 4, 4, 2, 4, 4, 4 + 6, 25)
    )
    over = dict(zip((UP, DOWN), over))
    x_in, cot_in, live_in, qkv_in, out_in, up_in, down_in, line_in = ins
    output_ref, input_grad_ref, *sums, line_out = outs
    (
        x_low,
        cot_low,
        upstream,
        hat1,
        inv1,
        normed,
        normed_t,
        qkv,
        probs,
        attended,
        attended_t,
        middle,
        hat2,
        inv2,
        second,
        second_t,
        hidden,
        hidden_t,
        pre_low,
        slope,
        incoming,
        middle_low,
        vec_grad,
    ) = acts
    joined, middle_grad, head_grad = qkv, hat2, normed
    exchange, (lines, vec, up_bias, line_grad, line_a, line_b) = extra[:4], extra[4:]
    (
        in_sem,
        own_sem,
        ring_s,
        ring_r,
        row_s,
        row_r,
        core_s,
        core_r,
        line_s,
        line_r,
        give_s,
        give_r,
        over_s,
        over_r,
        sum_s,
        sum_r,
        end_s,
        end_r,
        tail_s,
        tail_r,
        pair_s,
        pair_r,
    ) = sems[:22]
    line_pair = sems[22]
    pre_bias, score_rows = sems[23], sems[24]

    rows = qkv_in.shape[0]
    height = [ref.shape[0] for ref in (qkv_in, out_in, up_in, down_in)]
    sixth = [ref.shape[1] // 6 for ref in (qkv_in, out_in, up_in, down_in)]
    matrix_in = (qkv_in, out_in, up_in, down_in)
    hidden_units = up_in.shape[1]
    reach = (n // 2, n // 2 - 1)

    rep = lax.axis_index("rep")
    me = lax.axis_index("shard")
    core = rep % 2
    row = rep // 2
    position = ring_position(me, n)
    sign = 1 - 2 * core

    def at(k):
        return ring_index((position + sign * k + n) % n, n)

    peers = ((rep, at(1)), (rep, at(-1)))
    partner = (row * 2 + 1 - core, me)
    across = ((1 - row) * 2 + core, me)
    third = (2, row, 1 - row)

    def block(m, b):
        return pl.ds(pl.multiple_of(b * height[m], height[m]), height[m])

    def columns(m, slot, whose):
        width = sixth[m]
        return pl.ds(pl.multiple_of((2 * third[slot] + whose) * width, width), width)

    def piece(m, b, slot):
        return weights[m].at[block(m, b), columns(m, slot, core)]

    def came(d, h):
        return at(-1 - h) if d == 0 else at(1 + h)

    def own_copy(m, slot):
        return pltpu.make_async_copy(
            matrix_in[m].at[:, columns(m, slot, core)], piece(m, me, slot), own_sem.at[m, slot]
        )

    def gather_send(m, slot, d, h):
        view = piece(m, at(-h) if d == 0 else at(h), slot)
        return remote(view, view, ring_s.at[m, slot, d, h], ring_r.at[m, slot, d, h], peers[d])

    def gather_row(m, d, h, slot):
        view = piece(m, came(d, h), slot)
        k = d * reach[0] + h
        return remote(view, view, row_s.at[m, k], row_r.at[m, k], across)

    def gather_core(m, slot, whose):
        view = weights[m].at[:, columns(m, slot, whose)]
        return remote(view, view, core_s.at[m, slot], core_r.at[m, slot], partner)

    def gather_start(m):
        for slot in (MINE, SHARED):
            for d in (0, 1):
                gather_send(m, slot, d, 0).start()

    def gather_hop(m, h, slots=(MINE, SHARED)):
        for slot in slots:
            for d in (0, 1):
                if h < reach[d]:
                    view = piece(m, came(d, h), slot)
                    remote(
                        view, view, ring_s.at[m, slot, d, h], ring_r.at[m, slot, d, h], peers[d]
                    ).wait_recv()
                    if h + 1 < reach[d]:
                        gather_send(m, slot, d, h + 1).start()
                    if slot == MINE:
                        gather_row(m, d, h, MINE).start()

    def gather_relay(m):
        for slot in (MINE, SHARED):
            gather_core(m, slot, core).start()

    def gather_end(m):
        for d in (0, 1):
            for h in range(reach[d]):
                gather_row(m, d, h, YOURS).wait_recv()
        gather_core(m, YOURS, core).start()
        for slot in (MINE, SHARED, YOURS):
            gather_core(m, slot, 1 - core).wait_recv()

    def line_send(d, h):
        view = lines.at[at(-h) if d == 0 else at(h)]
        return remote(view, view, line_s.at[d, h], line_r.at[d, h], peers[d])

    def line_hop(h):
        for d in (0, 1):
            if h < reach[d]:
                view = lines.at[came(d, h)]
                remote(view, view, line_s.at[d, h], line_r.at[d, h], peers[d]).wait_recv()
                if h + 1 < reach[d]:
                    line_send(d, h + 1).start()

    def slots_of(m):
        return (SHARED, MINE) if m in over else (SHARED, MINE, YOURS)

    def owner(d, t):
        return at(reach[0] - t) if d == 0 else at(t - reach[1])

    def give(m, slot):
        return remote(
            halves[m].at[1, slot],
            given[m].at[slot],
            give_s.at[m, slot],
            give_r.at[m, slot],
            partner,
        )

    def hand_over(m, d, t):
        rows_of = block(m, owner(d, t))
        return remote(
            halves[m].at[0, YOURS, rows_of],
            over[m].at[rows_of],
            over_s.at[m, d, t],
            over_r.at[m, d, t],
            across,
        )

    def local(m, slot, b):
        total = halves[m][0, slot, block(m, b)].astype(F32) + given[m][slot, block(m, b)].astype(
            F32
        )
        if slot == MINE and m in over:
            total = total + over[m][block(m, b)].astype(F32)
        return total

    def ring_sum(m, slot, d, t):
        return remote(
            halves[m].at[0, slot, block(m, owner(d, t))],
            (arrive_a, arrive_b)[d][m].at[slot, t],
            sum_s.at[m, slot, d, t],
            sum_r.at[m, slot, d, t],
            peers[d],
        )

    def over_steps():
        return [(d, t) for t in range(reach[0] + 1) for d in (0, 1) if t < reach[d] + 1 - d]

    def reduce_over(m, p):
        if p == 0:
            give(m, YOURS).wait_recv()
        for d, t in over_steps():
            if min(t * 4 // reach[0], 3) == p:
                rows_of = block(m, owner(d, t))
                halves[m][0, YOURS, rows_of] = local(m, YOURS, owner(d, t)).astype(LOW)
                hand_over(m, d, t).start()

    def reduce_step(m, slot, t):
        if t == 0:
            give(m, slot).wait_recv()
        for d in (0, 1):
            if t < reach[d]:
                b = owner(d, t)
                if slot == MINE and m in over:
                    hand_over(m, d, t).wait_recv()
                total = local(m, slot, b)
                if t > 0:
                    ring_sum(m, slot, d, t - 1).wait_recv()
                    total = total + (arrive_a, arrive_b)[d][m][slot, t - 1].astype(F32)
                halves[m][0, slot, block(m, b)] = total.astype(LOW)
                ring_sum(m, slot, d, t).start()

    def sum_columns(m, slot, whose):
        width = sixth[m]
        which = third[slot] if m in over else (2, 0, 1)[slot]
        return pl.ds(pl.multiple_of((2 * which + whose) * width, width), width)

    def end_view(m, slot, whose):
        return sums[m].at[:, sum_columns(m, slot, whose)]

    def end_core(m, slot, whose):
        view = end_view(m, slot, whose)
        return remote(view, view, end_s.at[m, slot, 1], end_r.at[m, slot, 1], partner)

    def end_row(m, slot):
        return remote(
            halves[m].at[0, slot, block(m, me)],
            exchange[m].at[slot],
            end_s.at[m, slot, 0],
            end_r.at[m, slot, 0],
            across,
        )

    def end_other(m, slot):
        view = end_view(m, slot, core)
        return remote(view, view, end_s.at[m, MINE, 0], end_r.at[m, MINE, 0], across)

    def reduce_end(m, slot):
        if slot == MINE and m in over:
            hand_over(m, 0, reach[0]).wait_recv()
        total = local(m, slot, me)
        for d in (0, 1):
            if reach[d]:
                ring_sum(m, slot, d, reach[d] - 1).wait_recv()
                total = total + (arrive_a, arrive_b)[d][m][slot, reach[d] - 1].astype(F32)
        if slot == MINE and m in over:
            sums[m][:, sum_columns(m, MINE, core)] = total.astype(LOW)
            end_other(m, MINE).start()
            end_core(m, MINE, core).start()
        else:
            halves[m][0, slot, block(m, me)] = total.astype(LOW)
            end_row(m, slot).start()

    def reduce_exchange(m):
        for slot in slots_of(m):
            if slot == MINE and m in over:
                end_other(m, YOURS).wait_recv()
                end_core(m, YOURS, core).start()
            else:
                end_row(m, slot).wait_recv()
                total = halves[m][0, slot, block(m, me)].astype(F32) + exchange[m][slot].astype(F32)
                sums[m][:, sum_columns(m, slot, core)] = total.astype(LOW)
                end_core(m, slot, core).start()

    def reduce_finish(m):
        for slot in (SHARED, MINE, YOURS):
            end_core(m, slot, 1 - core).wait_recv()

    steps = padded // 16
    slices = [pl.ds(i * 16, 16) for i in range(steps)]
    gain = lambda i: vec[i : i + 1, :]
    live = live_in[0].astype(F32)
    row_id = lax.broadcasted_iota(jnp.int32, (padded, 1), 0)
    row_mask = (row_id < length).astype(F32)
    pair_width = 2 * HEAD_DIM
    pairs = model // pair_width

    def normalise(source, hat, inv):
        for s in slices:
            values = source[s, :]
            centred = values - jnp.mean(values, axis=-1, keepdims=True)
            spread = jnp.mean(centred * centred, axis=-1, keepdims=True)
            inv_std = lax.rsqrt(spread + NORM_EPS)
            hat[s, :] = centred * inv_std
            inv[s, :] = jnp.broadcast_to(inv_std, (16, LANES))

    def scale_shift(hat, low, g, b, mask):
        for i, s in enumerate(slices):
            value = hat[s, :] * gain(g) + gain(b)
            if mask and (i + 1) * 16 > length:
                value = value * row_mask[i * 16 : (i + 1) * 16]
            low[s, :] = value.astype(LOW)

    def transpose(source, target):
        def body(i, carry):
            cols = pl.ds(pl.multiple_of(i * 256, 256), 256)
            target[cols, :] = source[:, cols].T
            return carry

        lax.fori_loop(0, source.shape[1] // 256, body, 0)

    def begin():
        middle[...] = jnp.zeros_like(middle)
        middle[:length, :] = x_low[0].astype(F32)
        incoming[...] = jnp.zeros_like(incoming)
        incoming[:length, :] = cot_low[0].astype(F32) * live
        upstream[...] = incoming[...].astype(LOW)
        vec_grad[...] = jnp.zeros_like(vec_grad)
        vec_grad[7:8, :] = jnp.sum(incoming[...], axis=0, keepdims=True)
        normalise(middle, hat1, inv1)

    def vectors():
        for b in range(n):
            held = lines[b].astype(F32)
            vec[:, b * rows : (b + 1) * rows] = held[:, :rows]
            for e in range(4):
                first = (b * 4 + e) * rows
                up_bias[:, first : first + rows] = jnp.broadcast_to(
                    held[8 + e : 9 + e, :rows], (8, rows)
                )

    def first_norm():
        scale_shift(hat1, normed, 0, 1, True)
        transpose(normed, normed_t)
        zero = jnp.zeros((1, model), F32)
        for k, v in enumerate((vec[2:3, :], zero, vec[3:4, :])):
            pre_bias[:, k * model : (k + 1) * model] = jnp.broadcast_to(v, (8, model))

    def project(first, last):
        wide = 2 * sixth[QKV] // 2

        def body(c, carry):
            cols = pl.ds(pl.multiple_of(c * wide, wide), wide)
            value = (dot_nn(normed[...], weights[QKV][:, cols]) + pre_bias[0:1, cols]) * row_mask
            factor = jnp.where(c * wide < model, HEAD_DIM**-0.5, 1.0)
            qkv[:, cols] = (value.astype(LOW).astype(F32) * factor).astype(LOW)
            return carry

        lax.fori_loop(first, last, body, 0)

    lane = lax.broadcasted_iota(jnp.int32, (padded, pair_width), 1)
    low_lane = lane < HEAD_DIM
    key_mask = lax.broadcasted_iota(jnp.int32, (1, padded), 1) < length

    def heads(part, p):
        return qkv[:, pl.ds(pl.multiple_of(part * model + p * pair_width, LANES), pair_width)]

    def stacked(value, target):
        wide = value.astype(F32)
        target[:padded, :] = jnp.where(low_lane, wide, 0.0).astype(LOW)
        target[padded:, :] = jnp.where(low_lane, 0.0, wide).astype(LOW)

    def merged(value):
        return jnp.where(low_lane, value[:padded], value[padded:])

    def attend(first, last):
        def body(p, carry):
            stacked(heads(0, p), score_rows.at[0])
            scores = dot_nt(score_rows[0], heads(1, p))
            powers = jnp.where(key_mask, jnp.exp(scores), 0.0)
            total = jnp.sum(powers, axis=-1, keepdims=True)
            weight = (powers * (1.0 / total)).astype(LOW)
            probs[p] = weight
            cols = pl.ds(pl.multiple_of(p * pair_width, LANES), pair_width)
            attended[:, cols] = merged(dot_nn(weight, heads(2, p))).astype(LOW)
            return carry

        lax.fori_loop(first, last, body, 0)

    def mix():
        def body(c, carry):
            cols = pl.ds(pl.multiple_of(c * 256, 256), 256)
            middle[:, cols] = (
                middle[:, cols] + dot_nn(attended[...], weights[OUT][:, cols]) + vec[4:5, cols]
            )
            return carry

        lax.fori_loop(0, model // 256, body, 0)
        normalise(middle, hat2, inv2)
        scale_shift(hat2, second, 5, 6, False)

    def transposes():
        transpose(attended, attended_t)
        transpose(second, second_t)

    wide_hidden = 512

    def expand(first, last):
        def body(c, carry):
            cols = pl.ds(pl.multiple_of(c * wide_hidden, wide_hidden), wide_hidden)
            pre = dot_nn(second[...], weights[UP][:, cols]) + up_bias[0:1, cols]
            cdf = 0.5 * (1.0 + lax.erf(pre * ROOT_HALF))
            density = jnp.exp(-0.5 * pre * pre) * DENSITY_COEF
            value = (pre * cdf).astype(LOW)
            hidden[:, cols] = value
            slope[:, cols] = cdf + pre * density
            hidden_t[cols, :] = value.T
            return carry

        lax.fori_loop(first, last, body, 0)

    def contract():
        def body(c, carry):
            cols = pl.ds(pl.multiple_of(c * 256, 256), 256)
            value = dot_nn(hidden[...], weights[DOWN][:, cols]) + vec[7:8, cols]
            value = (middle[:, cols] + value) * live
            output_ref[0, :, cols] = value[:length].astype(LOW)
            return carry

        lax.fori_loop(0, model // 256, body, 0)

    def gradient(m, left, right, slot):
        width = sixth[m]
        base = (third[slot] if m in over else (2, 0, 1)[slot]) * 2 * width
        if width % 256 == 0:
            count, step = 2 * width // 256, 256
        elif (2 * width) % 256 == 0 and width < 256:
            count, step = 1, 2 * width
        else:
            count, step = 2, width
        tall = left.shape[0]
        high = min(tall, model)

        def body(i, carry):
            c, r = i % count, i // count
            cols = pl.ds(pl.multiple_of(base + c * step, LANES), step)
            down = pl.ds(pl.multiple_of(r * high, high), high)
            value = dot_nn(left[down, :], right[:, cols]).astype(LOW)
            if step > width:
                for whose in range(2):
                    halves[m][(whose + core) % 2, slot, down] = value[
                        :, whose * width : (whose + 1) * width
                    ]
            else:
                per = width // step
                start = pl.multiple_of((c % per) * step, LANES)
                halves[m][(c // per + core) % 2, slot, down, pl.ds(start, step)] = value
            return carry

        lax.fori_loop(0, count * (tall // high), body, 0)
        give(m, slot).start()

    def hidden_back(first, last):
        def body(c, carry):
            cols = pl.ds(pl.multiple_of(c * wide_hidden, wide_hidden), wide_hidden)
            value = dot_nt(upstream[...], weights[DOWN][cols, :]) * slope[:, cols]
            up_bias[:, cols] = jnp.broadcast_to(
                jnp.sum(value, axis=0, keepdims=True), (8, wide_hidden)
            )
            pre_low[:, cols] = value.astype(LOW)
            return carry

        lax.fori_loop(first, last, body, 0)

    def second_back():
        def body(c, carry):
            cols = pl.ds(pl.multiple_of(c * 256, 256), 256)
            incoming[:, cols] = dot_nt(pre_low[...], weights[UP][cols, :])
            return carry

        lax.fori_loop(0, model // 256, body, 0)

    def norm_back(hat, inv, g, add):
        gain_sum = jnp.zeros((1, model), F32)
        bias_sum = jnp.zeros((1, model), F32)
        add_sum = jnp.zeros((1, model), F32)
        for s in slices:
            came_in = incoming[s, :]
            hat_vals = hat[s, :]
            scaled = came_in * gain(g)
            average = jnp.mean(scaled, axis=-1, keepdims=True)
            along = jnp.mean(scaled * hat_vals, axis=-1, keepdims=True)
            value = add[s, :].astype(F32) + inv[s, 0:1] * (scaled - average - hat_vals * along)
            gain_sum += jnp.sum(came_in * hat_vals, axis=0, keepdims=True)
            bias_sum += jnp.sum(came_in, axis=0, keepdims=True)
            add_sum += jnp.sum(value, axis=0, keepdims=True)
            middle_grad[s, :] = value
            middle_low[s, :] = value.astype(LOW)
        vec_grad[g : g + 1, :] = gain_sum
        vec_grad[g + 1 : g + 2, :] = bias_sum
        return add_sum

    def attended_back():
        def body(c, carry):
            cols = pl.ds(pl.multiple_of(c * 256, 256), 256)
            head_grad[:, cols] = dot_nt(middle_low[...], weights[OUT][cols, :]).astype(LOW)
            return carry

        lax.fori_loop(0, model // 256, body, 0)

    def attend_back(first, last):
        def body(p, carry):
            start = pl.multiple_of(p * pair_width, LANES)
            cols = pl.ds(start, pair_width)
            stacked(head_grad[:, cols], score_rows.at[1])
            stacked(heads(0, p), score_rows.at[0])
            weight = probs[p]
            value_grad = dot_tn(weight, score_rows[1])
            prob_grad = dot_nt(score_rows[1], heads(2, p))
            wide = weight.astype(F32)
            along = jnp.sum(wide * prob_grad, axis=-1, keepdims=True)
            score_grad = (wide * (prob_grad - along)).astype(LOW)
            query_grad = merged(dot_nn(score_grad, heads(1, p))) * HEAD_DIM**-0.5
            key_grad = dot_tn(score_grad, score_rows[0])
            vec_grad[2:3, cols] = jnp.sum(query_grad, axis=0, keepdims=True)
            vec_grad[3:4, cols] = jnp.sum(value_grad, axis=0, keepdims=True)
            for k, value in enumerate((query_grad, key_grad, value_grad)):
                joined[:, pl.ds(pl.multiple_of(k * model + start, LANES), pair_width)] = (
                    value.astype(LOW)
                )
            return carry

        lax.fori_loop(first, last, body, 0)

    def first_back():
        def body(c, carry):
            cols = pl.ds(pl.multiple_of(c * 256, 256), 256)
            incoming[:, cols] = dot_nt(joined[...], weights[QKV][cols, :])
            return carry

        lax.fori_loop(0, model // 256, body, 0)

    def tail_local():
        line_grad[...] = jnp.zeros_like(line_grad)
        for b in range(n):
            line_grad[b, 0:8, 0:rows] = vec_grad[0:8, b * rows : (b + 1) * rows]
            for e in range(4):
                first = (b * 4 + e) * rows
                line_grad[b, 8 + e : 9 + e, 0:rows] = up_bias[0:1, first : first + rows]

    def tail_sum(d, t):
        b = at(reach[0] - t) if d == 0 else at(t - reach[1])
        arrive = (line_a, line_b)[d]
        return remote(line_grad.at[b], arrive.at[t], tail_s.at[d, t], tail_r.at[d, t], peers[d])

    def tail_step(t):
        for d in (0, 1):
            if t < reach[d]:
                b = at(reach[0] - t) if d == 0 else at(t - reach[1])
                if t > 0:
                    tail_sum(d, t - 1).wait_recv()
                    line_grad[b] = line_grad[b] + (line_a, line_b)[d][t - 1]
                tail_sum(d, t).start()

    def pair_copy(k, peer):
        return remote(
            line_pair.at[2 * k], line_pair.at[2 * k + 1], pair_s.at[k], pair_r.at[k], peer
        )

    def tail_end():
        total = line_grad[me]
        for d in (0, 1):
            if reach[d]:
                tail_sum(d, reach[d] - 1).wait_recv()
                total = total + (line_a, line_b)[d][reach[d] - 1]
        line_pair[0] = total
        pair_copy(0, across).start()

    def tail_pair():
        pair_copy(0, across).wait_recv()
        line_pair[2] = line_pair[0] + line_pair[1]
        pair_copy(1, partner).start()

    def tail_finish():
        pair_copy(1, partner).wait_recv()
        line_out[...] = line_pair[2] + line_pair[3]

    line_copy = pltpu.make_async_copy(line_in, lines.at[me], in_sem.at[0])
    x_copy = pltpu.make_async_copy(x_in, x_low, in_sem.at[1])
    cot_copy = pltpu.make_async_copy(cot_in, cot_low, in_sem.at[2])
    line_copy.start()
    for m in range(4):
        for slot in (MINE, SHARED, YOURS):
            own_copy(m, slot).start()
    x_copy.start()
    cot_copy.start()

    barrier = pltpu.get_barrier_semaphore()
    for peer in (*peers, partner, across):
        pl.semaphore_signal(barrier, inc=1, device_id=peer, device_id_type=MESH)
    pl.semaphore_wait(barrier, 4)

    line_copy.wait()
    for d in (0, 1):
        line_send(d, 0).start()
    for slot in (MINE, SHARED, YOURS):
        own_copy(QKV, slot).wait()
    gather_start(QKV)
    for m in (OUT, UP, DOWN):
        for slot in (MINE, SHARED, YOURS):
            own_copy(m, slot).wait()
    x_copy.wait()
    cot_copy.wait()
    begin()

    def part(total, p):
        return range(total * p // 4, total * (p + 1) // 4)

    def hops(m, p):
        for h in part(reach[0], p):
            gather_hop(m, h)

    def steps_of(m, slot, p):
        for t in part(reach[0], p):
            reduce_step(m, slot, t)

    def lines_of(p):
        for h in part(reach[0], p):
            line_hop(h)

    def tails_of(p):
        for t in part(reach[0], p):
            tail_step(t)

    def first_norm_back():
        norm_back(hat1, inv1, 0, middle_grad)
        input_grad_ref[0] = middle_grad[:length, :].astype(LOW)
        tail_local()

    def second_norm_back():
        vec_grad[4:5, :] = norm_back(hat2, inv2, 5, upstream)

    chunks = hidden_units // wide_hidden
    sides = {QKV: (normed_t, joined), OUT: (attended_t, middle_low)}
    sides |= {UP: (second_t, pre_low), DOWN: (hidden_t, upstream)}
    actions = {
        "v": lambda: (vectors(), first_norm()),
        "p": lambda: project(0, 6),
        "a0": lambda: attend(0, pairs // 2),
        "a1": lambda: attend(pairs // 2, pairs),
        "m": mix,
        "t": transposes,
        "u0": lambda: expand(0, chunks // 2),
        "u1": lambda: expand(chunks // 2, chunks),
        "c": contract,
        "hb": lambda: hidden_back(0, chunks),
        "sb": second_back,
        "nb": second_norm_back,
        "ob": attended_back,
        "ab0": lambda: attend_back(0, pairs // 2),
        "ab1": lambda: attend_back(pairs // 2, pairs),
        "fb": first_back,
        "fn": first_norm_back,
        "te": tail_end,
        "tp": tail_pair,
        "tf": tail_finish,
    }
    for p in range(4):
        actions[f"l{p}"] = functools.partial(lines_of, p)
        actions[f"t{p}"] = functools.partial(tails_of, p)
    for name, m in (("Q", QKV), ("O", OUT), ("U", UP), ("D", DOWN)):
        actions["G" + name] = functools.partial(gather_start, m)
        actions["R" + name] = functools.partial(gather_relay, m)
        actions["E" + name] = functools.partial(gather_end, m)
        actions["X" + name] = functools.partial(reduce_exchange, m)
        actions["F" + name] = functools.partial(reduce_finish, m)
        for p in range(4):
            actions[f"g{name}{p}"] = functools.partial(hops, m, p)
            actions[f"o{name}{p}"] = functools.partial(reduce_over, m, p)
        for key, slot in (("s", SHARED), ("m", MINE), ("y", YOURS)):
            actions[f"d{name}{key}"] = functools.partial(gradient, m, *sides[m], slot)
            actions[f"{name}{key}"] = functools.partial(reduce_end, m, slot)
            for p in range(4):
                actions[f"{name}{key}{p}"] = functools.partial(steps_of, m, slot, p)
    for name in ORDER:
        actions[name]()

    for m in range(4):
        for slot in (SHARED, MINE, YOURS):
            gather_core(m, slot, core).wait_send()
            give(m, slot).wait_send()
            end_core(m, slot, core).wait_send()
        for slot in slots_of(m):
            if slot == MINE and m in over:
                end_other(m, MINE).wait_send()
            else:
                end_row(m, slot).wait_send()
        if m in over:
            for d, t in over_steps():
                hand_over(m, d, t).wait_send()
        for d in (0, 1):
            for h in range(reach[d]):
                gather_row(m, d, h, MINE).wait_send()
                for slot in (SHARED, MINE):
                    gather_send(m, slot, d, h).wait_send()
                for slot in slots_of(m):
                    ring_sum(m, slot, d, h).wait_send()
    for d in (0, 1):
        for h in range(reach[d]):
            line_send(d, h).wait_send()
            tail_sum(d, h).wait_send()
    pair_copy(0, across).wait_send()
    pair_copy(1, partner).wait_send()


def run_layer(layer_input, cotangent, live, matrices, line, n):
    images, length, model = layer_input.shape
    padded = -(-length // 16) * 16
    hidden_units = matrices[UP].shape[1]
    vmem, dma = pltpu.VMEM, pltpu.SemaphoreType.DMA
    reach = (n // 2, n // 2 - 1)
    height = [a.shape[0] for a in matrices]
    sixth = [a.shape[1] // 6 for a in matrices]
    pairs = model // (2 * HEAD_DIM)
    wide = (padded, model)
    scratch = [vmem((n * a.shape[0], a.shape[1]), LOW) for a in matrices]
    scratch += [
        vmem((1, length, model), LOW),
        vmem((1, length, model), LOW),
        vmem(wide, LOW),
        vmem(wide, F32),
        vmem((padded, LANES), F32),
        vmem(wide, LOW),
        vmem((model, padded), LOW),
        vmem((padded, 3 * model), LOW),
        vmem((pairs, 2 * padded, padded), LOW),
        vmem(wide, LOW),
        vmem((model, padded), LOW),
        vmem(wide, F32),
        vmem(wide, F32),
        vmem((padded, LANES), F32),
        vmem(wide, LOW),
        vmem((model, padded), LOW),
        vmem((padded, hidden_units), LOW),
        vmem((hidden_units, padded), LOW),
        vmem((padded, hidden_units), LOW),
        vmem((padded, hidden_units), F32),
        vmem(wide, F32),
        vmem(wide, LOW),
        vmem((16, model), F32),
    ]
    scratch += [vmem((2, 3, n * r, w), LOW) for r, w in zip(height, sixth)]
    scratch += [vmem((3, n * r, w), LOW) for r, w in zip(height, sixth)]
    slots = (3, 3, 2, 2)
    scratch += [vmem((n * height[m], sixth[m]), LOW) for m in (UP, DOWN)]
    scratch += [vmem((k, reach[0], r, w), LOW) for k, r, w in zip(slots, height, sixth)]
    scratch += [vmem((k, max(reach[1], 1), r, w), LOW) for k, r, w in zip(slots, height, sixth)]
    scratch += [vmem((k - 1 + k // 3, r, w), LOW) for k, r, w in zip(slots, height, sixth)]
    scratch += [
        vmem((n,) + line.shape, LOW),
        vmem((16, model), F32),
        vmem((8, hidden_units), F32),
        vmem((n,) + line.shape, F32),
        vmem((reach[0],) + line.shape, F32),
        vmem((max(reach[1], 1),) + line.shape, F32),
    ]
    scratch += [
        dma((3,)),
        dma((4, 3)),
        dma((4, 2, 2, reach[0])),
        dma((4, 2, 2, reach[0])),
        dma((4, n - 1)),
        dma((4, n - 1)),
        dma((4, 3)),
        dma((4, 3)),
        dma((2, reach[0])),
        dma((2, reach[0])),
        dma((4, 3)),
        dma((4, 3)),
        dma((4, 2, reach[0] + 1)),
        dma((4, 2, reach[0] + 1)),
        dma((4, 3, 2, reach[0])),
        dma((4, 3, 2, reach[0])),
        dma((4, 3, 2)),
        dma((4, 3, 2)),
        dma((2, reach[0])),
        dma((2, reach[0])),
        dma((2,)),
        dma((2,)),
        vmem((4,) + line.shape, F32),
        vmem((8, 3 * model), F32),
        vmem((2, 2 * padded, 2 * HEAD_DIM), LOW),
    ]
    anywhere = pl.BlockSpec(memory_space=pl.ANY)
    near = pl.BlockSpec(memory_space=pltpu.VMEM)
    return pl.pallas_call(
        functools.partial(layer_kernel, n, length, padded, model),
        out_shape=[jax.ShapeDtypeStruct(layer_input.shape, LOW)] * 2
        + [jax.ShapeDtypeStruct(a.shape, LOW) for a in matrices]
        + [jax.ShapeDtypeStruct(line.shape, F32)],
        in_specs=[anywhere] * 2 + [pl.BlockSpec(memory_space=pltpu.SMEM)] + [anywhere] * 5,
        out_specs=[near] * 7,
        scratch_shapes=scratch,
        compiler_params=pltpu.CompilerParams(
            collective_id=0, has_side_effects=True, vmem_limit_bytes=60 * 1024 * 1024
        ),
        name="layer",
    )(layer_input, cotangent, live, *matrices, line)


norm_eps = 1e-06
root_half = 0.7071067811865476
density_coef = 0.3989422804014327


def matmul(operand, factor):
    flat = operand.reshape(-1, operand.shape[-1])
    product = jnp.dot(flat, factor, preferred_element_type=jnp.float32)
    return product.reshape(operand.shape[:-1] + (factor.shape[-1],))


def outer_product(operand, factor):
    return jnp.dot(
        operand.reshape(-1, operand.shape[-1]).T,
        factor.reshape(-1, factor.shape[-1]),
        preferred_element_type=jnp.float32,
    )


def batched(form, operand, factor):
    return jnp.einsum(form, operand, factor, preferred_element_type=jnp.float32)


def layer_norm(values, norm_gain, norm_bias):
    average = jnp.mean(values, axis=-1, keepdims=True)
    centred = values - average
    spread = jnp.mean(centred * centred, axis=-1, keepdims=True)
    inv_std = lax.rsqrt(spread + norm_eps)
    hat_vals = centred * inv_std
    return (
        hat_vals * norm_gain.astype(jnp.float32) + norm_bias.astype(jnp.float32),
        hat_vals,
        inv_std,
    )


def norm_back(incoming, hat_vals, inv_std, norm_gain):
    scaled = incoming * norm_gain.astype(jnp.float32)
    return inv_std * (
        scaled
        - jnp.mean(scaled, axis=-1, keepdims=True)
        - hat_vals * jnp.mean(scaled * hat_vals, axis=-1, keepdims=True)
    )


def forward_pass(params, layer_input, live):
    (
        first_gain,
        first_bias,
        qkv_weight,
        query_bias,
        value_bias,
        out_weight,
        out_bias,
        second_gain,
        second_bias,
        up_weight,
        up_bias,
        down_weight,
        down_bias,
    ) = params
    images, length, model_width = layer_input.shape
    head_count = model_width // HEAD_DIM
    score_scale = HEAD_DIM ** (-0.5)
    stream = layer_input.astype(jnp.float32)
    normed, first_hat, first_inv = layer_norm(stream, first_gain, first_bias)
    normed = normed.astype(jnp.bfloat16)
    projected = matmul(normed, qkv_weight)
    shape_heads = (images, length, head_count, HEAD_DIM)
    queries = (
        (projected[..., :model_width] + query_bias.astype(jnp.float32))
        .astype(jnp.bfloat16)
        .reshape(shape_heads)
    )
    key_rows = (
        projected[..., model_width : 2 * model_width].astype(jnp.bfloat16).reshape(shape_heads)
    )
    values = (
        (projected[..., 2 * model_width :] + value_bias.astype(jnp.float32))
        .astype(jnp.bfloat16)
        .reshape(shape_heads)
    )
    scores = batched("bqhd,bkhd->bhqk", queries, key_rows) * score_scale
    log_total = jnp.log(jnp.sum(jnp.exp(scores), axis=-1, keepdims=True))
    weights = jnp.exp(scores - log_total).astype(jnp.bfloat16)
    attended = (
        batched("bhqk,bkhd->bqhd", weights, values)
        .reshape(images, length, model_width)
        .astype(jnp.bfloat16)
    )
    middle = stream + matmul(attended, out_weight) + out_bias.astype(jnp.float32)
    second_normed, second_hat, second_inv = layer_norm(middle, second_gain, second_bias)
    second_normed = second_normed.astype(jnp.bfloat16)
    hidden_pre = matmul(second_normed, up_weight) + up_bias.astype(jnp.float32)
    normal_cdf = 0.5 * (1.0 + lax.erf(hidden_pre * root_half))
    hidden = (hidden_pre * normal_cdf).astype(jnp.bfloat16)
    result = middle + matmul(hidden, down_weight) + down_bias.astype(jnp.float32)
    image_mask = live.astype(jnp.float32)[:, None, None]
    output = (result * image_mask).astype(jnp.bfloat16)
    saved = (
        normed,
        first_hat,
        first_inv,
        queries,
        key_rows,
        values,
        log_total,
        attended,
        second_normed,
        second_hat,
        second_inv,
        hidden_pre,
        normal_cdf,
        hidden,
        image_mask,
    )
    return (output, saved)


def backward_pass(params, saved, cotangent):
    (
        first_gain,
        first_bias,
        qkv_weight,
        query_bias,
        value_bias,
        out_weight,
        out_bias,
        second_gain,
        second_bias,
        up_weight,
        up_bias,
        down_weight,
        down_bias,
    ) = params
    (
        normed,
        first_hat,
        first_inv,
        queries,
        key_rows,
        values,
        log_total,
        attended,
        second_normed,
        second_hat,
        second_inv,
        hidden_pre,
        normal_cdf,
        hidden,
        image_mask,
    ) = saved
    images, length, head_count, head_width = queries.shape
    flat_shape = (images, length, head_count * head_width)
    score_scale = HEAD_DIM ** (-0.5)
    upstream = cotangent.astype(jnp.float32) * image_mask
    upstream_low = upstream.astype(jnp.bfloat16)
    down_weight_grad = outer_product(hidden, upstream_low)
    down_bias_grad = jnp.sum(upstream, axis=(0, 1))
    hidden_grad = matmul(upstream_low, down_weight.T)
    density = jnp.exp(-0.5 * hidden_pre * hidden_pre) * density_coef
    pre_grad = hidden_grad * (normal_cdf + hidden_pre * density)
    pre_low = pre_grad.astype(jnp.bfloat16)
    up_weight_grad = outer_product(second_normed, pre_low)
    up_bias_grad = jnp.sum(pre_grad, axis=(0, 1))
    second_in = matmul(pre_low, up_weight.T)
    second_gain_grad = jnp.sum(second_in * second_hat, axis=(0, 1))
    second_bias_grad = jnp.sum(second_in, axis=(0, 1))
    middle_grad = upstream + norm_back(second_in, second_hat, second_inv, second_gain)
    middle_low = middle_grad.astype(jnp.bfloat16)
    out_weight_grad = outer_product(attended, middle_low)
    out_bias_grad = jnp.sum(middle_grad, axis=(0, 1))
    attended_grad = matmul(middle_low, out_weight.T).astype(jnp.bfloat16).reshape(queries.shape)
    again_scores = batched("bqhd,bkhd->bhqk", queries, key_rows) * score_scale
    probs = jnp.exp(again_scores - log_total)
    probs_low = probs.astype(jnp.bfloat16)
    value_grad = batched("bhqk,bqhd->bkhd", probs_low, attended_grad)
    prob_grad = batched("bqhd,bkhd->bhqk", attended_grad, values)
    score_grad = (
        probs * (prob_grad - jnp.sum(probs * prob_grad, axis=-1, keepdims=True)) * score_scale
    ).astype(jnp.bfloat16)
    query_grad = batched("bhqk,bkhd->bqhd", score_grad, key_rows).reshape(flat_shape)
    key_grad = batched("bhqk,bqhd->bkhd", score_grad, queries).reshape(flat_shape)
    value_grad = value_grad.reshape(flat_shape)
    joined = jnp.concatenate([query_grad, key_grad, value_grad], axis=-1).astype(jnp.bfloat16)
    qkv_weight_grad = outer_product(normed, joined)
    query_bias_grad = jnp.sum(query_grad, axis=(0, 1))
    value_bias_grad = jnp.sum(value_grad, axis=(0, 1))
    first_in = matmul(joined, qkv_weight.T)
    first_gain_grad = jnp.sum(first_in * first_hat, axis=(0, 1))
    first_bias_grad = jnp.sum(first_in, axis=(0, 1))
    middle_grad = middle_grad + norm_back(first_in, first_hat, first_inv, first_gain)
    input_grad = middle_grad.astype(jnp.bfloat16)
    grads = (
        first_gain_grad,
        first_bias_grad,
        qkv_weight_grad,
        query_bias_grad,
        value_bias_grad,
        out_weight_grad,
        out_bias_grad,
        second_gain_grad,
        second_bias_grad,
        up_weight_grad,
        up_bias_grad,
        down_weight_grad,
        down_bias_grad,
    )
    return (input_grad, grads)


def places(n):
    rep = lax.axis_index("rep")
    me = lax.axis_index("shard")
    core = rep % 2
    row = rep // 2
    position = ring_position(me, n)
    right = (rep, ring_index((position + 1) % n, n))
    left = (rep, ring_index((position + n - 1) % n, n))
    partner = (row * 2 + 1 - core, me)
    across = ((1 - row) * 2 + core, me)
    return me, core, row, position, right, left, partner, across


def greet(peers):
    barrier = pltpu.get_barrier_semaphore()
    for peer in peers:
        pl.semaphore_signal(barrier, inc=1, device_id=peer, device_id_type=MESH)
    pl.semaphore_wait(barrier, len(peers))


def remote(source, target, send, recv, device):
    return pltpu.make_async_remote_copy(
        src_ref=source,
        dst_ref=target,
        send_sem=send,
        recv_sem=recv,
        device_id=device,
        device_id_type=MESH,
    )


def window(refs, side, part, block, width):
    qkv, out, up, down = refs
    if side == 2:
        return [(None, down.at[block, part])]
    if side == 1:
        return [(None, up.at[block, :, pl.ds(pl.multiple_of(part * width, width), width)])]
    inner = part - part // 3
    return [
        (part < 3, qkv.at[block, :, pl.ds(pl.multiple_of(inner * width, width), width)]),
        (part == 3, out.at[block]),
    ]


def start_each(views, make):
    for condition, view in views:
        if condition is None:
            make(view).start()
        else:
            pl.when(condition)(make(view).start)


def gather_kernel(
    n,
    width,
    qkv_in,
    out_in,
    up_in,
    down_in,
    line_in,
    qkv_ref,
    out_ref,
    up_ref,
    down_ref,
    line_ref,
    local_sem,
    ring_s,
    ring_r,
    core_s,
    core_r,
    row_s,
    row_r,
    last_s,
    last_r,
    line_s,
    line_r,
):
    me, core, row, position, right, left, partner, across = places(n)
    refs = (qkv_ref, out_ref, up_ref, down_ref)
    pairs = zip((qkv_in, out_in, up_in, down_in, line_in), refs + (line_ref,))
    locals_ = [
        pltpu.make_async_copy(source, target.at[me], local_sem.at[i])
        for i, (source, target) in enumerate(pairs)
    ]
    for copy in locals_:
        copy.start()
    greet((right, left, partner, across))
    for copy in locals_:
        copy.wait()

    def block(way, r):
        return ring_index((position + (1 if way else n - 1) * r) % n, n)

    def views(i, r, whose):
        way, kind = i // 2, i % 2
        side, part = (2, 2 * whose + way) if kind else (way, 2 * whose + row)
        return window(refs, side, part, block(way, r), width)

    def over(way, r, whose):
        return window(refs, way, 2 * whose + 1 - row, block(way, r), width)

    def ring(i, r):
        peer = left if i // 2 else right
        return lambda v: remote(v, v, ring_s.at[i, r], ring_r.at[i, r], peer)

    def to_core(i, r):
        return lambda v: remote(v, v, core_s.at[i, r], core_r.at[i, r], partner)

    def to_row(way, r):
        return lambda v: remote(v, v, row_s.at[way, r], row_r.at[way, r], across)

    def to_last(way, r):
        return lambda v: remote(v, v, last_s.at[way, r], last_r.at[way, r], partner)

    def line(r):
        view = line_ref.at[block(0, r)]
        return remote(view, view, line_s.at[r], line_r.at[r], right)

    def one(vs):
        return vs[0][1]

    for i in range(4):
        start_each(views(i, 0, core), ring(i, 0))
    line(0).start()

    def relay(r):
        for way in range(2):
            to_row(way, r)(one(over(way, r + 1, core))).wait_recv()
            start_each(over(way, r + 1, core), to_last(way, r))

    def step(r, carry):
        for i in (0, 2, 1, 3):
            got = views(i, r + 1, core)
            ring(i, r)(one(got)).wait_recv()

            @pl.when(r < n - 2)
            def _():
                start_each(got, ring(i, r + 1))

            if i % 2 == 0:
                start_each(got, to_row(i // 2, r))
            start_each(got, to_core(i, r))
        line(r).wait_recv()

        @pl.when(r < n - 2)
        def _():
            line(r + 1).start()

        @pl.when(r > 0)
        def _():
            relay(r - 1)

        return carry

    lax.fori_loop(0, n - 1, step, 0)
    relay(n - 2)

    def finish(r, carry):
        for i in range(4):
            view = one(views(i, r, core))
            ring(i, r)(view).wait_send()
            to_core(i, r)(view).wait_send()
            to_core(i, r)(view).wait_recv()
        for way in range(2):
            view = one(views(2 * way, r, core))
            to_row(way, r)(view).wait_send()
            to_last(way, r)(view).wait_send()
            to_last(way, r)(view).wait_recv()
        line(r).wait_send()
        return carry

    lax.fori_loop(0, n - 1, finish, 0)


def gather_all(arrays, n, width):
    dma = pltpu.SemaphoreType.DMA
    return pl.pallas_call(
        functools.partial(gather_kernel, n, width),
        out_shape=[jax.ShapeDtypeStruct((n,) + a.shape, a.dtype) for a in arrays],
        in_specs=[pl.BlockSpec(memory_space=pltpu.VMEM)] * len(arrays),
        out_specs=[pl.BlockSpec(memory_space=pl.ANY)] * len(arrays),
        scratch_shapes=[dma((len(arrays),))]
        + [dma((4, n - 1))] * 4
        + [dma((2, n - 1))] * 4
        + [dma((n - 1,))] * 2,
        compiler_params=pltpu.CompilerParams(collective_id=0, has_side_effects=True),
        name="gather_all",
    )(*arrays)


def reduce_kernel(
    n,
    width,
    qkv_ref,
    out_ref,
    up_ref,
    down_ref,
    line_ref,
    sums,
    line_out,
    own,
    given,
    arrive,
    over,
    other,
    line_send,
    line_got,
    line_pair,
    own_sem,
    given_s,
    given_r,
    ring_s,
    ring_r,
    row_s,
    row_r,
    end_row_s,
    end_row_r,
    end_core_s,
    end_core_r,
    line_s,
    line_r,
    pair_s,
    pair_r,
):
    me, core, row, position, right, left, partner, across = places(n)
    refs = (qkv_ref, out_ref, up_ref, down_ref)
    f32 = jnp.float32

    def block(way, k):
        return ring_index((position + (1 if way else n - 1) * (k + 1)) % n, n)

    def source(i, k, whose):
        way, kind = i % 2, i // 2
        side, part = (
            (way, 2 * whose + row),
            (2, 2 * whose + way),
            (way, 2 * whose + 1 - row),
        )[kind]
        return window(refs, side, part, block(way, k), width)

    def load(i, k):
        return lambda v: pltpu.make_async_copy(v, own.at[i, k], own_sem.at[i, k])

    def give(i, k):
        return lambda v: remote(v, given.at[i, k], given_s.at[i, k], given_r.at[i, k], partner)

    def ring(i, k):
        peer = left if i % 2 else right
        return remote(own.at[i, k], arrive.at[i, k], ring_s.at[i, k], ring_r.at[i, k], peer)

    def to_row(way, k):
        return remote(
            own.at[4 + way, k], over.at[way, k], row_s.at[way, k], row_r.at[way, k], across
        )

    def line_ring(k):
        return remote(line_send.at[k], line_got.at[k], line_s.at[k], line_r.at[k], right)

    order = (4, 5, 2, 3, 0, 1)

    def loads(k, carry):
        for i in order:
            start_each(source(i, k, core), load(i, k))
        return carry

    lax.fori_loop(0, n, loads, 0)
    greet((right, left, partner, across))

    def gives(k, carry):
        for i in order:
            start_each(source(i, k, 1 - core), give(i, k))
        return carry

    lax.fori_loop(0, n, gives, 0)

    def take(i, k):
        view = source(i, k, core)[0][1]
        load(i, k)(view).wait()
        give(i, k)(view).wait_recv()
        return own[i, k].astype(f32) + given[i, k].astype(f32)

    def put(i, k, total):
        own[i, k] = total.astype(own.dtype)

    def ahead(k):
        for way in range(2):
            put(4 + way, k, take(4 + way, k))
            to_row(way, k).start()

    def partial(i, k, first):
        total = take(i, k)
        if i < 2:
            to_row(i, k).wait_recv()
            total = total + over[i, k].astype(f32)
        if not first:
            ring(i, k - 1).wait_recv()
            total = total + arrive[i, k - 1].astype(f32)
        return total

    ahead(0)
    line_send[0] = line_ref[block(0, 0)]
    line_ring(0).start()
    ahead(1)
    for i in (2, 3, 0, 1):
        put(i, 0, partial(i, 0, True))
        ring(i, 0).start()

    def step(k, carry):
        ahead(k + 1)
        for i in (2, 3, 0, 1):
            put(i, k, partial(i, k, False))
            ring(i, k).start()
        line_ring(k - 1).wait_recv()
        line_send[k] = line_ref[block(0, k)] + line_got[k - 1]
        line_ring(k).start()
        return carry

    lax.fori_loop(1, n - 1, step, 0)

    def end_row(i, k=None):
        if i < 2:
            view = sums.at[i, 2 * core + row]
            return remote(view, view, end_row_s.at[i], end_row_r.at[i], across)
        return remote(
            own.at[i, n - 1], other.at[i - 2], end_row_s.at[i], end_row_r.at[i], across
        )

    def end_core(j, side, part):
        view = sums.at[side, part]
        return remote(view, view, end_core_s.at[j], end_core_r.at[j], partner)

    for i in (2, 3):
        put(i, n - 1, partial(i, n - 1, False))
        end_row(i).start()
    line_ring(n - 2).wait_recv()
    line_pair[0] = line_ref[me] + line_got[n - 2]
    pair_row = remote(line_pair.at[0], line_pair.at[1], pair_s.at[0], pair_r.at[0], across)
    pair_row.start()
    for way in (0, 1):
        sums[way, 2 * core + row] = partial(way, n - 1, False).astype(sums.dtype)
        end_row(way).start()
        end_core(way, way, 2 * core + row).start()
    pair_row.wait()
    line_pair[2] = line_pair[0] + line_pair[1]
    pair_core = remote(line_pair.at[2], line_pair.at[3], pair_s.at[1], pair_r.at[1], partner)
    pair_core.start()
    for way in (0, 1):
        end_row(2 + way).wait_recv()
        total = own[2 + way, n - 1].astype(f32) + other[way].astype(f32)
        sums[2, 2 * core + way] = total.astype(sums.dtype)
        end_core(2 + way, 2, 2 * core + way).start()
    for way in (0, 1):
        end_row(way).wait_recv()
        end_core(4 + way, way, 2 * core + 1 - row).start()
    pair_core.wait()
    line_out[...] = line_pair[2] + line_pair[3]
    for i in range(4):
        end_row(i).wait_send()
    for j in range(6):
        copy = end_core(j, 0, 0)
        copy.wait_send()
        copy.wait_recv()

    def finish(k, carry):
        for i in range(6):
            give(i, k)(source(i, k, core)[0][1]).wait_send()
        for way in range(2):
            to_row(way, k).wait_send()
        return carry

    lax.fori_loop(0, n, finish, 0)

    def finish_ring(k, carry):
        for i in range(4):
            ring(i, k).wait_send()
        line_ring(k).wait_send()
        return carry

    lax.fori_loop(0, n - 1, finish_ring, 0)


def reduce_all(arrays, n, width):
    dma = pltpu.SemaphoreType.DMA
    vmem = pltpu.VMEM
    rows = arrays[0].shape[1]
    low = arrays[0].dtype
    line = arrays[-1].shape[1:]
    anywhere = pl.BlockSpec(memory_space=pl.ANY)
    near = pl.BlockSpec(memory_space=pltpu.VMEM)
    return pl.pallas_call(
        functools.partial(reduce_kernel, n, width),
        out_shape=[
            jax.ShapeDtypeStruct((3, 4, rows, width), low),
            jax.ShapeDtypeStruct(line, jnp.float32),
        ],
        in_specs=[anywhere] * 4 + [near],
        out_specs=[near, near],
        scratch_shapes=[
            vmem((6, n, rows, width), low),
            vmem((6, n, rows, width), low),
            vmem((4, n - 1, rows, width), low),
            vmem((2, n, rows, width), low),
            vmem((2, rows, width), low),
            vmem((n - 1,) + line, jnp.float32),
            vmem((n - 1,) + line, jnp.float32),
            vmem((4,) + line, jnp.float32),
            dma((6, n)),
            dma((6, n)),
            dma((6, n)),
            dma((4, n - 1)),
            dma((4, n - 1)),
            dma((2, n)),
            dma((2, n)),
            dma((4,)),
            dma((4,)),
            dma((6,)),
            dma((6,)),
            dma((n - 1,)),
            dma((n - 1,)),
            dma((2,)),
            dma((2,)),
        ],
        compiler_params=pltpu.CompilerParams(
            collective_id=1, has_side_effects=True, vmem_limit_bytes=56 * 1024 * 1024
        ),
        name="reduce_all",
    )(*arrays)


def per_device_in_parts(n, layer_input, cotangent, live, *params):
    width = params[0].shape[0] * n
    rows = params[0].shape[0]
    matrices = [i for i, p in enumerate(params) if p.ndim == 2]
    vectors = [i for i, p in enumerate(params) if p.ndim == 1]
    shapes = [params[i].shape for i in matrices]
    assert shapes == [(rows, 3 * width), (rows, width), (rows, 4 * width), (4 * rows, width)]
    lengths = [params[i].shape[0] for i in vectors]
    tall = -(-sum(lengths) // (16 * LANES)) * 16
    spare = tall * LANES - sum(lengths)

    line = jnp.concatenate([params[i] for i in vectors] + [jnp.zeros(spare, params[0].dtype)])
    sent = [params[i] for i in matrices]
    sent[3] = sent[3].reshape(4, rows, width)
    *full, lines = gather_all(sent + [line.reshape(tall, LANES)], n, width)
    gathered = [None] * len(params)
    for i, array in zip(matrices, full):
        gathered[i] = array.reshape(n * params[i].shape[0], params[i].shape[1])
    tail = lines.reshape(n, -1)
    at = 0
    for i, length in zip(vectors, lengths):
        gathered[i] = tail[:, at : at + length].reshape(-1)
        at += length

    output, saved = forward_pass(gathered, layer_input, live)
    input_grad, grads = backward_pass(gathered, saved, cotangent)

    low = jnp.bfloat16
    blocks = [grads[i].astype(low).reshape((n,) + a.shape) for i, a in zip(matrices, sent)]
    parts = [grads[i].reshape(n, -1) for i in vectors] + [jnp.zeros((n, spare), jnp.float32)]
    blocks.append(jnp.concatenate(parts, axis=1).reshape(n, tall, LANES))
    sums, tail = reduce_all(blocks, n, width)

    def joined(pieces):
        return jnp.swapaxes(pieces, 0, 1).reshape(rows, -1).astype(jnp.float32)

    results = [None] * len(params)
    whole = (
        joined(sums[0, :3]),
        sums[0, 3].astype(jnp.float32),
        joined(sums[1]),
        sums[2].reshape(4 * rows, width).astype(jnp.float32),
    )
    for i, array in zip(matrices, whole):
        results[i] = array
    tail = tail.reshape(-1)
    at = 0
    for i, length in zip(vectors, lengths):
        results[i] = tail[at : at + length]
        at += length
    return (output, input_grad, *results)


VECTORS = (0, 1, None, 2, 3, None, 4, 5, 6, None, 8, None, 7)


def per_device(n, layer_input, cotangent, live, *params):
    rows = params[0].shape[0]
    if rows % 16 or layer_input.shape[0] != 1:
        return per_device_in_parts(n, layer_input, cotangent, live, *params)
    matrices = [p for p in params if p.ndim == 2]
    order = sorted((place, i) for i, place in enumerate(VECTORS) if place is not None)
    stack = jnp.concatenate([params[i].reshape(-1, rows) for _, i in order])
    line = jnp.pad(stack, ((0, 16 - stack.shape[0]), (0, LANES - rows)))
    output, input_grad, *sums, tail = run_layer(layer_input, cotangent, live, matrices, line, n)
    results = []
    for i, p in enumerate(params):
        if p.ndim == 2:
            results.append(sums.pop(0).astype(F32))
        else:
            first = VECTORS[i]
            results.append(tail[first : first + p.shape[0] // rows, :rows].reshape(-1))
    return (output, input_grad, *results)


def solution(mesh):
    whole = P(("rep", "shard"), None, None)
    vector, matrix = P("shard"), P("shard", None)
    ranks = (1, 1, 2, 1, 1, 2, 1, 1, 1, 2, 1, 2, 1)
    params = tuple(matrix if rank == 2 else vector for rank in ranks)
    return jax.shard_map(
        functools.partial(per_device, mesh.shape["shard"]),
        mesh=mesh,
        in_specs=(whole, whole, P(("rep", "shard"))) + params,
        out_specs=(whole, whole) + params,
        check_vma=False,
    )
```

```python
import functools

import jax
import jax.numpy as jnp
from jax import lax
from jax.experimental import pallas as pl
from jax.experimental.pallas import tpu as pltpu
from jax.sharding import PartitionSpec as P

HEAD_DIM = 64
LANES = 128
NORM_EPS = 1e-06
ROOT_HALF = 0.7071067811865476
DENSITY_COEF = 0.3989422804014327
MESH = pl.DeviceIdType.MESH
F32 = jnp.float32
LOW = jnp.bfloat16

QKV, OUT, UP, DOWN = range(4)
SHARED, MINE, YOURS = range(3)


def ring_index(position, n):
    half = position // (n // 2)
    return (1 - half) * 2 * position + half * (2 * (n - 1 - position) + 1)


def ring_position(index, n):
    odd = index % 2
    step = index // 2
    return (1 - odd) * step + odd * (n - 1 - step)


def remote(source, target, send, recv, device):
    return pltpu.make_async_remote_copy(
        src_ref=source,
        dst_ref=target,
        send_sem=send,
        recv_sem=recv,
        device_id=device,
        device_id_type=MESH,
    )


def dot_nn(a, b):
    return jnp.dot(a, b, preferred_element_type=F32)


def dot_nt(a, b):
    return lax.dot_general(a, b, (((1,), (1,)), ((), ())), preferred_element_type=F32)


def dot_tn(a, b):
    return lax.dot_general(a, b, (((0,), (0,)), ((), ())), preferred_element_type=F32)


def split(refs, counts):
    at = 0
    for count in counts:
        yield refs[at : at + count]
        at += count

ORDER = (
    "GO", "GU", "gQ0", "gO0", "l0", "gU0", "gQ1", "gO1", "l1", "GD", "gU1", "gQ2", "gO2", "l2",
    "gU2", "gQ3", "gO3", "l3", "RQ", "RO", "gD0", "v", "EQ", "p", "gU3", "RU", "gD1", "a0", "EO",
    "a1", "gD2", "m", "t", "EU", "u0", "u1", "dDs", "dDy", "gD3", "RD", "dDm", "oD0", "Ds0", "oD1",
    "oD2", "oD3", "Dm0", "ED", "hb", "dUs", "dUy", "dUm", "Ds1", "Us0", "Dm1", "sb", "nb", "dOs",
    "dOm", "dOy", "oU0", "Ds2", "oU1", "oU2", "oU3", "ob", "Dm2", "Us1", "Os0", "Om0", "Oy0", "ab0",
    "Ds3", "Dm3", "ab1", "Um0", "dQs", "dQm", "dQy", "Us2", "Um1", "Qs0", "Qm0", "Qy0", "Os1",
    "Om1", "Oy1", "Ds", "Dm", "Us3", "Um2", "Qs1", "Qm1", "Qy1", "fb", "fn", "t0", "XD", "Um3",
    "Us", "Os2", "Om2", "Oy2", "Qs2", "Qm2", "Qy2", "t1", "c", "Um", "Os3", "Om3", "Oy3", "Qs3",
    "Qm3", "Qy3", "t2", "XU", "Os", "Om", "Oy", "t3", "Qs", "Qm", "Qy", "te", "XO", "tp", "XQ",
    "tf", "FQ", "FO", "FU", "FD",
)


def pack_layout(rows, padded, model):
    layout, first = [], 0
    for name, high, parts, width in (
        ("FD", 4 * rows, 1, model),
        ("FU", rows, 4, model),
        ("FQ", rows, 3, model),
        ("FO", rows, 1, model),
        ("c", padded, 1, model),
        ("fn", padded, 1, model),
        ("tf", 16, 1, 2 * LANES),
    ):
        for k in range(parts):
            layout.append((name, first, high, k * width, width))
            first += high
    return layout


def layer_kernel(n, length, padded, model, *refs):
    ins, outs, weights, acts, halves, given, over, arrive_a, arrive_b, extra, sems = split(
        refs, (7 + 9, 1, 4, 23, 4, 4, 2, 4, 4, 4 + 6, 25 + 9)
    )
    over = dict(zip((UP, DOWN), over))
    x_in, cot_in, live_in, qkv_in, out_in, up_in, down_in, *vectors_in = ins
    (packed,) = outs
    output_low, input_grad_low, *sums, line_low, line_wide, pack_sem = sems[25:]
    (
        x_low,
        cot_low,
        upstream,
        hat1,
        inv1,
        normed,
        normed_t,
        qkv,
        probs,
        attended,
        attended_t,
        middle,
        hat2,
        inv2,
        second,
        second_t,
        hidden,
        hidden_t,
        pre_low,
        slope,
        incoming,
        middle_low,
        vec_grad,
    ) = acts
    joined, middle_grad, head_grad = qkv, hat2, normed
    exchange, (lines, vec, up_bias, line_grad, line_a, line_b) = extra[:4], extra[4:]
    (
        in_sem,
        own_sem,
        ring_s,
        ring_r,
        row_s,
        row_r,
        core_s,
        core_r,
        line_s,
        line_r,
        give_s,
        give_r,
        over_s,
        over_r,
        sum_s,
        sum_r,
        end_s,
        end_r,
        tail_s,
        tail_r,
        pair_s,
        pair_r,
    ) = sems[:22]
    line_pair = sems[22]
    pre_bias, score_rows = sems[23], sems[24]

    rows = qkv_in.shape[0]
    height = [ref.shape[0] for ref in (qkv_in, out_in, up_in, down_in)]
    sixth = [ref.shape[1] // 6 for ref in (qkv_in, out_in, up_in, down_in)]
    matrix_in = (qkv_in, out_in, up_in, down_in)
    hidden_units = up_in.shape[1]
    reach = (n // 2, n // 2 - 1)

    rep = lax.axis_index("rep")
    me = lax.axis_index("shard")
    core = rep % 2
    row = rep // 2
    position = ring_position(me, n)
    sign = 1 - 2 * core

    def at(k):
        return ring_index((position + sign * k + n) % n, n)

    peers = ((rep, at(1)), (rep, at(-1)))
    partner = (row * 2 + 1 - core, me)
    across = ((1 - row) * 2 + core, me)
    third = (2, row, 1 - row)

    def block(m, b):
        return pl.ds(pl.multiple_of(b * height[m], height[m]), height[m])

    def columns(m, slot, whose):
        width = sixth[m]
        return pl.ds(pl.multiple_of((2 * third[slot] + whose) * width, width), width)

    def piece(m, b, slot):
        return weights[m].at[block(m, b), columns(m, slot, core)]

    def came(d, h):
        return at(-1 - h) if d == 0 else at(1 + h)

    def own_copy(m, slot):
        return pltpu.make_async_copy(
            matrix_in[m].at[:, columns(m, slot, core)], piece(m, me, slot), own_sem.at[m, slot]
        )

    def gather_send(m, slot, d, h):
        view = piece(m, at(-h) if d == 0 else at(h), slot)
        return remote(view, view, ring_s.at[m, slot, d, h], ring_r.at[m, slot, d, h], peers[d])

    def gather_row(m, d, h, slot):
        view = piece(m, came(d, h), slot)
        k = d * reach[0] + h
        return remote(view, view, row_s.at[m, k], row_r.at[m, k], across)

    def gather_core(m, slot, whose):
        view = weights[m].at[:, columns(m, slot, whose)]
        return remote(view, view, core_s.at[m, slot], core_r.at[m, slot], partner)

    def gather_start(m):
        for slot in (MINE, SHARED):
            for d in (0, 1):
                gather_send(m, slot, d, 0).start()

    def gather_hop(m, h, slots=(MINE, SHARED)):
        for slot in slots:
            for d in (0, 1):
                if h < reach[d]:
                    view = piece(m, came(d, h), slot)
                    remote(
                        view, view, ring_s.at[m, slot, d, h], ring_r.at[m, slot, d, h], peers[d]
                    ).wait_recv()
                    if h + 1 < reach[d]:
                        gather_send(m, slot, d, h + 1).start()
                    if slot == MINE:
                        gather_row(m, d, h, MINE).start()

    def gather_relay(m):
        for slot in (MINE, SHARED):
            gather_core(m, slot, core).start()

    def gather_end(m):
        for d in (0, 1):
            for h in range(reach[d]):
                gather_row(m, d, h, YOURS).wait_recv()
        gather_core(m, YOURS, core).start()
        for slot in (MINE, SHARED, YOURS):
            gather_core(m, slot, 1 - core).wait_recv()

    def line_send(d, h):
        view = lines.at[at(-h) if d == 0 else at(h)]
        return remote(view, view, line_s.at[d, h], line_r.at[d, h], peers[d])

    def line_hop(h):
        for d in (0, 1):
            if h < reach[d]:
                view = lines.at[came(d, h)]
                remote(view, view, line_s.at[d, h], line_r.at[d, h], peers[d]).wait_recv()
                if h + 1 < reach[d]:
                    line_send(d, h + 1).start()

    def slots_of(m):
        return (SHARED, MINE) if m in over else (SHARED, MINE, YOURS)

    def owner(d, t):
        return at(reach[0] - t) if d == 0 else at(t - reach[1])

    def give(m, slot):
        return remote(
            halves[m].at[1, slot],
            given[m].at[slot],
            give_s.at[m, slot],
            give_r.at[m, slot],
            partner,
        )

    def hand_over(m, d, t):
        rows_of = block(m, owner(d, t))
        return remote(
            halves[m].at[0, YOURS, rows_of],
            over[m].at[rows_of],
            over_s.at[m, d, t],
            over_r.at[m, d, t],
            across,
        )

    def local(m, slot, b):
        total = halves[m][0, slot, block(m, b)].astype(F32) + given[m][slot, block(m, b)].astype(
            F32
        )
        if slot == MINE and m in over:
            total = total + over[m][block(m, b)].astype(F32)
        return total

    def ring_sum(m, slot, d, t):
        return remote(
            halves[m].at[0, slot, block(m, owner(d, t))],
            (arrive_a, arrive_b)[d][m].at[slot, t],
            sum_s.at[m, slot, d, t],
            sum_r.at[m, slot, d, t],
            peers[d],
        )

    def over_steps():
        return [(d, t) for t in range(reach[0] + 1) for d in (0, 1) if t < reach[d] + 1 - d]

    def reduce_over(m, p):
        if p == 0:
            give(m, YOURS).wait_recv()
        for d, t in over_steps():
            if min(t * 4 // reach[0], 3) == p:
                rows_of = block(m, owner(d, t))
                halves[m][0, YOURS, rows_of] = local(m, YOURS, owner(d, t)).astype(LOW)
                hand_over(m, d, t).start()

    def reduce_step(m, slot, t):
        if t == 0:
            give(m, slot).wait_recv()
        for d in (0, 1):
            if t < reach[d]:
                b = owner(d, t)
                if slot == MINE and m in over:
                    hand_over(m, d, t).wait_recv()
                total = local(m, slot, b)
                if t > 0:
                    ring_sum(m, slot, d, t - 1).wait_recv()
                    total = total + (arrive_a, arrive_b)[d][m][slot, t - 1].astype(F32)
                halves[m][0, slot, block(m, b)] = total.astype(LOW)
                ring_sum(m, slot, d, t).start()

    def sum_columns(m, slot, whose):
        width = sixth[m]
        which = third[slot] if m in over else (2, 0, 1)[slot]
        return pl.ds(pl.multiple_of((2 * which + whose) * width, width), width)

    def end_view(m, slot, whose):
        return sums[m].at[:, sum_columns(m, slot, whose)]

    def end_core(m, slot, whose):
        view = end_view(m, slot, whose)
        return remote(view, view, end_s.at[m, slot, 1], end_r.at[m, slot, 1], partner)

    def end_row(m, slot):
        return remote(
            halves[m].at[0, slot, block(m, me)],
            exchange[m].at[slot],
            end_s.at[m, slot, 0],
            end_r.at[m, slot, 0],
            across,
        )

    def end_other(m, slot):
        view = end_view(m, slot, core)
        return remote(view, view, end_s.at[m, MINE, 0], end_r.at[m, MINE, 0], across)

    def reduce_end(m, slot):
        if slot == MINE and m in over:
            hand_over(m, 0, reach[0]).wait_recv()
        total = local(m, slot, me)
        for d in (0, 1):
            if reach[d]:
                ring_sum(m, slot, d, reach[d] - 1).wait_recv()
                total = total + (arrive_a, arrive_b)[d][m][slot, reach[d] - 1].astype(F32)
        if slot == MINE and m in over:
            sums[m][:, sum_columns(m, MINE, core)] = total.astype(LOW)
            end_other(m, MINE).start()
            end_core(m, MINE, core).start()
        else:
            halves[m][0, slot, block(m, me)] = total.astype(LOW)
            end_row(m, slot).start()

    def reduce_exchange(m):
        for slot in slots_of(m):
            if slot == MINE and m in over:
                end_other(m, YOURS).wait_recv()
                end_core(m, YOURS, core).start()
            else:
                end_row(m, slot).wait_recv()
                total = halves[m][0, slot, block(m, me)].astype(F32) + exchange[m][slot].astype(F32)
                sums[m][:, sum_columns(m, slot, core)] = total.astype(LOW)
                end_core(m, slot, core).start()

    def reduce_finish(m):
        for slot in (SHARED, MINE, YOURS):
            end_core(m, slot, 1 - core).wait_recv()

    steps = padded // 16
    slices = [pl.ds(i * 16, 16) for i in range(steps)]
    gain = lambda i: vec[i : i + 1, :]
    live = live_in[0].astype(F32)
    row_id = lax.broadcasted_iota(jnp.int32, (padded, 1), 0)
    row_mask = (row_id < length).astype(F32)
    pair_width = 2 * HEAD_DIM
    pairs = model // pair_width

    def normalise(source, hat, inv):
        for s in slices:
            values = source[s, :]
            centred = values - jnp.mean(values, axis=-1, keepdims=True)
            spread = jnp.mean(centred * centred, axis=-1, keepdims=True)
            inv_std = lax.rsqrt(spread + NORM_EPS)
            hat[s, :] = centred * inv_std
            inv[s, :] = jnp.broadcast_to(inv_std, (16, LANES))

    def scale_shift(hat, low, g, b, mask):
        for i, s in enumerate(slices):
            value = hat[s, :] * gain(g) + gain(b)
            if mask and (i + 1) * 16 > length:
                value = value * row_mask[i * 16 : (i + 1) * 16]
            low[s, :] = value.astype(LOW)

    def transpose(source, target):
        def body(i, carry):
            cols = pl.ds(pl.multiple_of(i * 256, 256), 256)
            target[cols, :] = source[:, cols].T
            return carry

        lax.fori_loop(0, source.shape[1] // 256, body, 0)

    def begin():
        middle[...] = jnp.zeros_like(middle)
        middle[:length, :] = x_low[0].astype(F32)
        incoming[...] = jnp.zeros_like(incoming)
        incoming[:length, :] = cot_low[0].astype(F32) * live
        upstream[...] = incoming[...].astype(LOW)
        vec_grad[...] = jnp.zeros_like(vec_grad)
        vec_grad[7:8, :] = jnp.sum(incoming[...], axis=0, keepdims=True)
        normalise(middle, hat1, inv1)

    def vectors():
        for b in range(n):
            held = lines[b]
            vec[:, b * rows : (b + 1) * rows] = held[:, :rows]
            for e in range(4 * rows // LANES):
                first = b * 4 * rows + e * LANES
                up_bias[:, first : first + LANES] = jnp.broadcast_to(
                    held[8 + e : 9 + e, :], (8, LANES)
                )

    def first_norm():
        scale_shift(hat1, normed, 0, 1, True)
        transpose(normed, normed_t)
        zero = jnp.zeros((1, model), F32)
        for k, v in enumerate((vec[2:3, :], zero, vec[3:4, :])):
            pre_bias[:, k * model : (k + 1) * model] = jnp.broadcast_to(v, (8, model))

    def project(first, last):
        wide = 2 * sixth[QKV] // 2

        def body(c, carry):
            cols = pl.ds(pl.multiple_of(c * wide, wide), wide)
            value = (dot_nn(normed[...], weights[QKV][:, cols]) + pre_bias[0:1, cols]) * row_mask
            factor = jnp.where(c * wide < model, HEAD_DIM**-0.5, 1.0)
            qkv[:, cols] = (value.astype(LOW).astype(F32) * factor).astype(LOW)
            return carry

        lax.fori_loop(first, last, body, 0)

    lane = lax.broadcasted_iota(jnp.int32, (padded, pair_width), 1)
    low_lane = lane < HEAD_DIM
    key_mask = lax.broadcasted_iota(jnp.int32, (1, padded), 1) < length

    def heads(part, p):
        return qkv[:, pl.ds(pl.multiple_of(part * model + p * pair_width, LANES), pair_width)]

    def stacked(value, target):
        wide = value.astype(F32)
        target[:padded, :] = jnp.where(low_lane, wide, 0.0).astype(LOW)
        target[padded:, :] = jnp.where(low_lane, 0.0, wide).astype(LOW)

    def merged(value):
        return jnp.where(low_lane, value[:padded], value[padded:])

    def attend(first, last):
        def body(p, carry):
            stacked(heads(0, p), score_rows.at[0])
            scores = dot_nt(score_rows[0], heads(1, p))
            powers = jnp.where(key_mask, jnp.exp(scores), 0.0)
            total = jnp.sum(powers, axis=-1, keepdims=True)
            weight = (powers * (1.0 / total)).astype(LOW)
            probs[p] = weight
            cols = pl.ds(pl.multiple_of(p * pair_width, LANES), pair_width)
            attended[:, cols] = merged(dot_nn(weight, heads(2, p))).astype(LOW)
            return carry

        lax.fori_loop(first, last, body, 0)

    def mix():
        def body(c, carry):
            cols = pl.ds(pl.multiple_of(c * 256, 256), 256)
            middle[:, cols] = (
                middle[:, cols] + dot_nn(attended[...], weights[OUT][:, cols]) + vec[4:5, cols]
            )
            return carry

        lax.fori_loop(0, model // 256, body, 0)
        normalise(middle, hat2, inv2)
        scale_shift(hat2, second, 5, 6, False)

    def transposes():
        transpose(attended, attended_t)
        transpose(second, second_t)

    wide_hidden = 512

    def expand(first, last):
        def body(c, carry):
            cols = pl.ds(pl.multiple_of(c * wide_hidden, wide_hidden), wide_hidden)
            pre = dot_nn(second[...], weights[UP][:, cols]) + up_bias[0:1, cols]
            cdf = 0.5 * (1.0 + lax.erf(pre * ROOT_HALF))
            density = jnp.exp(-0.5 * pre * pre) * DENSITY_COEF
            value = (pre * cdf).astype(LOW)
            hidden[:, cols] = value
            slope[:, cols] = cdf + pre * density
            hidden_t[cols, :] = value.T
            return carry

        lax.fori_loop(first, last, body, 0)

    def contract():
        def body(c, carry):
            cols = pl.ds(pl.multiple_of(c * 256, 256), 256)
            value = dot_nn(hidden[...], weights[DOWN][:, cols]) + vec[7:8, cols]
            value = (middle[:, cols] + value) * live
            output_low[:, cols] = value.astype(LOW)
            return carry

        lax.fori_loop(0, model // 256, body, 0)

    def gradient(m, left, right, slot):
        width = sixth[m]
        base = (third[slot] if m in over else (2, 0, 1)[slot]) * 2 * width
        if width % 256 == 0:
            count, step = 2 * width // 256, 256
        elif (2 * width) % 256 == 0 and width < 256:
            count, step = 1, 2 * width
        else:
            count, step = 2, width
        tall = left.shape[0]
        high = min(tall, model)

        def body(i, carry):
            c, r = i % count, i // count
            cols = pl.ds(pl.multiple_of(base + c * step, LANES), step)
            down = pl.ds(pl.multiple_of(r * high, high), high)
            value = dot_nn(left[down, :], right[:, cols]).astype(LOW)
            if step > width:
                for whose in range(2):
                    halves[m][(whose + core) % 2, slot, down] = value[
                        :, whose * width : (whose + 1) * width
                    ]
            else:
                per = width // step
                start = pl.multiple_of((c % per) * step, LANES)
                halves[m][(c // per + core) % 2, slot, down, pl.ds(start, step)] = value
            return carry

        lax.fori_loop(0, count * (tall // high), body, 0)
        give(m, slot).start()

    def hidden_back(first, last):
        def body(c, carry):
            cols = pl.ds(pl.multiple_of(c * wide_hidden, wide_hidden), wide_hidden)
            value = dot_nt(upstream[...], weights[DOWN][cols, :]) * slope[:, cols]
            up_bias[:, cols] = jnp.broadcast_to(
                jnp.sum(value, axis=0, keepdims=True), (8, wide_hidden)
            )
            pre_low[:, cols] = value.astype(LOW)
            return carry

        lax.fori_loop(first, last, body, 0)

    def second_back():
        def body(c, carry):
            cols = pl.ds(pl.multiple_of(c * 256, 256), 256)
            incoming[:, cols] = dot_nt(pre_low[...], weights[UP][cols, :])
            return carry

        lax.fori_loop(0, model // 256, body, 0)

    def norm_back(hat, inv, g, add):
        gain_sum = jnp.zeros((1, model), F32)
        bias_sum = jnp.zeros((1, model), F32)
        add_sum = jnp.zeros((1, model), F32)
        for s in slices:
            came_in = incoming[s, :]
            hat_vals = hat[s, :]
            scaled = came_in * gain(g)
            average = jnp.mean(scaled, axis=-1, keepdims=True)
            along = jnp.mean(scaled * hat_vals, axis=-1, keepdims=True)
            value = add[s, :].astype(F32) + inv[s, 0:1] * (scaled - average - hat_vals * along)
            gain_sum += jnp.sum(came_in * hat_vals, axis=0, keepdims=True)
            bias_sum += jnp.sum(came_in, axis=0, keepdims=True)
            add_sum += jnp.sum(value, axis=0, keepdims=True)
            middle_grad[s, :] = value
            middle_low[s, :] = value.astype(LOW)
        vec_grad[g : g + 1, :] = gain_sum
        vec_grad[g + 1 : g + 2, :] = bias_sum
        return add_sum

    def attended_back():
        def body(c, carry):
            cols = pl.ds(pl.multiple_of(c * 256, 256), 256)
            head_grad[:, cols] = dot_nt(middle_low[...], weights[OUT][cols, :]).astype(LOW)
            return carry

        lax.fori_loop(0, model // 256, body, 0)

    def attend_back(first, last):
        def body(p, carry):
            start = pl.multiple_of(p * pair_width, LANES)
            cols = pl.ds(start, pair_width)
            stacked(head_grad[:, cols], score_rows.at[1])
            stacked(heads(0, p), score_rows.at[0])
            weight = probs[p]
            value_grad = dot_tn(weight, score_rows[1])
            prob_grad = dot_nt(score_rows[1], heads(2, p))
            wide = weight.astype(F32)
            along = jnp.sum(wide * prob_grad, axis=-1, keepdims=True)
            score_grad = (wide * (prob_grad - along)).astype(LOW)
            query_grad = merged(dot_nn(score_grad, heads(1, p))) * HEAD_DIM**-0.5
            key_grad = dot_tn(score_grad, score_rows[0])
            vec_grad[2:3, cols] = jnp.sum(query_grad, axis=0, keepdims=True)
            vec_grad[3:4, cols] = jnp.sum(value_grad, axis=0, keepdims=True)
            for k, value in enumerate((query_grad, key_grad, value_grad)):
                joined[:, pl.ds(pl.multiple_of(k * model + start, LANES), pair_width)] = (
                    value.astype(LOW)
                )
            return carry

        lax.fori_loop(first, last, body, 0)

    def first_back():
        def body(c, carry):
            cols = pl.ds(pl.multiple_of(c * 256, 256), 256)
            incoming[:, cols] = dot_nt(joined[...], weights[QKV][cols, :])
            return carry

        lax.fori_loop(0, model // 256, body, 0)

    def tail_local():
        line_grad[...] = jnp.zeros_like(line_grad)
        for b in range(n):
            line_grad[b, 0:8, 0:rows] = vec_grad[0:8, b * rows : (b + 1) * rows]
            for e in range(4 * rows // LANES):
                first = b * 4 * rows + e * LANES
                line_grad[b, 8 + e : 9 + e, :] = up_bias[0:1, first : first + LANES]

    def tail_sum(d, t):
        b = at(reach[0] - t) if d == 0 else at(t - reach[1])
        arrive = (line_a, line_b)[d]
        return remote(line_grad.at[b], arrive.at[t], tail_s.at[d, t], tail_r.at[d, t], peers[d])

    def tail_step(t):
        for d in (0, 1):
            if t < reach[d]:
                b = at(reach[0] - t) if d == 0 else at(t - reach[1])
                if t > 0:
                    tail_sum(d, t - 1).wait_recv()
                    line_grad[b] = line_grad[b] + (line_a, line_b)[d][t - 1]
                tail_sum(d, t).start()

    def pair_copy(k, peer):
        return remote(
            line_pair.at[2 * k], line_pair.at[2 * k + 1], pair_s.at[k], pair_r.at[k], peer
        )

    def tail_end():
        total = line_grad[me]
        for d in (0, 1):
            if reach[d]:
                tail_sum(d, reach[d] - 1).wait_recv()
                total = total + (line_a, line_b)[d][reach[d] - 1]
        line_pair[0] = total
        pair_copy(0, across).start()

    def tail_pair():
        pair_copy(0, across).wait_recv()
        line_pair[2] = line_pair[0] + line_pair[1]
        pair_copy(1, partner).start()

    def tail_finish():
        pair_copy(1, partner).wait_recv()
        line_wide[...] = line_pair[2] + line_pair[3]
        high = line_wide[...].astype(LOW)
        line_low[:, :LANES] = high
        line_low[:, LANES:] = (line_wide[...] - high.astype(F32)).astype(LOW)

    layout = pack_layout(rows, padded, model)

    def pack_copies(name):
        source = {"c": output_low, "fn": input_grad_low, "tf": line_low}.get(name)
        if source is None:
            source = sums["QOUD".index(name[1])]
        copies = []
        for i, (key, first, high, left, width) in enumerate(layout):
            if key == name:
                target = packed.at[pl.ds(first, high), pl.ds(0, width)]
                view = source.at[:, pl.ds(left, width)]
                copies.append(pltpu.make_async_copy(view, target, pack_sem.at[i]))
        return copies

    x_copy = pltpu.make_async_copy(x_in, x_low, in_sem.at[1])
    cot_copy = pltpu.make_async_copy(cot_in, cot_low, in_sem.at[2])
    for m in range(4):
        for slot in (MINE, SHARED, YOURS):
            own_copy(m, slot).start()
    x_copy.start()
    cot_copy.start()

    lines[me] = jnp.zeros_like(lines[me])
    for i, ref in zip(VECTOR_ROWS, vectors_in):
        if i < 8:
            lines[me, i, 0:rows] = ref[...].astype(F32)
        else:
            for e in range(4 * rows // LANES):
                lines[me, i + e, :] = ref[pl.ds(e * LANES, LANES)].astype(F32)

    barrier = pltpu.get_barrier_semaphore()
    for peer in (*peers, partner, across):
        pl.semaphore_signal(barrier, inc=1, device_id=peer, device_id_type=MESH)
    pl.semaphore_wait(barrier, 4)

    for d in (0, 1):
        line_send(d, 0).start()
    for slot in (MINE, SHARED, YOURS):
        own_copy(QKV, slot).wait()
    gather_start(QKV)
    for m in (OUT, UP, DOWN):
        for slot in (MINE, SHARED, YOURS):
            own_copy(m, slot).wait()
    x_copy.wait()
    cot_copy.wait()
    begin()

    def part(total, p):
        return range(total * p // 4, total * (p + 1) // 4)

    def hops(m, p):
        for h in part(reach[0], p):
            gather_hop(m, h)

    def steps_of(m, slot, p):
        for t in part(reach[0], p):
            reduce_step(m, slot, t)

    def lines_of(p):
        for h in part(reach[0], p):
            line_hop(h)

    def tails_of(p):
        for t in part(reach[0], p):
            tail_step(t)

    def first_norm_back():
        norm_back(hat1, inv1, 0, middle_grad)
        input_grad_low[...] = middle_grad[...].astype(LOW)
        tail_local()

    def second_norm_back():
        vec_grad[4:5, :] = norm_back(hat2, inv2, 5, upstream)

    chunks = hidden_units // wide_hidden
    sides = {QKV: (normed_t, joined), OUT: (attended_t, middle_low)}
    sides |= {UP: (second_t, pre_low), DOWN: (hidden_t, upstream)}
    actions = {
        "v": lambda: (vectors(), first_norm()),
        "p": lambda: project(0, 6),
        "a0": lambda: attend(0, pairs // 2),
        "a1": lambda: attend(pairs // 2, pairs),
        "m": mix,
        "t": transposes,
        "u0": lambda: expand(0, chunks // 2),
        "u1": lambda: expand(chunks // 2, chunks),
        "c": contract,
        "hb": lambda: hidden_back(0, chunks),
        "sb": second_back,
        "nb": second_norm_back,
        "ob": attended_back,
        "ab0": lambda: attend_back(0, pairs // 2),
        "ab1": lambda: attend_back(pairs // 2, pairs),
        "fb": first_back,
        "fn": first_norm_back,
        "te": tail_end,
        "tp": tail_pair,
        "tf": tail_finish,
    }
    for p in range(4):
        actions[f"l{p}"] = functools.partial(lines_of, p)
        actions[f"t{p}"] = functools.partial(tails_of, p)
    for name, m in (("Q", QKV), ("O", OUT), ("U", UP), ("D", DOWN)):
        actions["G" + name] = functools.partial(gather_start, m)
        actions["R" + name] = functools.partial(gather_relay, m)
        actions["E" + name] = functools.partial(gather_end, m)
        actions["X" + name] = functools.partial(reduce_exchange, m)
        actions["F" + name] = functools.partial(reduce_finish, m)
        for p in range(4):
            actions[f"g{name}{p}"] = functools.partial(hops, m, p)
            actions[f"o{name}{p}"] = functools.partial(reduce_over, m, p)
        for key, slot in (("s", SHARED), ("m", MINE), ("y", YOURS)):
            actions[f"d{name}{key}"] = functools.partial(gradient, m, *sides[m], slot)
            actions[f"{name}{key}"] = functools.partial(reduce_end, m, slot)
            for p in range(4):
                actions[f"{name}{key}{p}"] = functools.partial(steps_of, m, slot, p)
    for name in ORDER:
        actions[name]()
        for copy in pack_copies(name) if name in {entry[0] for entry in layout} else ():
            copy.start()

    for m in range(4):
        for slot in (SHARED, MINE, YOURS):
            gather_core(m, slot, core).wait_send()
            give(m, slot).wait_send()
            end_core(m, slot, core).wait_send()
        for slot in slots_of(m):
            if slot == MINE and m in over:
                end_other(m, MINE).wait_send()
            else:
                end_row(m, slot).wait_send()
        if m in over:
            for d, t in over_steps():
                hand_over(m, d, t).wait_send()
        for d in (0, 1):
            for h in range(reach[d]):
                gather_row(m, d, h, MINE).wait_send()
                for slot in (SHARED, MINE):
                    gather_send(m, slot, d, h).wait_send()
                for slot in slots_of(m):
                    ring_sum(m, slot, d, h).wait_send()
    for d in (0, 1):
        for h in range(reach[d]):
            line_send(d, h).wait_send()
            tail_sum(d, h).wait_send()
    pair_copy(0, across).wait_send()
    pair_copy(1, partner).wait_send()
    for name in ("c", "fn", "tf", "FQ", "FO", "FU", "FD"):
        for copy in pack_copies(name):
            copy.wait()


def run_layer(layer_input, cotangent, live, matrices, vectors, n):
    line = (16, LANES)
    images, length, model = layer_input.shape
    padded = -(-length // 16) * 16
    hidden_units = matrices[UP].shape[1]
    vmem, dma = pltpu.VMEM, pltpu.SemaphoreType.DMA
    reach = (n // 2, n // 2 - 1)
    height = [a.shape[0] for a in matrices]
    sixth = [a.shape[1] // 6 for a in matrices]
    pairs = model // (2 * HEAD_DIM)
    wide = (padded, model)
    scratch = [vmem((n * a.shape[0], a.shape[1]), LOW) for a in matrices]
    scratch += [
        vmem((1, length, model), LOW),
        vmem((1, length, model), LOW),
        vmem(wide, LOW),
        vmem(wide, F32),
        vmem((padded, LANES), F32),
        vmem(wide, LOW),
        vmem((model, padded), LOW),
        vmem((padded, 3 * model), LOW),
        vmem((pairs, 2 * padded, padded), LOW),
        vmem(wide, LOW),
        vmem((model, padded), LOW),
        vmem(wide, F32),
        vmem(wide, F32),
        vmem((padded, LANES), F32),
        vmem(wide, LOW),
        vmem((model, padded), LOW),
        vmem((padded, hidden_units), LOW),
        vmem((hidden_units, padded), LOW),
        vmem((padded, hidden_units), LOW),
        vmem((padded, hidden_units), F32),
        vmem(wide, F32),
        vmem(wide, LOW),
        vmem((16, model), F32),
    ]
    scratch += [vmem((2, 3, n * r, w), LOW) for r, w in zip(height, sixth)]
    scratch += [vmem((3, n * r, w), LOW) for r, w in zip(height, sixth)]
    slots = (3, 3, 2, 2)
    scratch += [vmem((n * height[m], sixth[m]), LOW) for m in (UP, DOWN)]
    scratch += [vmem((k, reach[0], r, w), LOW) for k, r, w in zip(slots, height, sixth)]
    scratch += [vmem((k, max(reach[1], 1), r, w), LOW) for k, r, w in zip(slots, height, sixth)]
    scratch += [vmem((k - 1 + k // 3, r, w), LOW) for k, r, w in zip(slots, height, sixth)]
    scratch += [
        vmem((n,) + line, F32),
        vmem((16, model), F32),
        vmem((8, hidden_units), F32),
        vmem((n,) + line, F32),
        vmem((reach[0],) + line, F32),
        vmem((max(reach[1], 1),) + line, F32),
    ]
    scratch += [
        dma((3,)),
        dma((4, 3)),
        dma((4, 2, 2, reach[0])),
        dma((4, 2, 2, reach[0])),
        dma((4, n - 1)),
        dma((4, n - 1)),
        dma((4, 3)),
        dma((4, 3)),
        dma((2, reach[0])),
        dma((2, reach[0])),
        dma((4, 3)),
        dma((4, 3)),
        dma((4, 2, reach[0] + 1)),
        dma((4, 2, reach[0] + 1)),
        dma((4, 3, 2, reach[0])),
        dma((4, 3, 2, reach[0])),
        dma((4, 3, 2)),
        dma((4, 3, 2)),
        dma((2, reach[0])),
        dma((2, reach[0])),
        dma((2,)),
        dma((2,)),
        vmem((4,) + line, F32),
        vmem((8, 3 * model), F32),
        vmem((2, 2 * padded, 2 * HEAD_DIM), LOW),
    ]
    layout = pack_layout(matrices[QKV].shape[0], padded, model)
    scratch += [vmem(wide, LOW)] * 2 + [vmem(a.shape, LOW) for a in matrices]
    scratch += [vmem((16, 2 * LANES), LOW), vmem(line, F32), dma((len(layout),))]
    anywhere = pl.BlockSpec(memory_space=pl.ANY)
    near = pl.BlockSpec(memory_space=pltpu.VMEM)
    return pl.pallas_call(
        functools.partial(layer_kernel, n, length, padded, model),
        out_shape=jax.ShapeDtypeStruct((layout[-1][1] + layout[-1][2], model), LOW),
        in_specs=[anywhere] * 2 + [pl.BlockSpec(memory_space=pltpu.SMEM)] + [anywhere] * 4 + [near] * 9,
        out_specs=anywhere,
        scratch_shapes=scratch,
        compiler_params=pltpu.CompilerParams(
            collective_id=0, has_side_effects=True, vmem_limit_bytes=60 * 1024 * 1024
        ),
        name="layer",
    )(layer_input, cotangent, live, *matrices, *vectors)


norm_eps = 1e-06
root_half = 0.7071067811865476
density_coef = 0.3989422804014327


def matmul(operand, factor):
    flat = operand.reshape(-1, operand.shape[-1])
    product = jnp.dot(flat, factor, preferred_element_type=jnp.float32)
    return product.reshape(operand.shape[:-1] + (factor.shape[-1],))


def outer_product(operand, factor):
    return jnp.dot(
        operand.reshape(-1, operand.shape[-1]).T,
        factor.reshape(-1, factor.shape[-1]),
        preferred_element_type=jnp.float32,
    )


def batched(form, operand, factor):
    return jnp.einsum(form, operand, factor, preferred_element_type=jnp.float32)


def layer_norm(values, norm_gain, norm_bias):
    average = jnp.mean(values, axis=-1, keepdims=True)
    centred = values - average
    spread = jnp.mean(centred * centred, axis=-1, keepdims=True)
    inv_std = lax.rsqrt(spread + norm_eps)
    hat_vals = centred * inv_std
    return (
        hat_vals * norm_gain.astype(jnp.float32) + norm_bias.astype(jnp.float32),
        hat_vals,
        inv_std,
    )


def norm_back(incoming, hat_vals, inv_std, norm_gain):
    scaled = incoming * norm_gain.astype(jnp.float32)
    return inv_std * (
        scaled
        - jnp.mean(scaled, axis=-1, keepdims=True)
        - hat_vals * jnp.mean(scaled * hat_vals, axis=-1, keepdims=True)
    )


def forward_pass(params, layer_input, live):
    (
        first_gain,
        first_bias,
        qkv_weight,
        query_bias,
        value_bias,
        out_weight,
        out_bias,
        second_gain,
        second_bias,
        up_weight,
        up_bias,
        down_weight,
        down_bias,
    ) = params
    images, length, model_width = layer_input.shape
    head_count = model_width // HEAD_DIM
    score_scale = HEAD_DIM ** (-0.5)
    stream = layer_input.astype(jnp.float32)
    normed, first_hat, first_inv = layer_norm(stream, first_gain, first_bias)
    normed = normed.astype(jnp.bfloat16)
    projected = matmul(normed, qkv_weight)
    shape_heads = (images, length, head_count, HEAD_DIM)
    queries = (
        (projected[..., :model_width] + query_bias.astype(jnp.float32))
        .astype(jnp.bfloat16)
        .reshape(shape_heads)
    )
    key_rows = (
        projected[..., model_width : 2 * model_width].astype(jnp.bfloat16).reshape(shape_heads)
    )
    values = (
        (projected[..., 2 * model_width :] + value_bias.astype(jnp.float32))
        .astype(jnp.bfloat16)
        .reshape(shape_heads)
    )
    scores = batched("bqhd,bkhd->bhqk", queries, key_rows) * score_scale
    log_total = jnp.log(jnp.sum(jnp.exp(scores), axis=-1, keepdims=True))
    weights = jnp.exp(scores - log_total).astype(jnp.bfloat16)
    attended = (
        batched("bhqk,bkhd->bqhd", weights, values)
        .reshape(images, length, model_width)
        .astype(jnp.bfloat16)
    )
    middle = stream + matmul(attended, out_weight) + out_bias.astype(jnp.float32)
    second_normed, second_hat, second_inv = layer_norm(middle, second_gain, second_bias)
    second_normed = second_normed.astype(jnp.bfloat16)
    hidden_pre = matmul(second_normed, up_weight) + up_bias.astype(jnp.float32)
    normal_cdf = 0.5 * (1.0 + lax.erf(hidden_pre * root_half))
    hidden = (hidden_pre * normal_cdf).astype(jnp.bfloat16)
    result = middle + matmul(hidden, down_weight) + down_bias.astype(jnp.float32)
    image_mask = live.astype(jnp.float32)[:, None, None]
    output = (result * image_mask).astype(jnp.bfloat16)
    saved = (
        normed,
        first_hat,
        first_inv,
        queries,
        key_rows,
        values,
        log_total,
        attended,
        second_normed,
        second_hat,
        second_inv,
        hidden_pre,
        normal_cdf,
        hidden,
        image_mask,
    )
    return (output, saved)


def backward_pass(params, saved, cotangent):
    (
        first_gain,
        first_bias,
        qkv_weight,
        query_bias,
        value_bias,
        out_weight,
        out_bias,
        second_gain,
        second_bias,
        up_weight,
        up_bias,
        down_weight,
        down_bias,
    ) = params
    (
        normed,
        first_hat,
        first_inv,
        queries,
        key_rows,
        values,
        log_total,
        attended,
        second_normed,
        second_hat,
        second_inv,
        hidden_pre,
        normal_cdf,
        hidden,
        image_mask,
    ) = saved
    images, length, head_count, head_width = queries.shape
    flat_shape = (images, length, head_count * head_width)
    score_scale = HEAD_DIM ** (-0.5)
    upstream = cotangent.astype(jnp.float32) * image_mask
    upstream_low = upstream.astype(jnp.bfloat16)
    down_weight_grad = outer_product(hidden, upstream_low)
    down_bias_grad = jnp.sum(upstream, axis=(0, 1))
    hidden_grad = matmul(upstream_low, down_weight.T)
    density = jnp.exp(-0.5 * hidden_pre * hidden_pre) * density_coef
    pre_grad = hidden_grad * (normal_cdf + hidden_pre * density)
    pre_low = pre_grad.astype(jnp.bfloat16)
    up_weight_grad = outer_product(second_normed, pre_low)
    up_bias_grad = jnp.sum(pre_grad, axis=(0, 1))
    second_in = matmul(pre_low, up_weight.T)
    second_gain_grad = jnp.sum(second_in * second_hat, axis=(0, 1))
    second_bias_grad = jnp.sum(second_in, axis=(0, 1))
    middle_grad = upstream + norm_back(second_in, second_hat, second_inv, second_gain)
    middle_low = middle_grad.astype(jnp.bfloat16)
    out_weight_grad = outer_product(attended, middle_low)
    out_bias_grad = jnp.sum(middle_grad, axis=(0, 1))
    attended_grad = matmul(middle_low, out_weight.T).astype(jnp.bfloat16).reshape(queries.shape)
    again_scores = batched("bqhd,bkhd->bhqk", queries, key_rows) * score_scale
    probs = jnp.exp(again_scores - log_total)
    probs_low = probs.astype(jnp.bfloat16)
    value_grad = batched("bhqk,bqhd->bkhd", probs_low, attended_grad)
    prob_grad = batched("bqhd,bkhd->bhqk", attended_grad, values)
    score_grad = (
        probs * (prob_grad - jnp.sum(probs * prob_grad, axis=-1, keepdims=True)) * score_scale
    ).astype(jnp.bfloat16)
    query_grad = batched("bhqk,bkhd->bqhd", score_grad, key_rows).reshape(flat_shape)
    key_grad = batched("bhqk,bqhd->bkhd", score_grad, queries).reshape(flat_shape)
    value_grad = value_grad.reshape(flat_shape)
    joined = jnp.concatenate([query_grad, key_grad, value_grad], axis=-1).astype(jnp.bfloat16)
    qkv_weight_grad = outer_product(normed, joined)
    query_bias_grad = jnp.sum(query_grad, axis=(0, 1))
    value_bias_grad = jnp.sum(value_grad, axis=(0, 1))
    first_in = matmul(joined, qkv_weight.T)
    first_gain_grad = jnp.sum(first_in * first_hat, axis=(0, 1))
    first_bias_grad = jnp.sum(first_in, axis=(0, 1))
    middle_grad = middle_grad + norm_back(first_in, first_hat, first_inv, first_gain)
    input_grad = middle_grad.astype(jnp.bfloat16)
    grads = (
        first_gain_grad,
        first_bias_grad,
        qkv_weight_grad,
        query_bias_grad,
        value_bias_grad,
        out_weight_grad,
        out_bias_grad,
        second_gain_grad,
        second_bias_grad,
        up_weight_grad,
        up_bias_grad,
        down_weight_grad,
        down_bias_grad,
    )
    return (input_grad, grads)


def places(n):
    rep = lax.axis_index("rep")
    me = lax.axis_index("shard")
    core = rep % 2
    row = rep // 2
    position = ring_position(me, n)
    right = (rep, ring_index((position + 1) % n, n))
    left = (rep, ring_index((position + n - 1) % n, n))
    partner = (row * 2 + 1 - core, me)
    across = ((1 - row) * 2 + core, me)
    return me, core, row, position, right, left, partner, across


def greet(peers):
    barrier = pltpu.get_barrier_semaphore()
    for peer in peers:
        pl.semaphore_signal(barrier, inc=1, device_id=peer, device_id_type=MESH)
    pl.semaphore_wait(barrier, len(peers))


def remote(source, target, send, recv, device):
    return pltpu.make_async_remote_copy(
        src_ref=source,
        dst_ref=target,
        send_sem=send,
        recv_sem=recv,
        device_id=device,
        device_id_type=MESH,
    )


def window(refs, side, part, block, width):
    qkv, out, up, down = refs
    if side == 2:
        return [(None, down.at[block, part])]
    if side == 1:
        return [(None, up.at[block, :, pl.ds(pl.multiple_of(part * width, width), width)])]
    inner = part - part // 3
    return [
        (part < 3, qkv.at[block, :, pl.ds(pl.multiple_of(inner * width, width), width)]),
        (part == 3, out.at[block]),
    ]


def start_each(views, make):
    for condition, view in views:
        if condition is None:
            make(view).start()
        else:
            pl.when(condition)(make(view).start)


def gather_kernel(
    n,
    width,
    qkv_in,
    out_in,
    up_in,
    down_in,
    line_in,
    qkv_ref,
    out_ref,
    up_ref,
    down_ref,
    line_ref,
    local_sem,
    ring_s,
    ring_r,
    core_s,
    core_r,
    row_s,
    row_r,
    last_s,
    last_r,
    line_s,
    line_r,
):
    me, core, row, position, right, left, partner, across = places(n)
    refs = (qkv_ref, out_ref, up_ref, down_ref)
    pairs = zip((qkv_in, out_in, up_in, down_in, line_in), refs + (line_ref,))
    locals_ = [
        pltpu.make_async_copy(source, target.at[me], local_sem.at[i])
        for i, (source, target) in enumerate(pairs)
    ]
    for copy in locals_:
        copy.start()
    greet((right, left, partner, across))
    for copy in locals_:
        copy.wait()

    def block(way, r):
        return ring_index((position + (1 if way else n - 1) * r) % n, n)

    def views(i, r, whose):
        way, kind = i // 2, i % 2
        side, part = (2, 2 * whose + way) if kind else (way, 2 * whose + row)
        return window(refs, side, part, block(way, r), width)

    def over(way, r, whose):
        return window(refs, way, 2 * whose + 1 - row, block(way, r), width)

    def ring(i, r):
        peer = left if i // 2 else right
        return lambda v: remote(v, v, ring_s.at[i, r], ring_r.at[i, r], peer)

    def to_core(i, r):
        return lambda v: remote(v, v, core_s.at[i, r], core_r.at[i, r], partner)

    def to_row(way, r):
        return lambda v: remote(v, v, row_s.at[way, r], row_r.at[way, r], across)

    def to_last(way, r):
        return lambda v: remote(v, v, last_s.at[way, r], last_r.at[way, r], partner)

    def line(r):
        view = line_ref.at[block(0, r)]
        return remote(view, view, line_s.at[r], line_r.at[r], right)

    def one(vs):
        return vs[0][1]

    for i in range(4):
        start_each(views(i, 0, core), ring(i, 0))
    line(0).start()

    def relay(r):
        for way in range(2):
            to_row(way, r)(one(over(way, r + 1, core))).wait_recv()
            start_each(over(way, r + 1, core), to_last(way, r))

    def step(r, carry):
        for i in (0, 2, 1, 3):
            got = views(i, r + 1, core)
            ring(i, r)(one(got)).wait_recv()

            @pl.when(r < n - 2)
            def _():
                start_each(got, ring(i, r + 1))

            if i % 2 == 0:
                start_each(got, to_row(i // 2, r))
            start_each(got, to_core(i, r))
        line(r).wait_recv()

        @pl.when(r < n - 2)
        def _():
            line(r + 1).start()

        @pl.when(r > 0)
        def _():
            relay(r - 1)

        return carry

    lax.fori_loop(0, n - 1, step, 0)
    relay(n - 2)

    def finish(r, carry):
        for i in range(4):
            view = one(views(i, r, core))
            ring(i, r)(view).wait_send()
            to_core(i, r)(view).wait_send()
            to_core(i, r)(view).wait_recv()
        for way in range(2):
            view = one(views(2 * way, r, core))
            to_row(way, r)(view).wait_send()
            to_last(way, r)(view).wait_send()
            to_last(way, r)(view).wait_recv()
        line(r).wait_send()
        return carry

    lax.fori_loop(0, n - 1, finish, 0)


def gather_all(arrays, n, width):
    dma = pltpu.SemaphoreType.DMA
    return pl.pallas_call(
        functools.partial(gather_kernel, n, width),
        out_shape=[jax.ShapeDtypeStruct((n,) + a.shape, a.dtype) for a in arrays],
        in_specs=[pl.BlockSpec(memory_space=pltpu.VMEM)] * len(arrays),
        out_specs=[pl.BlockSpec(memory_space=pl.ANY)] * len(arrays),
        scratch_shapes=[dma((len(arrays),))]
        + [dma((4, n - 1))] * 4
        + [dma((2, n - 1))] * 4
        + [dma((n - 1,))] * 2,
        compiler_params=pltpu.CompilerParams(collective_id=0, has_side_effects=True),
        name="gather_all",
    )(*arrays)


def reduce_kernel(
    n,
    width,
    qkv_ref,
    out_ref,
    up_ref,
    down_ref,
    line_ref,
    sums,
    line_out,
    own,
    given,
    arrive,
    over,
    other,
    line_send,
    line_got,
    line_pair,
    own_sem,
    given_s,
    given_r,
    ring_s,
    ring_r,
    row_s,
    row_r,
    end_row_s,
    end_row_r,
    end_core_s,
    end_core_r,
    line_s,
    line_r,
    pair_s,
    pair_r,
):
    me, core, row, position, right, left, partner, across = places(n)
    refs = (qkv_ref, out_ref, up_ref, down_ref)
    f32 = jnp.float32

    def block(way, k):
        return ring_index((position + (1 if way else n - 1) * (k + 1)) % n, n)

    def source(i, k, whose):
        way, kind = i % 2, i // 2
        side, part = (
            (way, 2 * whose + row),
            (2, 2 * whose + way),
            (way, 2 * whose + 1 - row),
        )[kind]
        return window(refs, side, part, block(way, k), width)

    def load(i, k):
        return lambda v: pltpu.make_async_copy(v, own.at[i, k], own_sem.at[i, k])

    def give(i, k):
        return lambda v: remote(v, given.at[i, k], given_s.at[i, k], given_r.at[i, k], partner)

    def ring(i, k):
        peer = left if i % 2 else right
        return remote(own.at[i, k], arrive.at[i, k], ring_s.at[i, k], ring_r.at[i, k], peer)

    def to_row(way, k):
        return remote(
            own.at[4 + way, k], over.at[way, k], row_s.at[way, k], row_r.at[way, k], across
        )

    def line_ring(k):
        return remote(line_send.at[k], line_got.at[k], line_s.at[k], line_r.at[k], right)

    order = (4, 5, 2, 3, 0, 1)

    def loads(k, carry):
        for i in order:
            start_each(source(i, k, core), load(i, k))
        return carry

    lax.fori_loop(0, n, loads, 0)
    greet((right, left, partner, across))

    def gives(k, carry):
        for i in order:
            start_each(source(i, k, 1 - core), give(i, k))
        return carry

    lax.fori_loop(0, n, gives, 0)

    def take(i, k):
        view = source(i, k, core)[0][1]
        load(i, k)(view).wait()
        give(i, k)(view).wait_recv()
        return own[i, k].astype(f32) + given[i, k].astype(f32)

    def put(i, k, total):
        own[i, k] = total.astype(own.dtype)

    def ahead(k):
        for way in range(2):
            put(4 + way, k, take(4 + way, k))
            to_row(way, k).start()

    def partial(i, k, first):
        total = take(i, k)
        if i < 2:
            to_row(i, k).wait_recv()
            total = total + over[i, k].astype(f32)
        if not first:
            ring(i, k - 1).wait_recv()
            total = total + arrive[i, k - 1].astype(f32)
        return total

    ahead(0)
    line_send[0] = line_ref[block(0, 0)]
    line_ring(0).start()
    ahead(1)
    for i in (2, 3, 0, 1):
        put(i, 0, partial(i, 0, True))
        ring(i, 0).start()

    def step(k, carry):
        ahead(k + 1)
        for i in (2, 3, 0, 1):
            put(i, k, partial(i, k, False))
            ring(i, k).start()
        line_ring(k - 1).wait_recv()
        line_send[k] = line_ref[block(0, k)] + line_got[k - 1]
        line_ring(k).start()
        return carry

    lax.fori_loop(1, n - 1, step, 0)

    def end_row(i, k=None):
        if i < 2:
            view = sums.at[i, 2 * core + row]
            return remote(view, view, end_row_s.at[i], end_row_r.at[i], across)
        return remote(
            own.at[i, n - 1], other.at[i - 2], end_row_s.at[i], end_row_r.at[i], across
        )

    def end_core(j, side, part):
        view = sums.at[side, part]
        return remote(view, view, end_core_s.at[j], end_core_r.at[j], partner)

    for i in (2, 3):
        put(i, n - 1, partial(i, n - 1, False))
        end_row(i).start()
    line_ring(n - 2).wait_recv()
    line_pair[0] = line_ref[me] + line_got[n - 2]
    pair_row = remote(line_pair.at[0], line_pair.at[1], pair_s.at[0], pair_r.at[0], across)
    pair_row.start()
    for way in (0, 1):
        sums[way, 2 * core + row] = partial(way, n - 1, False).astype(sums.dtype)
        end_row(way).start()
        end_core(way, way, 2 * core + row).start()
    pair_row.wait()
    line_pair[2] = line_pair[0] + line_pair[1]
    pair_core = remote(line_pair.at[2], line_pair.at[3], pair_s.at[1], pair_r.at[1], partner)
    pair_core.start()
    for way in (0, 1):
        end_row(2 + way).wait_recv()
        total = own[2 + way, n - 1].astype(f32) + other[way].astype(f32)
        sums[2, 2 * core + way] = total.astype(sums.dtype)
        end_core(2 + way, 2, 2 * core + way).start()
    for way in (0, 1):
        end_row(way).wait_recv()
        end_core(4 + way, way, 2 * core + 1 - row).start()
    pair_core.wait()
    line_out[...] = line_pair[2] + line_pair[3]
    for i in range(4):
        end_row(i).wait_send()
    for j in range(6):
        copy = end_core(j, 0, 0)
        copy.wait_send()
        copy.wait_recv()

    def finish(k, carry):
        for i in range(6):
            give(i, k)(source(i, k, core)[0][1]).wait_send()
        for way in range(2):
            to_row(way, k).wait_send()
        return carry

    lax.fori_loop(0, n, finish, 0)

    def finish_ring(k, carry):
        for i in range(4):
            ring(i, k).wait_send()
        line_ring(k).wait_send()
        return carry

    lax.fori_loop(0, n - 1, finish_ring, 0)


def reduce_all(arrays, n, width):
    dma = pltpu.SemaphoreType.DMA
    vmem = pltpu.VMEM
    rows = arrays[0].shape[1]
    low = arrays[0].dtype
    line = arrays[-1].shape[1:]
    anywhere = pl.BlockSpec(memory_space=pl.ANY)
    near = pl.BlockSpec(memory_space=pltpu.VMEM)
    return pl.pallas_call(
        functools.partial(reduce_kernel, n, width),
        out_shape=[
            jax.ShapeDtypeStruct((3, 4, rows, width), low),
            jax.ShapeDtypeStruct(line, jnp.float32),
        ],
        in_specs=[anywhere] * 4 + [near],
        out_specs=[near, near],
        scratch_shapes=[
            vmem((6, n, rows, width), low),
            vmem((6, n, rows, width), low),
            vmem((4, n - 1, rows, width), low),
            vmem((2, n, rows, width), low),
            vmem((2, rows, width), low),
            vmem((n - 1,) + line, jnp.float32),
            vmem((n - 1,) + line, jnp.float32),
            vmem((4,) + line, jnp.float32),
            dma((6, n)),
            dma((6, n)),
            dma((6, n)),
            dma((4, n - 1)),
            dma((4, n - 1)),
            dma((2, n)),
            dma((2, n)),
            dma((4,)),
            dma((4,)),
            dma((6,)),
            dma((6,)),
            dma((n - 1,)),
            dma((n - 1,)),
            dma((2,)),
            dma((2,)),
        ],
        compiler_params=pltpu.CompilerParams(
            collective_id=1, has_side_effects=True, vmem_limit_bytes=56 * 1024 * 1024
        ),
        name="reduce_all",
    )(*arrays)


def per_device_in_parts(n, layer_input, cotangent, live, *params):
    width = params[0].shape[0] * n
    rows = params[0].shape[0]
    matrices = [i for i, p in enumerate(params) if p.ndim == 2]
    vectors = [i for i, p in enumerate(params) if p.ndim == 1]
    shapes = [params[i].shape for i in matrices]
    assert shapes == [(rows, 3 * width), (rows, width), (rows, 4 * width), (4 * rows, width)]
    lengths = [params[i].shape[0] for i in vectors]
    tall = -(-sum(lengths) // (16 * LANES)) * 16
    spare = tall * LANES - sum(lengths)

    line = jnp.concatenate([params[i] for i in vectors] + [jnp.zeros(spare, params[0].dtype)])
    sent = [params[i] for i in matrices]
    sent[3] = sent[3].reshape(4, rows, width)
    *full, lines = gather_all(sent + [line.reshape(tall, LANES)], n, width)
    gathered = [None] * len(params)
    for i, array in zip(matrices, full):
        gathered[i] = array.reshape(n * params[i].shape[0], params[i].shape[1])
    tail = lines.reshape(n, -1)
    at = 0
    for i, length in zip(vectors, lengths):
        gathered[i] = tail[:, at : at + length].reshape(-1)
        at += length

    output, saved = forward_pass(gathered, layer_input, live)
    input_grad, grads = backward_pass(gathered, saved, cotangent)

    low = jnp.bfloat16
    blocks = [grads[i].astype(low).reshape((n,) + a.shape) for i, a in zip(matrices, sent)]
    parts = [grads[i].reshape(n, -1) for i in vectors] + [jnp.zeros((n, spare), jnp.float32)]
    blocks.append(jnp.concatenate(parts, axis=1).reshape(n, tall, LANES))
    sums, tail = reduce_all(blocks, n, width)

    def joined(pieces):
        return jnp.swapaxes(pieces, 0, 1).reshape(rows, -1).astype(jnp.float32)

    results = [None] * len(params)
    whole = (
        joined(sums[0, :3]),
        sums[0, 3].astype(jnp.float32),
        joined(sums[1]),
        sums[2].reshape(4 * rows, width).astype(jnp.float32),
    )
    for i, array in zip(matrices, whole):
        results[i] = array
    tail = tail.reshape(-1)
    at = 0
    for i, length in zip(vectors, lengths):
        results[i] = tail[at : at + length]
        at += length
    return (output, input_grad, *results)


VECTOR_ROWS = (0, 1, 2, 3, 4, 5, 6, 8, 7)


def finish_kernel(rows, layout, packed, *refs):
    streams_out, wide_out, vectors_out, wide, streams, (low, in_sem, out_sem) = split(
        refs, (2, 4, 9, 4, 2, 3)
    )
    place = {}
    for i, (name, first, high, left, width) in enumerate(layout):
        view = pl.ds(first, high), pl.ds(0, width)
        copy = pltpu.make_async_copy(packed.at[view], low.at[view], in_sem.at[i])
        copy.start()
        place.setdefault(name, []).append((copy, first, high, left, width))
    store = [
        pltpu.make_async_copy(source, target, out_sem.at[i])
        for i, (source, target) in enumerate(zip((*wide, *streams), (*wide_out, *streams_out)))
    ]
    for m in (DOWN, UP, QKV, OUT):
        for copy, first, high, left, width in place[("FQ", "FO", "FU", "FD")[m]]:
            copy.wait()
            wide[m][:, left : left + width] = low[first : first + high, :].astype(F32)
        store[m].start()
    for i, name in enumerate(("c", "fn")):
        copy, first, high, _, _ = place[name][0]
        copy.wait()
        streams[i][0] = low[first : first + high, :][: streams[i].shape[1]]
        store[4 + i].start()
    copy, first, high, _, _ = place["tf"][0]
    copy.wait()
    line = low[first : first + high, :LANES].astype(F32)
    line = line + low[first : first + high, LANES : 2 * LANES].astype(F32)
    for i, ref in zip(VECTOR_ROWS, vectors_out):
        if i < 8:
            ref[...] = line[i, 0:rows]
        else:
            for e in range(4 * rows // LANES):
                ref[pl.ds(e * LANES, LANES)] = line[i + e, :]
    for copy in store:
        copy.wait()


def finish(packed, stream, matrices, vectors):
    rows, model = matrices[QKV].shape[0], stream.shape[2]
    layout = pack_layout(rows, -(-stream.shape[1] // 16) * 16, model)
    far = pl.BlockSpec(memory_space=pltpu.HBM)
    near = pl.BlockSpec(memory_space=pltpu.VMEM)
    shape = jax.ShapeDtypeStruct
    return pl.pallas_call(
        functools.partial(finish_kernel, rows, layout),
        out_shape=[shape(stream.shape, LOW)] * 2
        + [shape(a.shape, F32) for a in matrices]
        + [shape(a.shape, F32) for a in vectors],
        in_specs=[far],
        out_specs=[far] * 6 + [near] * 9,
        scratch_shapes=[pltpu.VMEM(a.shape, F32) for a in matrices]
        + [pltpu.VMEM(stream.shape, LOW)] * 2
        + [pltpu.VMEM(packed.shape, LOW)]
        + [pltpu.SemaphoreType.DMA((k,)) for k in (len(layout), 6)],
        compiler_params=pltpu.CompilerParams(vmem_limit_bytes=32 * 1024 * 1024),
        name="finish",
    )(packed)


def per_device(n, layer_input, cotangent, live, *params):
    rows = params[0].shape[0]
    if rows % 32 or rows > LANES or layer_input.shape[0] != 1:
        return per_device_in_parts(n, layer_input, cotangent, live, *params)
    matrices = [p for p in params if p.ndim == 2]
    vectors = [p for p in params if p.ndim == 1]
    packed = run_layer(layer_input, cotangent, live, matrices, vectors, n)
    done = finish(packed, layer_input, matrices, vectors)
    wide, tall = list(done[2:6]), list(done[6:])
    return (*done[:2], *((wide if p.ndim == 2 else tall).pop(0) for p in params))


def solution(mesh):
    whole = P(("rep", "shard"), None, None)
    vector, matrix = P("shard"), P("shard", None)
    ranks = (1, 1, 2, 1, 1, 2, 1, 1, 1, 2, 1, 2, 1)
    params = tuple(matrix if rank == 2 else vector for rank in ranks)
    return jax.shard_map(
        functools.partial(per_device, mesh.shape["shard"]),
        mesh=mesh,
        in_specs=(whole, whole, P(("rep", "shard"))) + params,
        out_specs=(whole, whole) + params,
        check_vma=False,
    )
```

```python
import functools

import jax
import jax.numpy as jnp
from jax import lax
from jax.experimental import pallas as pl
from jax.experimental.pallas import tpu as pltpu
from jax.sharding import PartitionSpec as P

HEAD_DIM = 64
LANES = 128
NORM_EPS = 1e-06
ROOT_HALF = 0.7071067811865476
DENSITY_COEF = 0.3989422804014327
MESH = pl.DeviceIdType.MESH
F32 = jnp.float32
LOW = jnp.bfloat16

QKV, OUT, UP, DOWN = range(4)
CROSS = (UP, DOWN)
SHARED, MINE, YOURS = range(3)


def ring_index(position, n):
    half = position // (n // 2)
    return (1 - half) * 2 * position + half * (2 * (n - 1 - position) + 1)


def ring_position(index, n):
    odd = index % 2
    step = index // 2
    return (1 - odd) * step + odd * (n - 1 - step)


def remote(source, target, send, recv, device):
    return pltpu.make_async_remote_copy(
        src_ref=source,
        dst_ref=target,
        send_sem=send,
        recv_sem=recv,
        device_id=device,
        device_id_type=MESH,
    )


def dot_nn(a, b):
    return jnp.dot(a, b, preferred_element_type=F32)


def dot_nt(a, b):
    return lax.dot_general(a, b, (((1,), (1,)), ((), ())), preferred_element_type=F32)


def dot_tn(a, b):
    return lax.dot_general(a, b, (((0,), (0,)), ((), ())), preferred_element_type=F32)


def split(refs, counts):
    at = 0
    for count in counts:
        yield refs[at : at + count]
        at += count

ORDER = (
    "GO", "gQ0", "gO0", "l0", "gQ1", "gO1", "l1", "gQ2", "gO2", "GU", "l2", "gQ3", "gO3", "l3",
    "RQ", "RO", "v", "gU0", "eQ", "eO", "gU1", "EQ", "p", "gU2", "GD", "a0", "gU3", "RU", "a1",
    "gD0", "EO", "m", "eU", "t", "gD1", "EU", "u0", "u1", "gD2", "dDy", "dDs", "dDm", "oD0", "Ds0",
    "gD3", "RD", "oD1", "Dm0", "eD", "Ds1", "oD2", "Dm1", "oD3", "ED", "hb0", "Ds2", "hb1", "dUs",
    "dUy", "dUm", "Dm2", "Us0", "oU0", "oU1", "oU2", "oU3", "sb", "Ds3", "nb", "Dm3", "Us1", "dOs",
    "dOm", "dOy", "Um0", "ob", "Os0", "Om0", "Oy0", "ab0", "Us2", "Um1", "Os1", "Om1", "Oy1", "ab1",
    "dQs", "dQm", "dQy", "Us3", "Um2", "Os2", "Om2", "Oy2", "Qs0", "Qm0", "Qy0", "Um3", "Os3",
    "Om3", "Oy3", "Ds", "Dm", "Qs1", "Qm1", "Qy1", "fb", "fn", "t0", "Us", "XD", "Qs2", "Qm2",
    "Qy2", "t1", "Um", "Os", "Om", "Oy", "c", "Qs3", "Qm3", "Qy3", "t2", "XU", "XO", "t3", "Qs",
    "Qm", "Qy", "te", "XQ", "tp", "tf", "FQ", "FO", "FU", "FD",
)


def pack_layout(rows, padded, model):
    layout, first = [], 0
    for name, high, parts, width in (
        ("FD", 4 * rows, 1, model),
        ("FU", rows, 4, model),
        ("FQ", rows, 3, model),
        ("FO", rows, 1, model),
        ("c", padded, 1, model),
        ("fn", padded, 1, model),
        ("tf", 16, 1, 2 * LANES),
    ):
        for k in range(parts):
            layout.append((name, first, high, k * width, width))
            first += high
    return layout


def layer_kernel(n, length, padded, model, *refs):
    ins, outs, weights, acts, halves, given, over, arrive_a, arrive_b, extra, sems = split(
        refs, (7 + 9, 1, 4, 23, 4, 4, len(CROSS), 4, 4, 4 + 6, 25 + 9)
    )
    over = dict(zip(CROSS, over))
    x_in, cot_in, live_in, qkv_in, out_in, up_in, down_in, *vectors_in = ins
    (packed,) = outs
    output_low, input_grad_low, *sums, line_low, line_wide, pack_sem = sems[25:]
    (
        x_low,
        cot_low,
        upstream,
        hat1,
        inv1,
        normed,
        normed_t,
        qkv,
        probs,
        attended,
        attended_t,
        middle,
        hat2,
        inv2,
        second,
        second_t,
        hidden,
        hidden_t,
        pre_low,
        slope,
        incoming,
        middle_low,
        vec_grad,
    ) = acts
    joined, middle_grad, head_grad = qkv, hat2, normed
    exchange, (lines, vec, up_bias, line_grad, line_a, line_b) = extra[:4], extra[4:]
    (
        in_sem,
        own_sem,
        ring_s,
        ring_r,
        row_s,
        row_r,
        core_s,
        core_r,
        line_s,
        line_r,
        give_s,
        give_r,
        over_s,
        over_r,
        sum_s,
        sum_r,
        end_s,
        end_r,
        tail_s,
        tail_r,
        pair_s,
        pair_r,
    ) = sems[:22]
    line_pair = sems[22]
    pre_bias, score_rows = sems[23], sems[24]

    rows = qkv_in.shape[0]
    height = [ref.shape[0] for ref in (qkv_in, out_in, up_in, down_in)]
    sixth = [ref.shape[1] // 6 for ref in (qkv_in, out_in, up_in, down_in)]
    matrix_in = (qkv_in, out_in, up_in, down_in)
    hidden_units = up_in.shape[1]
    reach = (n // 2, n // 2 - 1)

    rep = lax.axis_index("rep")
    me = lax.axis_index("shard")
    core = rep % 2
    row = rep // 2
    position = ring_position(me, n)
    sign = 1 - 2 * core

    def at(k):
        return ring_index((position + sign * k + n) % n, n)

    peers = ((rep, at(1)), (rep, at(-1)))
    partner = (row * 2 + 1 - core, me)
    across = ((1 - row) * 2 + core, me)
    third = (2, row, 1 - row)

    def block(m, b):
        return pl.ds(pl.multiple_of(b * height[m], height[m]), height[m])

    def columns(m, slot, whose):
        width = sixth[m]
        return pl.ds(pl.multiple_of((2 * third[slot] + whose) * width, width), width)

    def piece(m, b, slot):
        return weights[m].at[block(m, b), columns(m, slot, core)]

    def came(d, h):
        return at(-1 - h) if d == 0 else at(1 + h)

    def own_copy(m, slot):
        return pltpu.make_async_copy(
            matrix_in[m].at[:, columns(m, slot, core)], piece(m, me, slot), own_sem.at[m, slot]
        )

    def gather_send(m, slot, d, h):
        view = piece(m, at(-h) if d == 0 else at(h), slot)
        return remote(view, view, ring_s.at[m, slot, d, h], ring_r.at[m, slot, d, h], peers[d])

    def gather_row(m, d, h, slot):
        view = piece(m, came(d, h), slot)
        k = d * reach[0] + h
        return remote(view, view, row_s.at[m, k], row_r.at[m, k], across)

    def gather_core(m, slot, whose):
        view = weights[m].at[:, columns(m, slot, whose)]
        return remote(view, view, core_s.at[m, slot], core_r.at[m, slot], partner)

    def gather_start(m):
        for slot in (MINE, SHARED):
            for d in (0, 1):
                gather_send(m, slot, d, 0).start()

    def gather_hop(m, h, slots=(MINE, SHARED)):
        for slot in slots:
            for d in (0, 1):
                if h < reach[d]:
                    view = piece(m, came(d, h), slot)
                    remote(
                        view, view, ring_s.at[m, slot, d, h], ring_r.at[m, slot, d, h], peers[d]
                    ).wait_recv()
                    if h + 1 < reach[d]:
                        gather_send(m, slot, d, h + 1).start()
                    if slot == MINE:
                        gather_row(m, d, h, MINE).start()

    def gather_relay(m):
        for slot in (MINE, SHARED):
            gather_core(m, slot, core).start()

    def gather_rows(m):
        for d in (0, 1):
            for h in range(reach[d]):
                gather_row(m, d, h, YOURS).wait_recv()
        gather_core(m, YOURS, core).start()

    def gather_end(m):
        for slot in (MINE, SHARED, YOURS):
            gather_core(m, slot, 1 - core).wait_recv()

    def line_send(d, h):
        view = lines.at[at(-h) if d == 0 else at(h)]
        return remote(view, view, line_s.at[d, h], line_r.at[d, h], peers[d])

    def line_hop(h):
        for d in (0, 1):
            if h < reach[d]:
                view = lines.at[came(d, h)]
                remote(view, view, line_s.at[d, h], line_r.at[d, h], peers[d]).wait_recv()
                if h + 1 < reach[d]:
                    line_send(d, h + 1).start()

    def slots_of(m):
        return (SHARED, MINE) if m in over else (SHARED, MINE, YOURS)

    def owner(d, t):
        return at(reach[0] - t) if d == 0 else at(t - reach[1])

    def give(m, slot):
        return remote(
            halves[m].at[1, slot],
            given[m].at[slot],
            give_s.at[m, slot],
            give_r.at[m, slot],
            partner,
        )

    def hand_over(m, d, t):
        rows_of = block(m, owner(d, t))
        return remote(
            halves[m].at[0, YOURS, rows_of],
            over[m].at[rows_of],
            over_s.at[m, d, t],
            over_r.at[m, d, t],
            across,
        )

    def local(m, slot, b):
        total = halves[m][0, slot, block(m, b)].astype(F32) + given[m][slot, block(m, b)].astype(
            F32
        )
        if slot == MINE and m in over:
            total = total + over[m][block(m, b)].astype(F32)
        return total

    def ring_sum(m, slot, d, t):
        return remote(
            halves[m].at[0, slot, block(m, owner(d, t))],
            (arrive_a, arrive_b)[d][m].at[slot, t],
            sum_s.at[m, slot, d, t],
            sum_r.at[m, slot, d, t],
            peers[d],
        )

    def over_steps():
        return [(d, t) for t in range(reach[0] + 1) for d in (0, 1) if t < reach[d] + 1 - d]

    def reduce_over(m, p):
        if p == 0:
            give(m, YOURS).wait_recv()
        for d, t in over_steps():
            if min(t * 4 // reach[0], 3) == p:
                rows_of = block(m, owner(d, t))
                halves[m][0, YOURS, rows_of] = local(m, YOURS, owner(d, t)).astype(LOW)
                hand_over(m, d, t).start()

    def reduce_step(m, slot, t):
        if t == 0:
            give(m, slot).wait_recv()
        for d in (0, 1):
            if t < reach[d]:
                b = owner(d, t)
                if slot == MINE and m in over:
                    hand_over(m, d, t).wait_recv()
                total = local(m, slot, b)
                if t > 0:
                    ring_sum(m, slot, d, t - 1).wait_recv()
                    total = total + (arrive_a, arrive_b)[d][m][slot, t - 1].astype(F32)
                halves[m][0, slot, block(m, b)] = total.astype(LOW)
                ring_sum(m, slot, d, t).start()

    def sum_columns(m, slot, whose):
        width = sixth[m]
        which = third[slot] if m in over else (2, 0, 1)[slot]
        return pl.ds(pl.multiple_of((2 * which + whose) * width, width), width)

    def end_view(m, slot, whose):
        return sums[m].at[:, sum_columns(m, slot, whose)]

    def end_core(m, slot, whose):
        view = end_view(m, slot, whose)
        return remote(view, view, end_s.at[m, slot, 1], end_r.at[m, slot, 1], partner)

    def end_row(m, slot):
        return remote(
            halves[m].at[0, slot, block(m, me)],
            exchange[m].at[slot],
            end_s.at[m, slot, 0],
            end_r.at[m, slot, 0],
            across,
        )

    def end_other(m, slot):
        view = end_view(m, slot, core)
        return remote(view, view, end_s.at[m, MINE, 0], end_r.at[m, MINE, 0], across)

    def reduce_end(m, slot):
        if slot == MINE and m in over:
            hand_over(m, 0, reach[0]).wait_recv()
        total = local(m, slot, me)
        for d in (0, 1):
            if reach[d]:
                ring_sum(m, slot, d, reach[d] - 1).wait_recv()
                total = total + (arrive_a, arrive_b)[d][m][slot, reach[d] - 1].astype(F32)
        if slot == MINE and m in over:
            sums[m][:, sum_columns(m, MINE, core)] = total.astype(LOW)
            end_other(m, MINE).start()
            end_core(m, MINE, core).start()
        else:
            halves[m][0, slot, block(m, me)] = total.astype(LOW)
            end_row(m, slot).start()

    def reduce_exchange(m):
        for slot in slots_of(m):
            if slot == MINE and m in over:
                end_other(m, YOURS).wait_recv()
                end_core(m, YOURS, core).start()
            else:
                end_row(m, slot).wait_recv()
                total = halves[m][0, slot, block(m, me)].astype(F32) + exchange[m][slot].astype(F32)
                sums[m][:, sum_columns(m, slot, core)] = total.astype(LOW)
                end_core(m, slot, core).start()

    def reduce_finish(m):
        for slot in (SHARED, MINE, YOURS):
            end_core(m, slot, 1 - core).wait_recv()

    steps = padded // 16
    slices = [pl.ds(i * 16, 16) for i in range(steps)]
    gain = lambda i: vec[i : i + 1, :]
    live = live_in[0].astype(F32)
    row_id = lax.broadcasted_iota(jnp.int32, (padded, 1), 0)
    row_mask = (row_id < length).astype(F32)
    pair_width = 2 * HEAD_DIM
    pairs = model // pair_width

    def normalise(source, hat, inv):
        for s in slices:
            values = source[s, :]
            centred = values - jnp.mean(values, axis=-1, keepdims=True)
            spread = jnp.mean(centred * centred, axis=-1, keepdims=True)
            inv_std = lax.rsqrt(spread + NORM_EPS)
            hat[s, :] = centred * inv_std
            inv[s, :] = jnp.broadcast_to(inv_std, (16, LANES))

    def scale_shift(hat, low, g, b, mask):
        for i, s in enumerate(slices):
            value = hat[s, :] * gain(g) + gain(b)
            if mask and (i + 1) * 16 > length:
                value = value * row_mask[i * 16 : (i + 1) * 16]
            low[s, :] = value.astype(LOW)

    def transpose(source, target):
        def body(i, carry):
            cols = pl.ds(pl.multiple_of(i * 256, 256), 256)
            target[cols, :] = source[:, cols].T
            return carry

        lax.fori_loop(0, source.shape[1] // 256, body, 0)

    def begin():
        middle[...] = jnp.zeros_like(middle)
        middle[:length, :] = x_low[0].astype(F32)
        incoming[...] = jnp.zeros_like(incoming)
        incoming[:length, :] = cot_low[0].astype(F32) * live
        upstream[...] = incoming[...].astype(LOW)
        vec_grad[...] = jnp.zeros_like(vec_grad)
        vec_grad[7:8, :] = jnp.sum(incoming[...], axis=0, keepdims=True)
        normalise(middle, hat1, inv1)

    def vectors():
        for b in range(n):
            held = lines[b]
            vec[:, b * rows : (b + 1) * rows] = held[:, :rows]
            for e in range(4 * rows // LANES):
                first = b * 4 * rows + e * LANES
                up_bias[:, first : first + LANES] = jnp.broadcast_to(
                    held[8 + e : 9 + e, :], (8, LANES)
                )

    def first_norm():
        scale_shift(hat1, normed, 0, 1, True)
        transpose(normed, normed_t)
        zero = jnp.zeros((1, model), F32)
        for k, v in enumerate((vec[2:3, :], zero, vec[3:4, :])):
            pre_bias[:, k * model : (k + 1) * model] = jnp.broadcast_to(v, (8, model))

    def project(first, last):
        wide = 2 * sixth[QKV] // 2

        def body(c, carry):
            cols = pl.ds(pl.multiple_of(c * wide, wide), wide)
            value = (dot_nn(normed[...], weights[QKV][:, cols]) + pre_bias[0:1, cols]) * row_mask
            factor = jnp.where(c * wide < model, HEAD_DIM**-0.5, 1.0)
            qkv[:, cols] = (value.astype(LOW).astype(F32) * factor).astype(LOW)
            return carry

        lax.fori_loop(first, last, body, 0)

    lane = lax.broadcasted_iota(jnp.int32, (padded, pair_width), 1)
    low_lane = lane < HEAD_DIM
    key_mask = lax.broadcasted_iota(jnp.int32, (1, padded), 1) < length

    def heads(part, p):
        return qkv[:, pl.ds(pl.multiple_of(part * model + p * pair_width, LANES), pair_width)]

    def stacked(value, target):
        wide = value.astype(F32)
        target[:padded, :] = jnp.where(low_lane, wide, 0.0).astype(LOW)
        target[padded:, :] = jnp.where(low_lane, 0.0, wide).astype(LOW)

    def merged(value):
        return jnp.where(low_lane, value[:padded], value[padded:])

    def attend(first, last):
        def body(p, carry):
            stacked(heads(0, p), score_rows.at[0])
            scores = dot_nt(score_rows[0], heads(1, p))
            powers = jnp.where(key_mask, jnp.exp(scores), 0.0)
            total = jnp.sum(powers, axis=-1, keepdims=True)
            weight = (powers * (1.0 / total)).astype(LOW)
            probs[p] = weight
            cols = pl.ds(pl.multiple_of(p * pair_width, LANES), pair_width)
            attended[:, cols] = merged(dot_nn(weight, heads(2, p))).astype(LOW)
            return carry

        lax.fori_loop(first, last, body, 0)

    def mix():
        def body(c, carry):
            cols = pl.ds(pl.multiple_of(c * 256, 256), 256)
            middle[:, cols] = (
                middle[:, cols] + dot_nn(attended[...], weights[OUT][:, cols]) + vec[4:5, cols]
            )
            return carry

        lax.fori_loop(0, model // 256, body, 0)
        normalise(middle, hat2, inv2)
        scale_shift(hat2, second, 5, 6, False)

    def transposes():
        transpose(attended, attended_t)
        transpose(second, second_t)

    wide_hidden = 512

    def expand(first, last):
        def body(c, carry):
            cols = pl.ds(pl.multiple_of(c * wide_hidden, wide_hidden), wide_hidden)
            pre = dot_nn(second[...], weights[UP][:, cols]) + up_bias[0:1, cols]
            cdf = 0.5 * (1.0 + lax.erf(pre * ROOT_HALF))
            density = jnp.exp(-0.5 * pre * pre) * DENSITY_COEF
            value = (pre * cdf).astype(LOW)
            hidden[:, cols] = value
            slope[:, cols] = cdf + pre * density
            hidden_t[cols, :] = value.T
            return carry

        lax.fori_loop(first, last, body, 0)

    def contract():
        def body(c, carry):
            cols = pl.ds(pl.multiple_of(c * 256, 256), 256)
            value = dot_nn(hidden[...], weights[DOWN][:, cols]) + vec[7:8, cols]
            value = (middle[:, cols] + value) * live
            output_low[:, cols] = value.astype(LOW)
            return carry

        lax.fori_loop(0, model // 256, body, 0)

    def gradient(m, left, right, slot):
        width = sixth[m]
        base = (third[slot] if m in over else (2, 0, 1)[slot]) * 2 * width
        if width % 256 == 0:
            count, step = 2 * width // 256, 256
        elif (2 * width) % 256 == 0 and width < 256:
            count, step = 1, 2 * width
        else:
            count, step = 2, width
        tall = left.shape[0]
        high = min(tall, model)

        def body(i, carry):
            c, r = i % count, i // count
            cols = pl.ds(pl.multiple_of(base + c * step, LANES), step)
            down = pl.ds(pl.multiple_of(r * high, high), high)
            value = dot_nn(left[down, :], right[:, cols]).astype(LOW)
            if step > width:
                for whose in range(2):
                    halves[m][(whose + core) % 2, slot, down] = value[
                        :, whose * width : (whose + 1) * width
                    ]
            else:
                per = width // step
                start = pl.multiple_of((c % per) * step, LANES)
                halves[m][(c // per + core) % 2, slot, down, pl.ds(start, step)] = value
            return carry

        lax.fori_loop(0, count * (tall // high), body, 0)
        give(m, slot).start()

    def hidden_back(first, last):
        def body(c, carry):
            cols = pl.ds(pl.multiple_of(c * wide_hidden, wide_hidden), wide_hidden)
            value = dot_nt(upstream[...], weights[DOWN][cols, :]) * slope[:, cols]
            up_bias[:, cols] = jnp.broadcast_to(
                jnp.sum(value, axis=0, keepdims=True), (8, wide_hidden)
            )
            pre_low[:, cols] = value.astype(LOW)
            return carry

        lax.fori_loop(first, last, body, 0)

    def second_back():
        def body(c, carry):
            cols = pl.ds(pl.multiple_of(c * 256, 256), 256)
            incoming[:, cols] = dot_nt(pre_low[...], weights[UP][cols, :])
            return carry

        lax.fori_loop(0, model // 256, body, 0)

    def norm_back(hat, inv, g, add):
        gain_sum = jnp.zeros((1, model), F32)
        bias_sum = jnp.zeros((1, model), F32)
        add_sum = jnp.zeros((1, model), F32)
        for s in slices:
            came_in = incoming[s, :]
            hat_vals = hat[s, :]
            scaled = came_in * gain(g)
            average = jnp.mean(scaled, axis=-1, keepdims=True)
            along = jnp.mean(scaled * hat_vals, axis=-1, keepdims=True)
            value = add[s, :].astype(F32) + inv[s, 0:1] * (scaled - average - hat_vals * along)
            gain_sum += jnp.sum(came_in * hat_vals, axis=0, keepdims=True)
            bias_sum += jnp.sum(came_in, axis=0, keepdims=True)
            add_sum += jnp.sum(value, axis=0, keepdims=True)
            middle_grad[s, :] = value
            middle_low[s, :] = value.astype(LOW)
        vec_grad[g : g + 1, :] = gain_sum
        vec_grad[g + 1 : g + 2, :] = bias_sum
        return add_sum

    def attended_back():
        def body(c, carry):
            cols = pl.ds(pl.multiple_of(c * 256, 256), 256)
            head_grad[:, cols] = dot_nt(middle_low[...], weights[OUT][cols, :]).astype(LOW)
            return carry

        lax.fori_loop(0, model // 256, body, 0)

    def attend_back(first, last):
        def body(p, carry):
            start = pl.multiple_of(p * pair_width, LANES)
            cols = pl.ds(start, pair_width)
            stacked(head_grad[:, cols], score_rows.at[1])
            stacked(heads(0, p), score_rows.at[0])
            weight = probs[p]
            value_grad = dot_tn(weight, score_rows[1])
            prob_grad = dot_nt(score_rows[1], heads(2, p))
            wide = weight.astype(F32)
            along = jnp.sum(wide * prob_grad, axis=-1, keepdims=True)
            score_grad = (wide * (prob_grad - along)).astype(LOW)
            query_grad = merged(dot_nn(score_grad, heads(1, p))) * HEAD_DIM**-0.5
            key_grad = dot_tn(score_grad, score_rows[0])
            vec_grad[2:3, cols] = jnp.sum(query_grad, axis=0, keepdims=True)
            vec_grad[3:4, cols] = jnp.sum(value_grad, axis=0, keepdims=True)
            for k, value in enumerate((query_grad, key_grad, value_grad)):
                joined[:, pl.ds(pl.multiple_of(k * model + start, LANES), pair_width)] = (
                    value.astype(LOW)
                )
            return carry

        lax.fori_loop(first, last, body, 0)

    def first_back():
        def body(c, carry):
            cols = pl.ds(pl.multiple_of(c * 256, 256), 256)
            incoming[:, cols] = dot_nt(joined[...], weights[QKV][cols, :])
            return carry

        lax.fori_loop(0, model // 256, body, 0)

    def tail_local():
        line_grad[...] = jnp.zeros_like(line_grad)
        for b in range(n):
            line_grad[b, 0:8, 0:rows] = vec_grad[0:8, b * rows : (b + 1) * rows]
            for e in range(4 * rows // LANES):
                first = b * 4 * rows + e * LANES
                line_grad[b, 8 + e : 9 + e, :] = up_bias[0:1, first : first + LANES]

    def tail_sum(d, t):
        b = at(reach[0] - t) if d == 0 else at(t - reach[1])
        arrive = (line_a, line_b)[d]
        return remote(line_grad.at[b], arrive.at[t], tail_s.at[d, t], tail_r.at[d, t], peers[d])

    def tail_step(t):
        for d in (0, 1):
            if t < reach[d]:
                b = at(reach[0] - t) if d == 0 else at(t - reach[1])
                if t > 0:
                    tail_sum(d, t - 1).wait_recv()
                    line_grad[b] = line_grad[b] + (line_a, line_b)[d][t - 1]
                tail_sum(d, t).start()

    def pair_copy(k, peer):
        return remote(
            line_pair.at[2 * k], line_pair.at[2 * k + 1], pair_s.at[k], pair_r.at[k], peer
        )

    def tail_end():
        total = line_grad[me]
        for d in (0, 1):
            if reach[d]:
                tail_sum(d, reach[d] - 1).wait_recv()
                total = total + (line_a, line_b)[d][reach[d] - 1]
        line_pair[0] = total
        pair_copy(0, across).start()

    def tail_pair():
        pair_copy(0, across).wait_recv()
        line_pair[2] = line_pair[0] + line_pair[1]
        pair_copy(1, partner).start()

    def tail_finish():
        pair_copy(1, partner).wait_recv()
        line_wide[...] = line_pair[2] + line_pair[3]
        high = line_wide[...].astype(LOW)
        line_low[:, :LANES] = high
        line_low[:, LANES:] = (line_wide[...] - high.astype(F32)).astype(LOW)

    layout = pack_layout(rows, padded, model)

    def pack_copies(name):
        source = {"c": output_low, "fn": input_grad_low, "tf": line_low}.get(name)
        if source is None:
            source = sums["QOUD".index(name[1])]
        copies = []
        for i, (key, first, high, left, width) in enumerate(layout):
            if key == name:
                target = packed.at[pl.ds(first, high), pl.ds(0, width)]
                view = source.at[:, pl.ds(left, width)]
                copies.append(pltpu.make_async_copy(view, target, pack_sem.at[i]))
        return copies

    x_copy = pltpu.make_async_copy(x_in, x_low, in_sem.at[1])
    cot_copy = pltpu.make_async_copy(cot_in, cot_low, in_sem.at[2])
    for m in range(4):
        for slot in (MINE, SHARED, YOURS):
            own_copy(m, slot).start()
    x_copy.start()
    cot_copy.start()

    lines[me] = jnp.zeros_like(lines[me])
    for i, ref in zip(VECTOR_ROWS, vectors_in):
        if i < 8:
            lines[me, i, 0:rows] = ref[...].astype(F32)
        else:
            for e in range(4 * rows // LANES):
                lines[me, i + e, :] = ref[pl.ds(e * LANES, LANES)].astype(F32)

    barrier = pltpu.get_barrier_semaphore()
    for peer in (*peers, partner, across):
        pl.semaphore_signal(barrier, inc=1, device_id=peer, device_id_type=MESH)
    pl.semaphore_wait(barrier, 4)

    for d in (0, 1):
        line_send(d, 0).start()
    for slot in (MINE, SHARED, YOURS):
        own_copy(QKV, slot).wait()
    gather_start(QKV)
    for m in (OUT, UP, DOWN):
        for slot in (MINE, SHARED, YOURS):
            own_copy(m, slot).wait()
    x_copy.wait()
    cot_copy.wait()
    begin()

    def part(total, p):
        return range(total * p // 4, total * (p + 1) // 4)

    def hops(m, p):
        for h in part(reach[0], p):
            gather_hop(m, h)

    def steps_of(m, slot, p):
        for t in part(reach[0], p):
            reduce_step(m, slot, t)

    def lines_of(p):
        for h in part(reach[0], p):
            line_hop(h)

    def tails_of(p):
        for t in part(reach[0], p):
            tail_step(t)

    def first_norm_back():
        norm_back(hat1, inv1, 0, middle_grad)
        input_grad_low[...] = middle_grad[...].astype(LOW)
        tail_local()

    def second_norm_back():
        vec_grad[4:5, :] = norm_back(hat2, inv2, 5, upstream)

    chunks = hidden_units // wide_hidden
    sides = {QKV: (normed_t, joined), OUT: (attended_t, middle_low)}
    sides |= {UP: (second_t, pre_low), DOWN: (hidden_t, upstream)}
    actions = {
        "v": lambda: (vectors(), first_norm()),
        "p": lambda: project(0, 6),
        "a0": lambda: attend(0, pairs // 2),
        "a1": lambda: attend(pairs // 2, pairs),
        "m": mix,
        "t": transposes,
        "u0": lambda: expand(0, chunks // 2),
        "u1": lambda: expand(chunks // 2, chunks),
        "c": contract,
        "hb0": lambda: hidden_back(0, chunks // 2),
        "hb1": lambda: hidden_back(chunks // 2, chunks),
        "sb": second_back,
        "nb": second_norm_back,
        "ob": attended_back,
        "ab0": lambda: attend_back(0, pairs // 2),
        "ab1": lambda: attend_back(pairs // 2, pairs),
        "fb": first_back,
        "fn": first_norm_back,
        "te": tail_end,
        "tp": tail_pair,
        "tf": tail_finish,
    }
    for p in range(4):
        actions[f"l{p}"] = functools.partial(lines_of, p)
        actions[f"t{p}"] = functools.partial(tails_of, p)
    for name, m in (("Q", QKV), ("O", OUT), ("U", UP), ("D", DOWN)):
        actions["G" + name] = functools.partial(gather_start, m)
        actions["R" + name] = functools.partial(gather_relay, m)
        actions["e" + name] = functools.partial(gather_rows, m)
        actions["E" + name] = functools.partial(gather_end, m)
        actions["X" + name] = functools.partial(reduce_exchange, m)
        actions["F" + name] = functools.partial(reduce_finish, m)
        for p in range(4):
            actions[f"g{name}{p}"] = functools.partial(hops, m, p)
            actions[f"o{name}{p}"] = functools.partial(reduce_over, m, p)
        for key, slot in (("s", SHARED), ("m", MINE), ("y", YOURS)):
            actions[f"d{name}{key}"] = functools.partial(gradient, m, *sides[m], slot)
            actions[f"{name}{key}"] = functools.partial(reduce_end, m, slot)
            for p in range(4):
                actions[f"{name}{key}{p}"] = functools.partial(steps_of, m, slot, p)
    for name in ORDER:
        actions[name]()
        for copy in pack_copies(name) if name in {entry[0] for entry in layout} else ():
            copy.start()

    for m in range(4):
        for slot in (SHARED, MINE, YOURS):
            gather_core(m, slot, core).wait_send()
            give(m, slot).wait_send()
            end_core(m, slot, core).wait_send()
        for slot in slots_of(m):
            if slot == MINE and m in over:
                end_other(m, MINE).wait_send()
            else:
                end_row(m, slot).wait_send()
        if m in over:
            for d, t in over_steps():
                hand_over(m, d, t).wait_send()
        for d in (0, 1):
            for h in range(reach[d]):
                gather_row(m, d, h, MINE).wait_send()
                for slot in (SHARED, MINE):
                    gather_send(m, slot, d, h).wait_send()
                for slot in slots_of(m):
                    ring_sum(m, slot, d, h).wait_send()
    for d in (0, 1):
        for h in range(reach[d]):
            line_send(d, h).wait_send()
            tail_sum(d, h).wait_send()
    pair_copy(0, across).wait_send()
    pair_copy(1, partner).wait_send()
    for name in ("c", "fn", "tf", "FQ", "FO", "FU", "FD"):
        for copy in pack_copies(name):
            copy.wait()


def run_layer(layer_input, cotangent, live, matrices, vectors, n):
    line = (16, LANES)
    images, length, model = layer_input.shape
    padded = -(-length // 16) * 16
    hidden_units = matrices[UP].shape[1]
    vmem, dma = pltpu.VMEM, pltpu.SemaphoreType.DMA
    reach = (n // 2, n // 2 - 1)
    height = [a.shape[0] for a in matrices]
    sixth = [a.shape[1] // 6 for a in matrices]
    pairs = model // (2 * HEAD_DIM)
    wide = (padded, model)
    scratch = [vmem((n * a.shape[0], a.shape[1]), LOW) for a in matrices]
    scratch += [
        vmem((1, length, model), LOW),
        vmem((1, length, model), LOW),
        vmem(wide, LOW),
        vmem(wide, F32),
        vmem((padded, LANES), F32),
        vmem(wide, LOW),
        vmem((model, padded), LOW),
        vmem((padded, 3 * model), LOW),
        vmem((pairs, 2 * padded, padded), LOW),
        vmem(wide, LOW),
        vmem((model, padded), LOW),
        vmem(wide, F32),
        vmem(wide, F32),
        vmem((padded, LANES), F32),
        vmem(wide, LOW),
        vmem((model, padded), LOW),
        vmem((padded, hidden_units), LOW),
        vmem((hidden_units, padded), LOW),
        vmem((padded, hidden_units), LOW),
        vmem((padded, hidden_units), F32),
        vmem(wide, F32),
        vmem(wide, LOW),
        vmem((16, model), F32),
    ]
    scratch += [vmem((2, 3, n * r, w), LOW) for r, w in zip(height, sixth)]
    scratch += [vmem((3, n * r, w), LOW) for r, w in zip(height, sixth)]
    slots = [3 - (m in CROSS) for m in range(4)]
    scratch += [vmem((n * height[m], sixth[m]), LOW) for m in CROSS]
    scratch += [vmem((k, reach[0], r, w), LOW) for k, r, w in zip(slots, height, sixth)]
    scratch += [vmem((k, max(reach[1], 1), r, w), LOW) for k, r, w in zip(slots, height, sixth)]
    scratch += [vmem((k - 1 + k // 3, r, w), LOW) for k, r, w in zip(slots, height, sixth)]
    scratch += [
        vmem((n,) + line, F32),
        vmem((16, model), F32),
        vmem((8, hidden_units), F32),
        vmem((n,) + line, F32),
        vmem((reach[0],) + line, F32),
        vmem((max(reach[1], 1),) + line, F32),
    ]
    scratch += [
        dma((3,)),
        dma((4, 3)),
        dma((4, 2, 2, reach[0])),
        dma((4, 2, 2, reach[0])),
        dma((4, n - 1)),
        dma((4, n - 1)),
        dma((4, 3)),
        dma((4, 3)),
        dma((2, reach[0])),
        dma((2, reach[0])),
        dma((4, 3)),
        dma((4, 3)),
        dma((4, 2, reach[0] + 1)),
        dma((4, 2, reach[0] + 1)),
        dma((4, 3, 2, reach[0])),
        dma((4, 3, 2, reach[0])),
        dma((4, 3, 2)),
        dma((4, 3, 2)),
        dma((2, reach[0])),
        dma((2, reach[0])),
        dma((2,)),
        dma((2,)),
        vmem((4,) + line, F32),
        vmem((8, 3 * model), F32),
        vmem((2, 2 * padded, 2 * HEAD_DIM), LOW),
    ]
    layout = pack_layout(matrices[QKV].shape[0], padded, model)
    scratch += [vmem(wide, LOW)] * 2 + [vmem(a.shape, LOW) for a in matrices]
    scratch += [vmem((16, 2 * LANES), LOW), vmem(line, F32), dma((len(layout),))]
    anywhere = pl.BlockSpec(memory_space=pl.ANY)
    near = pl.BlockSpec(memory_space=pltpu.VMEM)
    return pl.pallas_call(
        functools.partial(layer_kernel, n, length, padded, model),
        out_shape=jax.ShapeDtypeStruct((layout[-1][1] + layout[-1][2], model), LOW),
        in_specs=[anywhere] * 2 + [pl.BlockSpec(memory_space=pltpu.SMEM)] + [anywhere] * 4 + [near] * 9,
        out_specs=anywhere,
        scratch_shapes=scratch,
        compiler_params=pltpu.CompilerParams(
            collective_id=0, has_side_effects=True, vmem_limit_bytes=60 * 1024 * 1024
        ),
        name="layer",
    )(layer_input, cotangent, live, *matrices, *vectors)


norm_eps = 1e-06
root_half = 0.7071067811865476
density_coef = 0.3989422804014327


def matmul(operand, factor):
    flat = operand.reshape(-1, operand.shape[-1])
    product = jnp.dot(flat, factor, preferred_element_type=jnp.float32)
    return product.reshape(operand.shape[:-1] + (factor.shape[-1],))


def outer_product(operand, factor):
    return jnp.dot(
        operand.reshape(-1, operand.shape[-1]).T,
        factor.reshape(-1, factor.shape[-1]),
        preferred_element_type=jnp.float32,
    )


def batched(form, operand, factor):
    return jnp.einsum(form, operand, factor, preferred_element_type=jnp.float32)


def layer_norm(values, norm_gain, norm_bias):
    average = jnp.mean(values, axis=-1, keepdims=True)
    centred = values - average
    spread = jnp.mean(centred * centred, axis=-1, keepdims=True)
    inv_std = lax.rsqrt(spread + norm_eps)
    hat_vals = centred * inv_std
    return (
        hat_vals * norm_gain.astype(jnp.float32) + norm_bias.astype(jnp.float32),
        hat_vals,
        inv_std,
    )


def norm_back(incoming, hat_vals, inv_std, norm_gain):
    scaled = incoming * norm_gain.astype(jnp.float32)
    return inv_std * (
        scaled
        - jnp.mean(scaled, axis=-1, keepdims=True)
        - hat_vals * jnp.mean(scaled * hat_vals, axis=-1, keepdims=True)
    )


def forward_pass(params, layer_input, live):
    (
        first_gain,
        first_bias,
        qkv_weight,
        query_bias,
        value_bias,
        out_weight,
        out_bias,
        second_gain,
        second_bias,
        up_weight,
        up_bias,
        down_weight,
        down_bias,
    ) = params
    images, length, model_width = layer_input.shape
    head_count = model_width // HEAD_DIM
    score_scale = HEAD_DIM ** (-0.5)
    stream = layer_input.astype(jnp.float32)
    normed, first_hat, first_inv = layer_norm(stream, first_gain, first_bias)
    normed = normed.astype(jnp.bfloat16)
    projected = matmul(normed, qkv_weight)
    shape_heads = (images, length, head_count, HEAD_DIM)
    queries = (
        (projected[..., :model_width] + query_bias.astype(jnp.float32))
        .astype(jnp.bfloat16)
        .reshape(shape_heads)
    )
    key_rows = (
        projected[..., model_width : 2 * model_width].astype(jnp.bfloat16).reshape(shape_heads)
    )
    values = (
        (projected[..., 2 * model_width :] + value_bias.astype(jnp.float32))
        .astype(jnp.bfloat16)
        .reshape(shape_heads)
    )
    scores = batched("bqhd,bkhd->bhqk", queries, key_rows) * score_scale
    log_total = jnp.log(jnp.sum(jnp.exp(scores), axis=-1, keepdims=True))
    weights = jnp.exp(scores - log_total).astype(jnp.bfloat16)
    attended = (
        batched("bhqk,bkhd->bqhd", weights, values)
        .reshape(images, length, model_width)
        .astype(jnp.bfloat16)
    )
    middle = stream + matmul(attended, out_weight) + out_bias.astype(jnp.float32)
    second_normed, second_hat, second_inv = layer_norm(middle, second_gain, second_bias)
    second_normed = second_normed.astype(jnp.bfloat16)
    hidden_pre = matmul(second_normed, up_weight) + up_bias.astype(jnp.float32)
    normal_cdf = 0.5 * (1.0 + lax.erf(hidden_pre * root_half))
    hidden = (hidden_pre * normal_cdf).astype(jnp.bfloat16)
    result = middle + matmul(hidden, down_weight) + down_bias.astype(jnp.float32)
    image_mask = live.astype(jnp.float32)[:, None, None]
    output = (result * image_mask).astype(jnp.bfloat16)
    saved = (
        normed,
        first_hat,
        first_inv,
        queries,
        key_rows,
        values,
        log_total,
        attended,
        second_normed,
        second_hat,
        second_inv,
        hidden_pre,
        normal_cdf,
        hidden,
        image_mask,
    )
    return (output, saved)


def backward_pass(params, saved, cotangent):
    (
        first_gain,
        first_bias,
        qkv_weight,
        query_bias,
        value_bias,
        out_weight,
        out_bias,
        second_gain,
        second_bias,
        up_weight,
        up_bias,
        down_weight,
        down_bias,
    ) = params
    (
        normed,
        first_hat,
        first_inv,
        queries,
        key_rows,
        values,
        log_total,
        attended,
        second_normed,
        second_hat,
        second_inv,
        hidden_pre,
        normal_cdf,
        hidden,
        image_mask,
    ) = saved
    images, length, head_count, head_width = queries.shape
    flat_shape = (images, length, head_count * head_width)
    score_scale = HEAD_DIM ** (-0.5)
    upstream = cotangent.astype(jnp.float32) * image_mask
    upstream_low = upstream.astype(jnp.bfloat16)
    down_weight_grad = outer_product(hidden, upstream_low)
    down_bias_grad = jnp.sum(upstream, axis=(0, 1))
    hidden_grad = matmul(upstream_low, down_weight.T)
    density = jnp.exp(-0.5 * hidden_pre * hidden_pre) * density_coef
    pre_grad = hidden_grad * (normal_cdf + hidden_pre * density)
    pre_low = pre_grad.astype(jnp.bfloat16)
    up_weight_grad = outer_product(second_normed, pre_low)
    up_bias_grad = jnp.sum(pre_grad, axis=(0, 1))
    second_in = matmul(pre_low, up_weight.T)
    second_gain_grad = jnp.sum(second_in * second_hat, axis=(0, 1))
    second_bias_grad = jnp.sum(second_in, axis=(0, 1))
    middle_grad = upstream + norm_back(second_in, second_hat, second_inv, second_gain)
    middle_low = middle_grad.astype(jnp.bfloat16)
    out_weight_grad = outer_product(attended, middle_low)
    out_bias_grad = jnp.sum(middle_grad, axis=(0, 1))
    attended_grad = matmul(middle_low, out_weight.T).astype(jnp.bfloat16).reshape(queries.shape)
    again_scores = batched("bqhd,bkhd->bhqk", queries, key_rows) * score_scale
    probs = jnp.exp(again_scores - log_total)
    probs_low = probs.astype(jnp.bfloat16)
    value_grad = batched("bhqk,bqhd->bkhd", probs_low, attended_grad)
    prob_grad = batched("bqhd,bkhd->bhqk", attended_grad, values)
    score_grad = (
        probs * (prob_grad - jnp.sum(probs * prob_grad, axis=-1, keepdims=True)) * score_scale
    ).astype(jnp.bfloat16)
    query_grad = batched("bhqk,bkhd->bqhd", score_grad, key_rows).reshape(flat_shape)
    key_grad = batched("bhqk,bqhd->bkhd", score_grad, queries).reshape(flat_shape)
    value_grad = value_grad.reshape(flat_shape)
    joined = jnp.concatenate([query_grad, key_grad, value_grad], axis=-1).astype(jnp.bfloat16)
    qkv_weight_grad = outer_product(normed, joined)
    query_bias_grad = jnp.sum(query_grad, axis=(0, 1))
    value_bias_grad = jnp.sum(value_grad, axis=(0, 1))
    first_in = matmul(joined, qkv_weight.T)
    first_gain_grad = jnp.sum(first_in * first_hat, axis=(0, 1))
    first_bias_grad = jnp.sum(first_in, axis=(0, 1))
    middle_grad = middle_grad + norm_back(first_in, first_hat, first_inv, first_gain)
    input_grad = middle_grad.astype(jnp.bfloat16)
    grads = (
        first_gain_grad,
        first_bias_grad,
        qkv_weight_grad,
        query_bias_grad,
        value_bias_grad,
        out_weight_grad,
        out_bias_grad,
        second_gain_grad,
        second_bias_grad,
        up_weight_grad,
        up_bias_grad,
        down_weight_grad,
        down_bias_grad,
    )
    return (input_grad, grads)


def places(n):
    rep = lax.axis_index("rep")
    me = lax.axis_index("shard")
    core = rep % 2
    row = rep // 2
    position = ring_position(me, n)
    right = (rep, ring_index((position + 1) % n, n))
    left = (rep, ring_index((position + n - 1) % n, n))
    partner = (row * 2 + 1 - core, me)
    across = ((1 - row) * 2 + core, me)
    return me, core, row, position, right, left, partner, across


def greet(peers):
    barrier = pltpu.get_barrier_semaphore()
    for peer in peers:
        pl.semaphore_signal(barrier, inc=1, device_id=peer, device_id_type=MESH)
    pl.semaphore_wait(barrier, len(peers))


def remote(source, target, send, recv, device):
    return pltpu.make_async_remote_copy(
        src_ref=source,
        dst_ref=target,
        send_sem=send,
        recv_sem=recv,
        device_id=device,
        device_id_type=MESH,
    )


def window(refs, side, part, block, width):
    qkv, out, up, down = refs
    if side == 2:
        return [(None, down.at[block, part])]
    if side == 1:
        return [(None, up.at[block, :, pl.ds(pl.multiple_of(part * width, width), width)])]
    inner = part - part // 3
    return [
        (part < 3, qkv.at[block, :, pl.ds(pl.multiple_of(inner * width, width), width)]),
        (part == 3, out.at[block]),
    ]


def start_each(views, make):
    for condition, view in views:
        if condition is None:
            make(view).start()
        else:
            pl.when(condition)(make(view).start)


def gather_kernel(
    n,
    width,
    qkv_in,
    out_in,
    up_in,
    down_in,
    line_in,
    qkv_ref,
    out_ref,
    up_ref,
    down_ref,
    line_ref,
    local_sem,
    ring_s,
    ring_r,
    core_s,
    core_r,
    row_s,
    row_r,
    last_s,
    last_r,
    line_s,
    line_r,
):
    me, core, row, position, right, left, partner, across = places(n)
    refs = (qkv_ref, out_ref, up_ref, down_ref)
    pairs = zip((qkv_in, out_in, up_in, down_in, line_in), refs + (line_ref,))
    locals_ = [
        pltpu.make_async_copy(source, target.at[me], local_sem.at[i])
        for i, (source, target) in enumerate(pairs)
    ]
    for copy in locals_:
        copy.start()
    greet((right, left, partner, across))
    for copy in locals_:
        copy.wait()

    def block(way, r):
        return ring_index((position + (1 if way else n - 1) * r) % n, n)

    def views(i, r, whose):
        way, kind = i // 2, i % 2
        side, part = (2, 2 * whose + way) if kind else (way, 2 * whose + row)
        return window(refs, side, part, block(way, r), width)

    def over(way, r, whose):
        return window(refs, way, 2 * whose + 1 - row, block(way, r), width)

    def ring(i, r):
        peer = left if i // 2 else right
        return lambda v: remote(v, v, ring_s.at[i, r], ring_r.at[i, r], peer)

    def to_core(i, r):
        return lambda v: remote(v, v, core_s.at[i, r], core_r.at[i, r], partner)

    def to_row(way, r):
        return lambda v: remote(v, v, row_s.at[way, r], row_r.at[way, r], across)

    def to_last(way, r):
        return lambda v: remote(v, v, last_s.at[way, r], last_r.at[way, r], partner)

    def line(r):
        view = line_ref.at[block(0, r)]
        return remote(view, view, line_s.at[r], line_r.at[r], right)

    def one(vs):
        return vs[0][1]

    for i in range(4):
        start_each(views(i, 0, core), ring(i, 0))
    line(0).start()

    def relay(r):
        for way in range(2):
            to_row(way, r)(one(over(way, r + 1, core))).wait_recv()
            start_each(over(way, r + 1, core), to_last(way, r))

    def step(r, carry):
        for i in (0, 2, 1, 3):
            got = views(i, r + 1, core)
            ring(i, r)(one(got)).wait_recv()

            @pl.when(r < n - 2)
            def _():
                start_each(got, ring(i, r + 1))

            if i % 2 == 0:
                start_each(got, to_row(i // 2, r))
            start_each(got, to_core(i, r))
        line(r).wait_recv()

        @pl.when(r < n - 2)
        def _():
            line(r + 1).start()

        @pl.when(r > 0)
        def _():
            relay(r - 1)

        return carry

    lax.fori_loop(0, n - 1, step, 0)
    relay(n - 2)

    def finish(r, carry):
        for i in range(4):
            view = one(views(i, r, core))
            ring(i, r)(view).wait_send()
            to_core(i, r)(view).wait_send()
            to_core(i, r)(view).wait_recv()
        for way in range(2):
            view = one(views(2 * way, r, core))
            to_row(way, r)(view).wait_send()
            to_last(way, r)(view).wait_send()
            to_last(way, r)(view).wait_recv()
        line(r).wait_send()
        return carry

    lax.fori_loop(0, n - 1, finish, 0)


def gather_all(arrays, n, width):
    dma = pltpu.SemaphoreType.DMA
    return pl.pallas_call(
        functools.partial(gather_kernel, n, width),
        out_shape=[jax.ShapeDtypeStruct((n,) + a.shape, a.dtype) for a in arrays],
        in_specs=[pl.BlockSpec(memory_space=pltpu.VMEM)] * len(arrays),
        out_specs=[pl.BlockSpec(memory_space=pl.ANY)] * len(arrays),
        scratch_shapes=[dma((len(arrays),))]
        + [dma((4, n - 1))] * 4
        + [dma((2, n - 1))] * 4
        + [dma((n - 1,))] * 2,
        compiler_params=pltpu.CompilerParams(collective_id=0, has_side_effects=True),
        name="gather_all",
    )(*arrays)


def reduce_kernel(
    n,
    width,
    qkv_ref,
    out_ref,
    up_ref,
    down_ref,
    line_ref,
    sums,
    line_out,
    own,
    given,
    arrive,
    over,
    other,
    line_send,
    line_got,
    line_pair,
    own_sem,
    given_s,
    given_r,
    ring_s,
    ring_r,
    row_s,
    row_r,
    end_row_s,
    end_row_r,
    end_core_s,
    end_core_r,
    line_s,
    line_r,
    pair_s,
    pair_r,
):
    me, core, row, position, right, left, partner, across = places(n)
    refs = (qkv_ref, out_ref, up_ref, down_ref)
    f32 = jnp.float32

    def block(way, k):
        return ring_index((position + (1 if way else n - 1) * (k + 1)) % n, n)

    def source(i, k, whose):
        way, kind = i % 2, i // 2
        side, part = (
            (way, 2 * whose + row),
            (2, 2 * whose + way),
            (way, 2 * whose + 1 - row),
        )[kind]
        return window(refs, side, part, block(way, k), width)

    def load(i, k):
        return lambda v: pltpu.make_async_copy(v, own.at[i, k], own_sem.at[i, k])

    def give(i, k):
        return lambda v: remote(v, given.at[i, k], given_s.at[i, k], given_r.at[i, k], partner)

    def ring(i, k):
        peer = left if i % 2 else right
        return remote(own.at[i, k], arrive.at[i, k], ring_s.at[i, k], ring_r.at[i, k], peer)

    def to_row(way, k):
        return remote(
            own.at[4 + way, k], over.at[way, k], row_s.at[way, k], row_r.at[way, k], across
        )

    def line_ring(k):
        return remote(line_send.at[k], line_got.at[k], line_s.at[k], line_r.at[k], right)

    order = (4, 5, 2, 3, 0, 1)

    def loads(k, carry):
        for i in order:
            start_each(source(i, k, core), load(i, k))
        return carry

    lax.fori_loop(0, n, loads, 0)
    greet((right, left, partner, across))

    def gives(k, carry):
        for i in order:
            start_each(source(i, k, 1 - core), give(i, k))
        return carry

    lax.fori_loop(0, n, gives, 0)

    def take(i, k):
        view = source(i, k, core)[0][1]
        load(i, k)(view).wait()
        give(i, k)(view).wait_recv()
        return own[i, k].astype(f32) + given[i, k].astype(f32)

    def put(i, k, total):
        own[i, k] = total.astype(own.dtype)

    def ahead(k):
        for way in range(2):
            put(4 + way, k, take(4 + way, k))
            to_row(way, k).start()

    def partial(i, k, first):
        total = take(i, k)
        if i < 2:
            to_row(i, k).wait_recv()
            total = total + over[i, k].astype(f32)
        if not first:
            ring(i, k - 1).wait_recv()
            total = total + arrive[i, k - 1].astype(f32)
        return total

    ahead(0)
    line_send[0] = line_ref[block(0, 0)]
    line_ring(0).start()
    ahead(1)
    for i in (2, 3, 0, 1):
        put(i, 0, partial(i, 0, True))
        ring(i, 0).start()

    def step(k, carry):
        ahead(k + 1)
        for i in (2, 3, 0, 1):
            put(i, k, partial(i, k, False))
            ring(i, k).start()
        line_ring(k - 1).wait_recv()
        line_send[k] = line_ref[block(0, k)] + line_got[k - 1]
        line_ring(k).start()
        return carry

    lax.fori_loop(1, n - 1, step, 0)

    def end_row(i, k=None):
        if i < 2:
            view = sums.at[i, 2 * core + row]
            return remote(view, view, end_row_s.at[i], end_row_r.at[i], across)
        return remote(
            own.at[i, n - 1], other.at[i - 2], end_row_s.at[i], end_row_r.at[i], across
        )

    def end_core(j, side, part):
        view = sums.at[side, part]
        return remote(view, view, end_core_s.at[j], end_core_r.at[j], partner)

    for i in (2, 3):
        put(i, n - 1, partial(i, n - 1, False))
        end_row(i).start()
    line_ring(n - 2).wait_recv()
    line_pair[0] = line_ref[me] + line_got[n - 2]
    pair_row = remote(line_pair.at[0], line_pair.at[1], pair_s.at[0], pair_r.at[0], across)
    pair_row.start()
    for way in (0, 1):
        sums[way, 2 * core + row] = partial(way, n - 1, False).astype(sums.dtype)
        end_row(way).start()
        end_core(way, way, 2 * core + row).start()
    pair_row.wait()
    line_pair[2] = line_pair[0] + line_pair[1]
    pair_core = remote(line_pair.at[2], line_pair.at[3], pair_s.at[1], pair_r.at[1], partner)
    pair_core.start()
    for way in (0, 1):
        end_row(2 + way).wait_recv()
        total = own[2 + way, n - 1].astype(f32) + other[way].astype(f32)
        sums[2, 2 * core + way] = total.astype(sums.dtype)
        end_core(2 + way, 2, 2 * core + way).start()
    for way in (0, 1):
        end_row(way).wait_recv()
        end_core(4 + way, way, 2 * core + 1 - row).start()
    pair_core.wait()
    line_out[...] = line_pair[2] + line_pair[3]
    for i in range(4):
        end_row(i).wait_send()
    for j in range(6):
        copy = end_core(j, 0, 0)
        copy.wait_send()
        copy.wait_recv()

    def finish(k, carry):
        for i in range(6):
            give(i, k)(source(i, k, core)[0][1]).wait_send()
        for way in range(2):
            to_row(way, k).wait_send()
        return carry

    lax.fori_loop(0, n, finish, 0)

    def finish_ring(k, carry):
        for i in range(4):
            ring(i, k).wait_send()
        line_ring(k).wait_send()
        return carry

    lax.fori_loop(0, n - 1, finish_ring, 0)


def reduce_all(arrays, n, width):
    dma = pltpu.SemaphoreType.DMA
    vmem = pltpu.VMEM
    rows = arrays[0].shape[1]
    low = arrays[0].dtype
    line = arrays[-1].shape[1:]
    anywhere = pl.BlockSpec(memory_space=pl.ANY)
    near = pl.BlockSpec(memory_space=pltpu.VMEM)
    return pl.pallas_call(
        functools.partial(reduce_kernel, n, width),
        out_shape=[
            jax.ShapeDtypeStruct((3, 4, rows, width), low),
            jax.ShapeDtypeStruct(line, jnp.float32),
        ],
        in_specs=[anywhere] * 4 + [near],
        out_specs=[near, near],
        scratch_shapes=[
            vmem((6, n, rows, width), low),
            vmem((6, n, rows, width), low),
            vmem((4, n - 1, rows, width), low),
            vmem((2, n, rows, width), low),
            vmem((2, rows, width), low),
            vmem((n - 1,) + line, jnp.float32),
            vmem((n - 1,) + line, jnp.float32),
            vmem((4,) + line, jnp.float32),
            dma((6, n)),
            dma((6, n)),
            dma((6, n)),
            dma((4, n - 1)),
            dma((4, n - 1)),
            dma((2, n)),
            dma((2, n)),
            dma((4,)),
            dma((4,)),
            dma((6,)),
            dma((6,)),
            dma((n - 1,)),
            dma((n - 1,)),
            dma((2,)),
            dma((2,)),
        ],
        compiler_params=pltpu.CompilerParams(
            collective_id=1, has_side_effects=True, vmem_limit_bytes=56 * 1024 * 1024
        ),
        name="reduce_all",
    )(*arrays)


def per_device_in_parts(n, layer_input, cotangent, live, *params):
    width = params[0].shape[0] * n
    rows = params[0].shape[0]
    matrices = [i for i, p in enumerate(params) if p.ndim == 2]
    vectors = [i for i, p in enumerate(params) if p.ndim == 1]
    shapes = [params[i].shape for i in matrices]
    assert shapes == [(rows, 3 * width), (rows, width), (rows, 4 * width), (4 * rows, width)]
    lengths = [params[i].shape[0] for i in vectors]
    tall = -(-sum(lengths) // (16 * LANES)) * 16
    spare = tall * LANES - sum(lengths)

    line = jnp.concatenate([params[i] for i in vectors] + [jnp.zeros(spare, params[0].dtype)])
    sent = [params[i] for i in matrices]
    sent[3] = sent[3].reshape(4, rows, width)
    *full, lines = gather_all(sent + [line.reshape(tall, LANES)], n, width)
    gathered = [None] * len(params)
    for i, array in zip(matrices, full):
        gathered[i] = array.reshape(n * params[i].shape[0], params[i].shape[1])
    tail = lines.reshape(n, -1)
    at = 0
    for i, length in zip(vectors, lengths):
        gathered[i] = tail[:, at : at + length].reshape(-1)
        at += length

    output, saved = forward_pass(gathered, layer_input, live)
    input_grad, grads = backward_pass(gathered, saved, cotangent)

    low = jnp.bfloat16
    blocks = [grads[i].astype(low).reshape((n,) + a.shape) for i, a in zip(matrices, sent)]
    parts = [grads[i].reshape(n, -1) for i in vectors] + [jnp.zeros((n, spare), jnp.float32)]
    blocks.append(jnp.concatenate(parts, axis=1).reshape(n, tall, LANES))
    sums, tail = reduce_all(blocks, n, width)

    def joined(pieces):
        return jnp.swapaxes(pieces, 0, 1).reshape(rows, -1).astype(jnp.float32)

    results = [None] * len(params)
    whole = (
        joined(sums[0, :3]),
        sums[0, 3].astype(jnp.float32),
        joined(sums[1]),
        sums[2].reshape(4 * rows, width).astype(jnp.float32),
    )
    for i, array in zip(matrices, whole):
        results[i] = array
    tail = tail.reshape(-1)
    at = 0
    for i, length in zip(vectors, lengths):
        results[i] = tail[at : at + length]
        at += length
    return (output, input_grad, *results)


VECTOR_ROWS = (0, 1, 2, 3, 4, 5, 6, 8, 7)


def finish_kernel(rows, layout, packed, *refs):
    streams_out, wide_out, vectors_out, wide, streams, (low, in_sem, out_sem) = split(
        refs, (2, 4, 9, 4, 2, 3)
    )
    place = {}
    for i, (name, first, high, left, width) in enumerate(layout):
        view = pl.ds(first, high), pl.ds(0, width)
        copy = pltpu.make_async_copy(packed.at[view], low.at[view], in_sem.at[i])
        copy.start()
        place.setdefault(name, []).append((copy, first, high, left, width))
    store = [
        pltpu.make_async_copy(source, target, out_sem.at[i])
        for i, (source, target) in enumerate(zip((*wide, *streams), (*wide_out, *streams_out)))
    ]
    for m in (DOWN, UP, QKV, OUT):
        for copy, first, high, left, width in place[("FQ", "FO", "FU", "FD")[m]]:
            copy.wait()
            wide[m][:, left : left + width] = low[first : first + high, :].astype(F32)
        store[m].start()
    for i, name in enumerate(("c", "fn")):
        copy, first, high, _, _ = place[name][0]
        copy.wait()
        streams[i][0] = low[first : first + high, :][: streams[i].shape[1]]
        store[4 + i].start()
    copy, first, high, _, _ = place["tf"][0]
    copy.wait()
    line = low[first : first + high, :LANES].astype(F32)
    line = line + low[first : first + high, LANES : 2 * LANES].astype(F32)
    for i, ref in zip(VECTOR_ROWS, vectors_out):
        if i < 8:
            ref[...] = line[i, 0:rows]
        else:
            for e in range(4 * rows // LANES):
                ref[pl.ds(e * LANES, LANES)] = line[i + e, :]
    for copy in store:
        copy.wait()


def finish(packed, stream, matrices, vectors):
    rows, model = matrices[QKV].shape[0], stream.shape[2]
    layout = pack_layout(rows, -(-stream.shape[1] // 16) * 16, model)
    far = pl.BlockSpec(memory_space=pltpu.HBM)
    near = pl.BlockSpec(memory_space=pltpu.VMEM)
    shape = jax.ShapeDtypeStruct
    return pl.pallas_call(
        functools.partial(finish_kernel, rows, layout),
        out_shape=[shape(stream.shape, LOW)] * 2
        + [shape(a.shape, F32) for a in matrices]
        + [shape(a.shape, F32) for a in vectors],
        in_specs=[far],
        out_specs=[far] * 6 + [near] * 9,
        scratch_shapes=[pltpu.VMEM(a.shape, F32) for a in matrices]
        + [pltpu.VMEM(stream.shape, LOW)] * 2
        + [pltpu.VMEM(packed.shape, LOW)]
        + [pltpu.SemaphoreType.DMA((k,)) for k in (len(layout), 6)],
        compiler_params=pltpu.CompilerParams(vmem_limit_bytes=32 * 1024 * 1024),
        name="finish",
    )(packed)


def per_device(n, layer_input, cotangent, live, *params):
    rows = params[0].shape[0]
    if rows % 32 or rows > LANES or layer_input.shape[0] != 1:
        return per_device_in_parts(n, layer_input, cotangent, live, *params)
    matrices = [p for p in params if p.ndim == 2]
    vectors = [p for p in params if p.ndim == 1]
    packed = run_layer(layer_input, cotangent, live, matrices, vectors, n)
    done = finish(packed, layer_input, matrices, vectors)
    wide, tall = list(done[2:6]), list(done[6:])
    return (*done[:2], *((wide if p.ndim == 2 else tall).pop(0) for p in params))


def solution(mesh):
    whole = P(("rep", "shard"), None, None)
    vector, matrix = P("shard"), P("shard", None)
    ranks = (1, 1, 2, 1, 1, 2, 1, 1, 1, 2, 1, 2, 1)
    params = tuple(matrix if rank == 2 else vector for rank in ranks)
    return jax.shard_map(
        functools.partial(per_device, mesh.shape["shard"]),
        mesh=mesh,
        in_specs=(whole, whole, P(("rep", "shard"))) + params,
        out_specs=(whole, whole) + params,
        check_vma=False,
    )
```

```python
import functools

import jax
import jax.numpy as jnp
from jax import lax
from jax.experimental import pallas as pl
from jax.experimental.pallas import tpu as pltpu
from jax.sharding import PartitionSpec as P

HEAD_DIM = 64
LANES = 128
NORM_EPS = 1e-06
ROOT_HALF = 0.7071067811865476
DENSITY_COEF = 0.3989422804014327
MESH = pl.DeviceIdType.MESH
F32 = jnp.float32
LOW = jnp.bfloat16

QKV, OUT, UP, DOWN = range(4)
CROSS = (UP, DOWN)
SHARED, MINE, YOURS = range(3)


def ring_index(position, n):
    half = position // (n // 2)
    return (1 - half) * 2 * position + half * (2 * (n - 1 - position) + 1)


def ring_position(index, n):
    odd = index % 2
    step = index // 2
    return (1 - odd) * step + odd * (n - 1 - step)


def remote(source, target, send, recv, device):
    return pltpu.make_async_remote_copy(
        src_ref=source,
        dst_ref=target,
        send_sem=send,
        recv_sem=recv,
        device_id=device,
        device_id_type=MESH,
    )


def dot_nn(a, b):
    return jnp.dot(a, b, preferred_element_type=F32)


def dot_nt(a, b):
    return lax.dot_general(a, b, (((1,), (1,)), ((), ())), preferred_element_type=F32)


def dot_tn(a, b):
    return lax.dot_general(a, b, (((0,), (0,)), ((), ())), preferred_element_type=F32)


def split(refs, counts):
    at = 0
    for count in counts:
        yield refs[at : at + count]
        at += count

ORDER = (
    "GO", "gQ0", "gO0", "l0", "gQ1", "gO1", "l1", "gQ2", "gO2", "GU", "l2", "gQ3", "gO3", "l3",
    "RQ", "RO", "v", "gU0", "eQ", "eO", "gU1", "EQ", "p", "gU2", "GD", "a0", "gU3", "RU", "a1",
    "gD0", "EO", "m", "eU", "t", "gD1", "EU", "u0", "u1", "gD2", "dDy", "dDs", "dDm", "oD0", "Ds0",
    "gD3", "RD", "oD1", "Dm0", "eD", "Ds1", "oD2", "Dm1", "oD3", "ED", "hb0", "Ds2", "hb1", "dUs",
    "dUy", "dUm", "Dm2", "Us0", "oU0", "oU1", "oU2", "oU3", "sb", "Ds3", "nb", "Dm3", "Us1", "dOs",
    "dOm", "dOy", "Um0", "ob", "Os0", "Om0", "Oy0", "ab0", "Us2", "Um1", "Os1", "Om1", "Oy1", "ab1",
    "dQs", "dQm", "dQy", "Us3", "Um2", "Os2", "Om2", "Oy2", "Qs0", "Qm0", "Qy0", "Um3", "Os3",
    "Om3", "Oy3", "Ds", "Dm", "fb", "fn", "t0", "Qs1", "Qm1", "Qy1", "Us", "t1", "XD", "Um", "Qs2",
    "Qm2", "Qy2", "t2", "Os", "Om", "Oy", "XU", "c", "Qs3", "Qm3", "Qy3", "t3", "XO", "Qs", "Qm",
    "Qy", "te", "XQ", "tp", "tf", "FQ", "FO", "FU", "FD",
)


def pack_layout(rows, padded, model):
    layout, first = [], 0
    for name, high, parts, width in (
        ("FD", 4 * rows, 1, model),
        ("FU", rows, 4, model),
        ("FQ", rows, 3, model),
        ("FO", rows, 1, model),
        ("c", padded, 1, model),
        ("fn", padded, 1, model),
        ("tf", 16, 1, 2 * LANES),
    ):
        for k in range(parts):
            layout.append((name, first, high, k * width, width))
            first += high
    return layout


def layer_kernel(n, length, padded, model, *refs):
    ins, outs, weights, acts, halves, given, over, arrive_a, arrive_b, extra, sems = split(
        refs, (7 + 9, 1, 4, 23, 4, 4, len(CROSS), 4, 4, 4 + 6, 25 + 9)
    )
    over = dict(zip(CROSS, over))
    x_in, cot_in, live_in, qkv_in, out_in, up_in, down_in, *vectors_in = ins
    (packed,) = outs
    output_low, input_grad_low, *sums, line_low, line_wide, pack_sem = sems[25:]
    (
        x_low,
        cot_low,
        upstream,
        hat1,
        inv1,
        normed,
        normed_t,
        qkv,
        probs,
        attended,
        attended_t,
        middle,
        hat2,
        inv2,
        second,
        second_t,
        hidden,
        hidden_t,
        pre_low,
        slope,
        incoming,
        middle_low,
        vec_grad,
    ) = acts
    joined, middle_grad, head_grad = qkv, hat2, normed
    exchange, (lines, vec, up_bias, line_grad, line_a, line_b) = extra[:4], extra[4:]
    (
        in_sem,
        own_sem,
        ring_s,
        ring_r,
        row_s,
        row_r,
        core_s,
        core_r,
        line_s,
        line_r,
        give_s,
        give_r,
        over_s,
        over_r,
        sum_s,
        sum_r,
        end_s,
        end_r,
        tail_s,
        tail_r,
        pair_s,
        pair_r,
    ) = sems[:22]
    line_pair = sems[22]
    pre_bias, score_rows = sems[23], sems[24]

    rows = qkv_in.shape[0]
    height = [ref.shape[0] for ref in (qkv_in, out_in, up_in, down_in)]
    sixth = [ref.shape[1] // 6 for ref in (qkv_in, out_in, up_in, down_in)]
    matrix_in = (qkv_in, out_in, up_in, down_in)
    hidden_units = up_in.shape[1]
    reach = (n // 2, n // 2 - 1)

    rep = lax.axis_index("rep")
    me = lax.axis_index("shard")
    core = rep % 2
    row = rep // 2
    position = ring_position(me, n)
    sign = 1 - 2 * core

    def at(k):
        return ring_index((position + sign * k + n) % n, n)

    peers = ((rep, at(1)), (rep, at(-1)))
    partner = (row * 2 + 1 - core, me)
    across = ((1 - row) * 2 + core, me)
    third = (2, row, 1 - row)

    def block(m, b):
        return pl.ds(pl.multiple_of(b * height[m], height[m]), height[m])

    def columns(m, slot, whose):
        width = sixth[m]
        return pl.ds(pl.multiple_of((2 * third[slot] + whose) * width, width), width)

    def piece(m, b, slot):
        return weights[m].at[block(m, b), columns(m, slot, core)]

    def came(d, h):
        return at(-1 - h) if d == 0 else at(1 + h)

    def own_copy(m, slot):
        return pltpu.make_async_copy(
            matrix_in[m].at[:, columns(m, slot, core)], piece(m, me, slot), own_sem.at[m, slot]
        )

    def gather_send(m, slot, d, h):
        view = piece(m, at(-h) if d == 0 else at(h), slot)
        return remote(view, view, ring_s.at[m, slot, d, h], ring_r.at[m, slot, d, h], peers[d])

    def gather_row(m, d, h, slot):
        view = piece(m, came(d, h), slot)
        k = d * reach[0] + h
        return remote(view, view, row_s.at[m, k], row_r.at[m, k], across)

    def gather_core(m, slot, whose):
        view = weights[m].at[:, columns(m, slot, whose)]
        return remote(view, view, core_s.at[m, slot], core_r.at[m, slot], partner)

    def gather_start(m):
        for slot in (MINE, SHARED):
            for d in (0, 1):
                gather_send(m, slot, d, 0).start()

    def gather_hop(m, h, slots=(MINE, SHARED)):
        for slot in slots:
            for d in (0, 1):
                if h < reach[d]:
                    view = piece(m, came(d, h), slot)
                    remote(
                        view, view, ring_s.at[m, slot, d, h], ring_r.at[m, slot, d, h], peers[d]
                    ).wait_recv()
                    if h + 1 < reach[d]:
                        gather_send(m, slot, d, h + 1).start()
                    if slot == MINE:
                        gather_row(m, d, h, MINE).start()

    def gather_relay(m):
        for slot in (MINE, SHARED):
            gather_core(m, slot, core).start()

    def gather_rows(m):
        for d in (0, 1):
            for h in range(reach[d]):
                gather_row(m, d, h, YOURS).wait_recv()
        gather_core(m, YOURS, core).start()

    def gather_end(m):
        for slot in (MINE, SHARED, YOURS):
            gather_core(m, slot, 1 - core).wait_recv()

    def line_send(d, h):
        view = lines.at[at(-h) if d == 0 else at(h)]
        return remote(view, view, line_s.at[d, h], line_r.at[d, h], peers[d])

    def line_hop(h):
        for d in (0, 1):
            if h < reach[d]:
                view = lines.at[came(d, h)]
                remote(view, view, line_s.at[d, h], line_r.at[d, h], peers[d]).wait_recv()
                if h + 1 < reach[d]:
                    line_send(d, h + 1).start()

    def slots_of(m):
        return (SHARED, MINE) if m in over else (SHARED, MINE, YOURS)

    def owner(d, t):
        return at(reach[0] - t) if d == 0 else at(t - reach[1])

    def give(m, slot):
        return remote(
            halves[m].at[1, slot],
            given[m].at[slot],
            give_s.at[m, slot],
            give_r.at[m, slot],
            partner,
        )

    def hand_over(m, d, t):
        rows_of = block(m, owner(d, t))
        return remote(
            halves[m].at[0, YOURS, rows_of],
            over[m].at[rows_of],
            over_s.at[m, d, t],
            over_r.at[m, d, t],
            across,
        )

    def local(m, slot, b):
        total = halves[m][0, slot, block(m, b)].astype(F32) + given[m][slot, block(m, b)].astype(
            F32
        )
        if slot == MINE and m in over:
            total = total + over[m][block(m, b)].astype(F32)
        return total

    def ring_sum(m, slot, d, t):
        return remote(
            halves[m].at[0, slot, block(m, owner(d, t))],
            (arrive_a, arrive_b)[d][m].at[slot, t],
            sum_s.at[m, slot, d, t],
            sum_r.at[m, slot, d, t],
            peers[d],
        )

    def over_steps():
        return [(d, t) for t in range(reach[0] + 1) for d in (0, 1) if t < reach[d] + 1 - d]

    def reduce_over(m, p):
        if p == 0:
            give(m, YOURS).wait_recv()
        for d, t in over_steps():
            if min(t * 4 // reach[0], 3) == p:
                rows_of = block(m, owner(d, t))
                halves[m][0, YOURS, rows_of] = local(m, YOURS, owner(d, t)).astype(LOW)
                hand_over(m, d, t).start()

    def reduce_step(m, slot, t):
        if t == 0:
            give(m, slot).wait_recv()
        for d in (0, 1):
            if t < reach[d]:
                b = owner(d, t)
                if slot == MINE and m in over:
                    hand_over(m, d, t).wait_recv()
                total = local(m, slot, b)
                if t > 0:
                    ring_sum(m, slot, d, t - 1).wait_recv()
                    total = total + (arrive_a, arrive_b)[d][m][slot, t - 1].astype(F32)
                halves[m][0, slot, block(m, b)] = total.astype(LOW)
                ring_sum(m, slot, d, t).start()

    def sum_columns(m, slot, whose):
        width = sixth[m]
        which = third[slot] if m in over else (2, 0, 1)[slot]
        return pl.ds(pl.multiple_of((2 * which + whose) * width, width), width)

    def end_view(m, slot, whose):
        return sums[m].at[:, sum_columns(m, slot, whose)]

    def end_core(m, slot, whose):
        view = end_view(m, slot, whose)
        return remote(view, view, end_s.at[m, slot, 1], end_r.at[m, slot, 1], partner)

    def end_row(m, slot):
        return remote(
            halves[m].at[0, slot, block(m, me)],
            exchange[m].at[slot],
            end_s.at[m, slot, 0],
            end_r.at[m, slot, 0],
            across,
        )

    def end_other(m, slot):
        view = end_view(m, slot, core)
        return remote(view, view, end_s.at[m, MINE, 0], end_r.at[m, MINE, 0], across)

    def reduce_end(m, slot):
        if slot == MINE and m in over:
            hand_over(m, 0, reach[0]).wait_recv()
        total = local(m, slot, me)
        for d in (0, 1):
            if reach[d]:
                ring_sum(m, slot, d, reach[d] - 1).wait_recv()
                total = total + (arrive_a, arrive_b)[d][m][slot, reach[d] - 1].astype(F32)
        if slot == MINE and m in over:
            sums[m][:, sum_columns(m, MINE, core)] = total.astype(LOW)
            end_other(m, MINE).start()
            end_core(m, MINE, core).start()
        else:
            halves[m][0, slot, block(m, me)] = total.astype(LOW)
            end_row(m, slot).start()

    def reduce_exchange(m):
        for slot in slots_of(m):
            if slot == MINE and m in over:
                end_other(m, YOURS).wait_recv()
                end_core(m, YOURS, core).start()
            else:
                end_row(m, slot).wait_recv()
                total = halves[m][0, slot, block(m, me)].astype(F32) + exchange[m][slot].astype(F32)
                sums[m][:, sum_columns(m, slot, core)] = total.astype(LOW)
                end_core(m, slot, core).start()

    def reduce_finish(m):
        for slot in (SHARED, MINE, YOURS):
            end_core(m, slot, 1 - core).wait_recv()

    steps = padded // 16
    slices = [pl.ds(i * 16, 16) for i in range(steps)]
    gain = lambda i: vec[i : i + 1, :]
    live = live_in[0].astype(F32)
    row_id = lax.broadcasted_iota(jnp.int32, (padded, 1), 0)
    row_mask = (row_id < length).astype(F32)
    pair_width = 2 * HEAD_DIM
    pairs = model // pair_width

    def normalise(source, hat, inv):
        for s in slices:
            values = source[s, :]
            centred = values - jnp.mean(values, axis=-1, keepdims=True)
            spread = jnp.mean(centred * centred, axis=-1, keepdims=True)
            inv_std = lax.rsqrt(spread + NORM_EPS)
            hat[s, :] = centred * inv_std
            inv[s, :] = jnp.broadcast_to(inv_std, (16, LANES))

    def scale_shift(hat, low, g, b, mask):
        for i, s in enumerate(slices):
            value = hat[s, :] * gain(g) + gain(b)
            if mask and (i + 1) * 16 > length:
                value = value * row_mask[i * 16 : (i + 1) * 16]
            low[s, :] = value.astype(LOW)

    def transpose(source, target):
        def body(i, carry):
            cols = pl.ds(pl.multiple_of(i * 256, 256), 256)
            target[cols, :] = source[:, cols].T
            return carry

        lax.fori_loop(0, source.shape[1] // 256, body, 0)

    def begin():
        middle[...] = jnp.zeros_like(middle)
        middle[:length, :] = x_low[0].astype(F32)
        incoming[...] = jnp.zeros_like(incoming)
        incoming[:length, :] = cot_low[0].astype(F32) * live
        upstream[...] = incoming[...].astype(LOW)
        vec_grad[...] = jnp.zeros_like(vec_grad)
        vec_grad[7:8, :] = jnp.sum(incoming[...], axis=0, keepdims=True)
        normalise(middle, hat1, inv1)

    def vectors():
        for b in range(n):
            held = lines[b]
            vec[:, b * rows : (b + 1) * rows] = held[:, :rows]
            for e in range(4 * rows // LANES):
                first = b * 4 * rows + e * LANES
                up_bias[:, first : first + LANES] = jnp.broadcast_to(
                    held[8 + e : 9 + e, :], (8, LANES)
                )

    def first_norm():
        scale_shift(hat1, normed, 0, 1, True)
        transpose(normed, normed_t)
        zero = jnp.zeros((1, model), F32)
        for k, v in enumerate((vec[2:3, :], zero, vec[3:4, :])):
            pre_bias[:, k * model : (k + 1) * model] = jnp.broadcast_to(v, (8, model))

    def project(first, last):
        wide = 2 * sixth[QKV] // 2

        def body(c, carry):
            cols = pl.ds(pl.multiple_of(c * wide, wide), wide)
            value = (dot_nn(normed[...], weights[QKV][:, cols]) + pre_bias[0:1, cols]) * row_mask
            factor = jnp.where(c * wide < model, HEAD_DIM**-0.5, 1.0)
            qkv[:, cols] = (value.astype(LOW).astype(F32) * factor).astype(LOW)
            return carry

        lax.fori_loop(first, last, body, 0)

    lane = lax.broadcasted_iota(jnp.int32, (padded, pair_width), 1)
    low_lane = lane < HEAD_DIM
    key_mask = lax.broadcasted_iota(jnp.int32, (1, padded), 1) < length

    def heads(part, p):
        return qkv[:, pl.ds(pl.multiple_of(part * model + p * pair_width, LANES), pair_width)]

    def stacked(value, target):
        wide = value.astype(F32)
        target[:padded, :] = jnp.where(low_lane, wide, 0.0).astype(LOW)
        target[padded:, :] = jnp.where(low_lane, 0.0, wide).astype(LOW)

    def merged(value):
        return jnp.where(low_lane, value[:padded], value[padded:])

    def attend(first, last):
        def body(p, carry):
            stacked(heads(0, p), score_rows.at[0])
            scores = dot_nt(score_rows[0], heads(1, p))
            powers = jnp.where(key_mask, jnp.exp(scores), 0.0)
            total = jnp.sum(powers, axis=-1, keepdims=True)
            weight = (powers * (1.0 / total)).astype(LOW)
            probs[p] = weight
            cols = pl.ds(pl.multiple_of(p * pair_width, LANES), pair_width)
            attended[:, cols] = merged(dot_nn(weight, heads(2, p))).astype(LOW)
            return carry

        lax.fori_loop(first, last, body, 0)

    def mix():
        def body(c, carry):
            cols = pl.ds(pl.multiple_of(c * 256, 256), 256)
            middle[:, cols] = (
                middle[:, cols] + dot_nn(attended[...], weights[OUT][:, cols]) + vec[4:5, cols]
            )
            return carry

        lax.fori_loop(0, model // 256, body, 0)
        normalise(middle, hat2, inv2)
        scale_shift(hat2, second, 5, 6, False)

    def transposes():
        transpose(attended, attended_t)
        transpose(second, second_t)

    wide_hidden = 512

    def expand(first, last):
        def body(c, carry):
            cols = pl.ds(pl.multiple_of(c * wide_hidden, wide_hidden), wide_hidden)
            pre = dot_nn(second[...], weights[UP][:, cols]) + up_bias[0:1, cols]
            cdf = 0.5 * (1.0 + lax.erf(pre * ROOT_HALF))
            density = jnp.exp(-0.5 * pre * pre) * DENSITY_COEF
            value = (pre * cdf).astype(LOW)
            hidden[:, cols] = value
            slope[:, cols] = cdf + pre * density
            hidden_t[cols, :] = value.T
            return carry

        lax.fori_loop(first, last, body, 0)

    def contract():
        def body(c, carry):
            cols = pl.ds(pl.multiple_of(c * 256, 256), 256)
            value = dot_nn(hidden[...], weights[DOWN][:, cols]) + vec[7:8, cols]
            value = (middle[:, cols] + value) * live
            output_low[:, cols] = value.astype(LOW)
            return carry

        lax.fori_loop(0, model // 256, body, 0)

    def gradient(m, left, right, slot):
        width = sixth[m]
        base = (third[slot] if m in over else (2, 0, 1)[slot]) * 2 * width
        if width % 256 == 0:
            count, step = 2 * width // 256, 256
        elif (2 * width) % 256 == 0 and width < 256:
            count, step = 1, 2 * width
        else:
            count, step = 2, width
        tall = left.shape[0]
        high = min(tall, model)

        def body(i, carry):
            c, r = i % count, i // count
            cols = pl.ds(pl.multiple_of(base + c * step, LANES), step)
            down = pl.ds(pl.multiple_of(r * high, high), high)
            value = dot_nn(left[down, :], right[:, cols]).astype(LOW)
            if step > width:
                for whose in range(2):
                    halves[m][(whose + core) % 2, slot, down] = value[
                        :, whose * width : (whose + 1) * width
                    ]
            else:
                per = width // step
                start = pl.multiple_of((c % per) * step, LANES)
                halves[m][(c // per + core) % 2, slot, down, pl.ds(start, step)] = value
            return carry

        lax.fori_loop(0, count * (tall // high), body, 0)
        give(m, slot).start()

    def hidden_back(first, last):
        def body(c, carry):
            cols = pl.ds(pl.multiple_of(c * wide_hidden, wide_hidden), wide_hidden)
            value = dot_nt(upstream[...], weights[DOWN][cols, :]) * slope[:, cols]
            up_bias[:, cols] = jnp.broadcast_to(
                jnp.sum(value, axis=0, keepdims=True), (8, wide_hidden)
            )
            pre_low[:, cols] = value.astype(LOW)
            return carry

        lax.fori_loop(first, last, body, 0)

    def second_back():
        def body(c, carry):
            cols = pl.ds(pl.multiple_of(c * 256, 256), 256)
            incoming[:, cols] = dot_nt(pre_low[...], weights[UP][cols, :])
            return carry

        lax.fori_loop(0, model // 256, body, 0)

    def norm_back(hat, inv, g, add):
        gain_sum = jnp.zeros((1, model), F32)
        bias_sum = jnp.zeros((1, model), F32)
        add_sum = jnp.zeros((1, model), F32)
        for s in slices:
            came_in = incoming[s, :]
            hat_vals = hat[s, :]
            scaled = came_in * gain(g)
            average = jnp.mean(scaled, axis=-1, keepdims=True)
            along = jnp.mean(scaled * hat_vals, axis=-1, keepdims=True)
            value = add[s, :].astype(F32) + inv[s, 0:1] * (scaled - average - hat_vals * along)
            gain_sum += jnp.sum(came_in * hat_vals, axis=0, keepdims=True)
            bias_sum += jnp.sum(came_in, axis=0, keepdims=True)
            add_sum += jnp.sum(value, axis=0, keepdims=True)
            middle_grad[s, :] = value
            middle_low[s, :] = value.astype(LOW)
        vec_grad[g : g + 1, :] = gain_sum
        vec_grad[g + 1 : g + 2, :] = bias_sum
        return add_sum

    def attended_back():
        def body(c, carry):
            cols = pl.ds(pl.multiple_of(c * 256, 256), 256)
            head_grad[:, cols] = dot_nt(middle_low[...], weights[OUT][cols, :]).astype(LOW)
            return carry

        lax.fori_loop(0, model // 256, body, 0)

    def attend_back(first, last):
        def body(p, carry):
            start = pl.multiple_of(p * pair_width, LANES)
            cols = pl.ds(start, pair_width)
            stacked(head_grad[:, cols], score_rows.at[1])
            stacked(heads(0, p), score_rows.at[0])
            weight = probs[p]
            value_grad = dot_tn(weight, score_rows[1])
            prob_grad = dot_nt(score_rows[1], heads(2, p))
            wide = weight.astype(F32)
            along = jnp.sum(wide * prob_grad, axis=-1, keepdims=True)
            score_grad = (wide * (prob_grad - along)).astype(LOW)
            query_grad = merged(dot_nn(score_grad, heads(1, p))) * HEAD_DIM**-0.5
            key_grad = dot_tn(score_grad, score_rows[0])
            vec_grad[2:3, cols] = jnp.sum(query_grad, axis=0, keepdims=True)
            vec_grad[3:4, cols] = jnp.sum(value_grad, axis=0, keepdims=True)
            for k, value in enumerate((query_grad, key_grad, value_grad)):
                joined[:, pl.ds(pl.multiple_of(k * model + start, LANES), pair_width)] = (
                    value.astype(LOW)
                )
            return carry

        lax.fori_loop(first, last, body, 0)

    def first_back():
        def body(c, carry):
            cols = pl.ds(pl.multiple_of(c * 256, 256), 256)
            incoming[:, cols] = dot_nt(joined[...], weights[QKV][cols, :])
            return carry

        lax.fori_loop(0, model // 256, body, 0)

    def tail_local():
        line_grad[...] = jnp.zeros_like(line_grad)
        for b in range(n):
            line_grad[b, 0:8, 0:rows] = vec_grad[0:8, b * rows : (b + 1) * rows]
            for e in range(4 * rows // LANES):
                first = b * 4 * rows + e * LANES
                line_grad[b, 8 + e : 9 + e, :] = up_bias[0:1, first : first + LANES]

    def tail_sum(d, t):
        b = at(reach[0] - t) if d == 0 else at(t - reach[1])
        arrive = (line_a, line_b)[d]
        return remote(line_grad.at[b], arrive.at[t], tail_s.at[d, t], tail_r.at[d, t], peers[d])

    def tail_step(t):
        for d in (0, 1):
            if t < reach[d]:
                b = at(reach[0] - t) if d == 0 else at(t - reach[1])
                if t > 0:
                    tail_sum(d, t - 1).wait_recv()
                    line_grad[b] = line_grad[b] + (line_a, line_b)[d][t - 1]
                tail_sum(d, t).start()

    def pair_copy(k, peer):
        return remote(
            line_pair.at[2 * k], line_pair.at[2 * k + 1], pair_s.at[k], pair_r.at[k], peer
        )

    def tail_end():
        total = line_grad[me]
        for d in (0, 1):
            if reach[d]:
                tail_sum(d, reach[d] - 1).wait_recv()
                total = total + (line_a, line_b)[d][reach[d] - 1]
        line_pair[0] = total
        pair_copy(0, across).start()

    def tail_pair():
        pair_copy(0, across).wait_recv()
        line_pair[2] = line_pair[0] + line_pair[1]
        pair_copy(1, partner).start()

    def tail_finish():
        pair_copy(1, partner).wait_recv()
        line_wide[...] = line_pair[2] + line_pair[3]
        high = line_wide[...].astype(LOW)
        line_low[:, :LANES] = high
        line_low[:, LANES:] = (line_wide[...] - high.astype(F32)).astype(LOW)

    layout = pack_layout(rows, padded, model)

    def pack_copies(name):
        source = {"c": output_low, "fn": input_grad_low, "tf": line_low}.get(name)
        if source is None:
            source = sums["QOUD".index(name[1])]
        copies = []
        for i, (key, first, high, left, width) in enumerate(layout):
            if key == name:
                target = packed.at[pl.ds(first, high), pl.ds(0, width)]
                view = source.at[:, pl.ds(left, width)]
                copies.append(pltpu.make_async_copy(view, target, pack_sem.at[i]))
        return copies

    x_copy = pltpu.make_async_copy(x_in, x_low, in_sem.at[1])
    cot_copy = pltpu.make_async_copy(cot_in, cot_low, in_sem.at[2])
    for m in range(4):
        for slot in (MINE, SHARED, YOURS):
            own_copy(m, slot).start()
    x_copy.start()
    cot_copy.start()

    lines[me] = jnp.zeros_like(lines[me])
    for i, ref in zip(VECTOR_ROWS, vectors_in):
        if i < 8:
            lines[me, i, 0:rows] = ref[...].astype(F32)
        else:
            for e in range(4 * rows // LANES):
                lines[me, i + e, :] = ref[pl.ds(e * LANES, LANES)].astype(F32)

    barrier = pltpu.get_barrier_semaphore()
    for peer in (*peers, partner, across):
        pl.semaphore_signal(barrier, inc=1, device_id=peer, device_id_type=MESH)
    pl.semaphore_wait(barrier, 4)

    for d in (0, 1):
        line_send(d, 0).start()
    for slot in (MINE, SHARED, YOURS):
        own_copy(QKV, slot).wait()
    gather_start(QKV)
    for m in (OUT, UP, DOWN):
        for slot in (MINE, SHARED, YOURS):
            own_copy(m, slot).wait()
    x_copy.wait()
    cot_copy.wait()
    begin()

    def part(total, p):
        return range(total * p // 4, total * (p + 1) // 4)

    def hops(m, p):
        for h in part(reach[0], p):
            gather_hop(m, h)

    def steps_of(m, slot, p):
        for t in part(reach[0], p):
            reduce_step(m, slot, t)

    def lines_of(p):
        for h in part(reach[0], p):
            line_hop(h)

    def tails_of(p):
        for t in part(reach[0], p):
            tail_step(t)

    def first_norm_back():
        norm_back(hat1, inv1, 0, middle_grad)
        input_grad_low[...] = middle_grad[...].astype(LOW)
        tail_local()

    def second_norm_back():
        vec_grad[4:5, :] = norm_back(hat2, inv2, 5, upstream)

    chunks = hidden_units // wide_hidden
    sides = {QKV: (normed_t, joined), OUT: (attended_t, middle_low)}
    sides |= {UP: (second_t, pre_low), DOWN: (hidden_t, upstream)}
    actions = {
        "v": lambda: (vectors(), first_norm()),
        "p": lambda: project(0, 6),
        "a0": lambda: attend(0, pairs // 2),
        "a1": lambda: attend(pairs // 2, pairs),
        "m": mix,
        "t": transposes,
        "u0": lambda: expand(0, chunks // 2),
        "u1": lambda: expand(chunks // 2, chunks),
        "c": contract,
        "hb0": lambda: hidden_back(0, chunks // 2),
        "hb1": lambda: hidden_back(chunks // 2, chunks),
        "sb": second_back,
        "nb": second_norm_back,
        "ob": attended_back,
        "ab0": lambda: attend_back(0, pairs // 2),
        "ab1": lambda: attend_back(pairs // 2, pairs),
        "fb": first_back,
        "fn": first_norm_back,
        "te": tail_end,
        "tp": tail_pair,
        "tf": tail_finish,
    }
    for p in range(4):
        actions[f"l{p}"] = functools.partial(lines_of, p)
        actions[f"t{p}"] = functools.partial(tails_of, p)
    for name, m in (("Q", QKV), ("O", OUT), ("U", UP), ("D", DOWN)):
        actions["G" + name] = functools.partial(gather_start, m)
        actions["R" + name] = functools.partial(gather_relay, m)
        actions["e" + name] = functools.partial(gather_rows, m)
        actions["E" + name] = functools.partial(gather_end, m)
        actions["X" + name] = functools.partial(reduce_exchange, m)
        actions["F" + name] = functools.partial(reduce_finish, m)
        for p in range(4):
            actions[f"g{name}{p}"] = functools.partial(hops, m, p)
            actions[f"o{name}{p}"] = functools.partial(reduce_over, m, p)
        for key, slot in (("s", SHARED), ("m", MINE), ("y", YOURS)):
            actions[f"d{name}{key}"] = functools.partial(gradient, m, *sides[m], slot)
            actions[f"{name}{key}"] = functools.partial(reduce_end, m, slot)
            for p in range(4):
                actions[f"{name}{key}{p}"] = functools.partial(steps_of, m, slot, p)
    for name in ORDER:
        actions[name]()
        for copy in pack_copies(name) if name in {entry[0] for entry in layout} else ():
            copy.start()

    for m in range(4):
        for slot in (SHARED, MINE, YOURS):
            gather_core(m, slot, core).wait_send()
            give(m, slot).wait_send()
            end_core(m, slot, core).wait_send()
        for slot in slots_of(m):
            if slot == MINE and m in over:
                end_other(m, MINE).wait_send()
            else:
                end_row(m, slot).wait_send()
        if m in over:
            for d, t in over_steps():
                hand_over(m, d, t).wait_send()
        for d in (0, 1):
            for h in range(reach[d]):
                gather_row(m, d, h, MINE).wait_send()
                for slot in (SHARED, MINE):
                    gather_send(m, slot, d, h).wait_send()
                for slot in slots_of(m):
                    ring_sum(m, slot, d, h).wait_send()
    for d in (0, 1):
        for h in range(reach[d]):
            line_send(d, h).wait_send()
            tail_sum(d, h).wait_send()
    pair_copy(0, across).wait_send()
    pair_copy(1, partner).wait_send()
    for name in ("c", "fn", "tf", "FQ", "FO", "FU", "FD"):
        for copy in pack_copies(name):
            copy.wait()


def run_layer(layer_input, cotangent, live, matrices, vectors, n):
    line = (16, LANES)
    images, length, model = layer_input.shape
    padded = -(-length // 16) * 16
    hidden_units = matrices[UP].shape[1]
    vmem, dma = pltpu.VMEM, pltpu.SemaphoreType.DMA
    reach = (n // 2, n // 2 - 1)
    height = [a.shape[0] for a in matrices]
    sixth = [a.shape[1] // 6 for a in matrices]
    pairs = model // (2 * HEAD_DIM)
    wide = (padded, model)
    scratch = [vmem((n * a.shape[0], a.shape[1]), LOW) for a in matrices]
    scratch += [
        vmem((1, length, model), LOW),
        vmem((1, length, model), LOW),
        vmem(wide, LOW),
        vmem(wide, F32),
        vmem((padded, LANES), F32),
        vmem(wide, LOW),
        vmem((model, padded), LOW),
        vmem((padded, 3 * model), LOW),
        vmem((pairs, 2 * padded, padded), LOW),
        vmem(wide, LOW),
        vmem((model, padded), LOW),
        vmem(wide, F32),
        vmem(wide, F32),
        vmem((padded, LANES), F32),
        vmem(wide, LOW),
        vmem((model, padded), LOW),
        vmem((padded, hidden_units), LOW),
        vmem((hidden_units, padded), LOW),
        vmem((padded, hidden_units), LOW),
        vmem((padded, hidden_units), F32),
        vmem(wide, F32),
        vmem(wide, LOW),
        vmem((16, model), F32),
    ]
    scratch += [vmem((2, 3, n * r, w), LOW) for r, w in zip(height, sixth)]
    scratch += [vmem((3, n * r, w), LOW) for r, w in zip(height, sixth)]
    slots = [3 - (m in CROSS) for m in range(4)]
    scratch += [vmem((n * height[m], sixth[m]), LOW) for m in CROSS]
    scratch += [vmem((k, reach[0], r, w), LOW) for k, r, w in zip(slots, height, sixth)]
    scratch += [vmem((k, max(reach[1], 1), r, w), LOW) for k, r, w in zip(slots, height, sixth)]
    scratch += [vmem((k - 1 + k // 3, r, w), LOW) for k, r, w in zip(slots, height, sixth)]
    scratch += [
        vmem((n,) + line, F32),
        vmem((16, model), F32),
        vmem((8, hidden_units), F32),
        vmem((n,) + line, F32),
        vmem((reach[0],) + line, F32),
        vmem((max(reach[1], 1),) + line, F32),
    ]
    scratch += [
        dma((3,)),
        dma((4, 3)),
        dma((4, 2, 2, reach[0])),
        dma((4, 2, 2, reach[0])),
        dma((4, n - 1)),
        dma((4, n - 1)),
        dma((4, 3)),
        dma((4, 3)),
        dma((2, reach[0])),
        dma((2, reach[0])),
        dma((4, 3)),
        dma((4, 3)),
        dma((4, 2, reach[0] + 1)),
        dma((4, 2, reach[0] + 1)),
        dma((4, 3, 2, reach[0])),
        dma((4, 3, 2, reach[0])),
        dma((4, 3, 2)),
        dma((4, 3, 2)),
        dma((2, reach[0])),
        dma((2, reach[0])),
        dma((2,)),
        dma((2,)),
        vmem((4,) + line, F32),
        vmem((8, 3 * model), F32),
        vmem((2, 2 * padded, 2 * HEAD_DIM), LOW),
    ]
    layout = pack_layout(matrices[QKV].shape[0], padded, model)
    scratch += [vmem(wide, LOW)] * 2 + [vmem(a.shape, LOW) for a in matrices]
    scratch += [vmem((16, 2 * LANES), LOW), vmem(line, F32), dma((len(layout),))]
    anywhere = pl.BlockSpec(memory_space=pl.ANY)
    near = pl.BlockSpec(memory_space=pltpu.VMEM)
    return pl.pallas_call(
        functools.partial(layer_kernel, n, length, padded, model),
        out_shape=jax.ShapeDtypeStruct((layout[-1][1] + layout[-1][2], model), LOW),
        in_specs=[anywhere] * 2 + [pl.BlockSpec(memory_space=pltpu.SMEM)] + [anywhere] * 4 + [near] * 9,
        out_specs=anywhere,
        scratch_shapes=scratch,
        compiler_params=pltpu.CompilerParams(
            collective_id=0, has_side_effects=True, vmem_limit_bytes=60 * 1024 * 1024
        ),
        name="layer",
    )(layer_input, cotangent, live, *matrices, *vectors)


norm_eps = 1e-06
root_half = 0.7071067811865476
density_coef = 0.3989422804014327


def matmul(operand, factor):
    flat = operand.reshape(-1, operand.shape[-1])
    product = jnp.dot(flat, factor, preferred_element_type=jnp.float32)
    return product.reshape(operand.shape[:-1] + (factor.shape[-1],))


def outer_product(operand, factor):
    return jnp.dot(
        operand.reshape(-1, operand.shape[-1]).T,
        factor.reshape(-1, factor.shape[-1]),
        preferred_element_type=jnp.float32,
    )


def batched(form, operand, factor):
    return jnp.einsum(form, operand, factor, preferred_element_type=jnp.float32)


def layer_norm(values, norm_gain, norm_bias):
    average = jnp.mean(values, axis=-1, keepdims=True)
    centred = values - average
    spread = jnp.mean(centred * centred, axis=-1, keepdims=True)
    inv_std = lax.rsqrt(spread + norm_eps)
    hat_vals = centred * inv_std
    return (
        hat_vals * norm_gain.astype(jnp.float32) + norm_bias.astype(jnp.float32),
        hat_vals,
        inv_std,
    )


def norm_back(incoming, hat_vals, inv_std, norm_gain):
    scaled = incoming * norm_gain.astype(jnp.float32)
    return inv_std * (
        scaled
        - jnp.mean(scaled, axis=-1, keepdims=True)
        - hat_vals * jnp.mean(scaled * hat_vals, axis=-1, keepdims=True)
    )


def forward_pass(params, layer_input, live):
    (
        first_gain,
        first_bias,
        qkv_weight,
        query_bias,
        value_bias,
        out_weight,
        out_bias,
        second_gain,
        second_bias,
        up_weight,
        up_bias,
        down_weight,
        down_bias,
    ) = params
    images, length, model_width = layer_input.shape
    head_count = model_width // HEAD_DIM
    score_scale = HEAD_DIM ** (-0.5)
    stream = layer_input.astype(jnp.float32)
    normed, first_hat, first_inv = layer_norm(stream, first_gain, first_bias)
    normed = normed.astype(jnp.bfloat16)
    projected = matmul(normed, qkv_weight)
    shape_heads = (images, length, head_count, HEAD_DIM)
    queries = (
        (projected[..., :model_width] + query_bias.astype(jnp.float32))
        .astype(jnp.bfloat16)
        .reshape(shape_heads)
    )
    key_rows = (
        projected[..., model_width : 2 * model_width].astype(jnp.bfloat16).reshape(shape_heads)
    )
    values = (
        (projected[..., 2 * model_width :] + value_bias.astype(jnp.float32))
        .astype(jnp.bfloat16)
        .reshape(shape_heads)
    )
    scores = batched("bqhd,bkhd->bhqk", queries, key_rows) * score_scale
    log_total = jnp.log(jnp.sum(jnp.exp(scores), axis=-1, keepdims=True))
    weights = jnp.exp(scores - log_total).astype(jnp.bfloat16)
    attended = (
        batched("bhqk,bkhd->bqhd", weights, values)
        .reshape(images, length, model_width)
        .astype(jnp.bfloat16)
    )
    middle = stream + matmul(attended, out_weight) + out_bias.astype(jnp.float32)
    second_normed, second_hat, second_inv = layer_norm(middle, second_gain, second_bias)
    second_normed = second_normed.astype(jnp.bfloat16)
    hidden_pre = matmul(second_normed, up_weight) + up_bias.astype(jnp.float32)
    normal_cdf = 0.5 * (1.0 + lax.erf(hidden_pre * root_half))
    hidden = (hidden_pre * normal_cdf).astype(jnp.bfloat16)
    result = middle + matmul(hidden, down_weight) + down_bias.astype(jnp.float32)
    image_mask = live.astype(jnp.float32)[:, None, None]
    output = (result * image_mask).astype(jnp.bfloat16)
    saved = (
        normed,
        first_hat,
        first_inv,
        queries,
        key_rows,
        values,
        log_total,
        attended,
        second_normed,
        second_hat,
        second_inv,
        hidden_pre,
        normal_cdf,
        hidden,
        image_mask,
    )
    return (output, saved)


def backward_pass(params, saved, cotangent):
    (
        first_gain,
        first_bias,
        qkv_weight,
        query_bias,
        value_bias,
        out_weight,
        out_bias,
        second_gain,
        second_bias,
        up_weight,
        up_bias,
        down_weight,
        down_bias,
    ) = params
    (
        normed,
        first_hat,
        first_inv,
        queries,
        key_rows,
        values,
        log_total,
        attended,
        second_normed,
        second_hat,
        second_inv,
        hidden_pre,
        normal_cdf,
        hidden,
        image_mask,
    ) = saved
    images, length, head_count, head_width = queries.shape
    flat_shape = (images, length, head_count * head_width)
    score_scale = HEAD_DIM ** (-0.5)
    upstream = cotangent.astype(jnp.float32) * image_mask
    upstream_low = upstream.astype(jnp.bfloat16)
    down_weight_grad = outer_product(hidden, upstream_low)
    down_bias_grad = jnp.sum(upstream, axis=(0, 1))
    hidden_grad = matmul(upstream_low, down_weight.T)
    density = jnp.exp(-0.5 * hidden_pre * hidden_pre) * density_coef
    pre_grad = hidden_grad * (normal_cdf + hidden_pre * density)
    pre_low = pre_grad.astype(jnp.bfloat16)
    up_weight_grad = outer_product(second_normed, pre_low)
    up_bias_grad = jnp.sum(pre_grad, axis=(0, 1))
    second_in = matmul(pre_low, up_weight.T)
    second_gain_grad = jnp.sum(second_in * second_hat, axis=(0, 1))
    second_bias_grad = jnp.sum(second_in, axis=(0, 1))
    middle_grad = upstream + norm_back(second_in, second_hat, second_inv, second_gain)
    middle_low = middle_grad.astype(jnp.bfloat16)
    out_weight_grad = outer_product(attended, middle_low)
    out_bias_grad = jnp.sum(middle_grad, axis=(0, 1))
    attended_grad = matmul(middle_low, out_weight.T).astype(jnp.bfloat16).reshape(queries.shape)
    again_scores = batched("bqhd,bkhd->bhqk", queries, key_rows) * score_scale
    probs = jnp.exp(again_scores - log_total)
    probs_low = probs.astype(jnp.bfloat16)
    value_grad = batched("bhqk,bqhd->bkhd", probs_low, attended_grad)
    prob_grad = batched("bqhd,bkhd->bhqk", attended_grad, values)
    score_grad = (
        probs * (prob_grad - jnp.sum(probs * prob_grad, axis=-1, keepdims=True)) * score_scale
    ).astype(jnp.bfloat16)
    query_grad = batched("bhqk,bkhd->bqhd", score_grad, key_rows).reshape(flat_shape)
    key_grad = batched("bhqk,bqhd->bkhd", score_grad, queries).reshape(flat_shape)
    value_grad = value_grad.reshape(flat_shape)
    joined = jnp.concatenate([query_grad, key_grad, value_grad], axis=-1).astype(jnp.bfloat16)
    qkv_weight_grad = outer_product(normed, joined)
    query_bias_grad = jnp.sum(query_grad, axis=(0, 1))
    value_bias_grad = jnp.sum(value_grad, axis=(0, 1))
    first_in = matmul(joined, qkv_weight.T)
    first_gain_grad = jnp.sum(first_in * first_hat, axis=(0, 1))
    first_bias_grad = jnp.sum(first_in, axis=(0, 1))
    middle_grad = middle_grad + norm_back(first_in, first_hat, first_inv, first_gain)
    input_grad = middle_grad.astype(jnp.bfloat16)
    grads = (
        first_gain_grad,
        first_bias_grad,
        qkv_weight_grad,
        query_bias_grad,
        value_bias_grad,
        out_weight_grad,
        out_bias_grad,
        second_gain_grad,
        second_bias_grad,
        up_weight_grad,
        up_bias_grad,
        down_weight_grad,
        down_bias_grad,
    )
    return (input_grad, grads)


def places(n):
    rep = lax.axis_index("rep")
    me = lax.axis_index("shard")
    core = rep % 2
    row = rep // 2
    position = ring_position(me, n)
    right = (rep, ring_index((position + 1) % n, n))
    left = (rep, ring_index((position + n - 1) % n, n))
    partner = (row * 2 + 1 - core, me)
    across = ((1 - row) * 2 + core, me)
    return me, core, row, position, right, left, partner, across


def greet(peers):
    barrier = pltpu.get_barrier_semaphore()
    for peer in peers:
        pl.semaphore_signal(barrier, inc=1, device_id=peer, device_id_type=MESH)
    pl.semaphore_wait(barrier, len(peers))


def remote(source, target, send, recv, device):
    return pltpu.make_async_remote_copy(
        src_ref=source,
        dst_ref=target,
        send_sem=send,
        recv_sem=recv,
        device_id=device,
        device_id_type=MESH,
    )


def window(refs, side, part, block, width):
    qkv, out, up, down = refs
    if side == 2:
        return [(None, down.at[block, part])]
    if side == 1:
        return [(None, up.at[block, :, pl.ds(pl.multiple_of(part * width, width), width)])]
    inner = part - part // 3
    return [
        (part < 3, qkv.at[block, :, pl.ds(pl.multiple_of(inner * width, width), width)]),
        (part == 3, out.at[block]),
    ]


def start_each(views, make):
    for condition, view in views:
        if condition is None:
            make(view).start()
        else:
            pl.when(condition)(make(view).start)


def gather_kernel(
    n,
    width,
    qkv_in,
    out_in,
    up_in,
    down_in,
    line_in,
    qkv_ref,
    out_ref,
    up_ref,
    down_ref,
    line_ref,
    local_sem,
    ring_s,
    ring_r,
    core_s,
    core_r,
    row_s,
    row_r,
    last_s,
    last_r,
    line_s,
    line_r,
):
    me, core, row, position, right, left, partner, across = places(n)
    refs = (qkv_ref, out_ref, up_ref, down_ref)
    pairs = zip((qkv_in, out_in, up_in, down_in, line_in), refs + (line_ref,))
    locals_ = [
        pltpu.make_async_copy(source, target.at[me], local_sem.at[i])
        for i, (source, target) in enumerate(pairs)
    ]
    for copy in locals_:
        copy.start()
    greet((right, left, partner, across))
    for copy in locals_:
        copy.wait()

    def block(way, r):
        return ring_index((position + (1 if way else n - 1) * r) % n, n)

    def views(i, r, whose):
        way, kind = i // 2, i % 2
        side, part = (2, 2 * whose + way) if kind else (way, 2 * whose + row)
        return window(refs, side, part, block(way, r), width)

    def over(way, r, whose):
        return window(refs, way, 2 * whose + 1 - row, block(way, r), width)

    def ring(i, r):
        peer = left if i // 2 else right
        return lambda v: remote(v, v, ring_s.at[i, r], ring_r.at[i, r], peer)

    def to_core(i, r):
        return lambda v: remote(v, v, core_s.at[i, r], core_r.at[i, r], partner)

    def to_row(way, r):
        return lambda v: remote(v, v, row_s.at[way, r], row_r.at[way, r], across)

    def to_last(way, r):
        return lambda v: remote(v, v, last_s.at[way, r], last_r.at[way, r], partner)

    def line(r):
        view = line_ref.at[block(0, r)]
        return remote(view, view, line_s.at[r], line_r.at[r], right)

    def one(vs):
        return vs[0][1]

    for i in range(4):
        start_each(views(i, 0, core), ring(i, 0))
    line(0).start()

    def relay(r):
        for way in range(2):
            to_row(way, r)(one(over(way, r + 1, core))).wait_recv()
            start_each(over(way, r + 1, core), to_last(way, r))

    def step(r, carry):
        for i in (0, 2, 1, 3):
            got = views(i, r + 1, core)
            ring(i, r)(one(got)).wait_recv()

            @pl.when(r < n - 2)
            def _():
                start_each(got, ring(i, r + 1))

            if i % 2 == 0:
                start_each(got, to_row(i // 2, r))
            start_each(got, to_core(i, r))
        line(r).wait_recv()

        @pl.when(r < n - 2)
        def _():
            line(r + 1).start()

        @pl.when(r > 0)
        def _():
            relay(r - 1)

        return carry

    lax.fori_loop(0, n - 1, step, 0)
    relay(n - 2)

    def finish(r, carry):
        for i in range(4):
            view = one(views(i, r, core))
            ring(i, r)(view).wait_send()
            to_core(i, r)(view).wait_send()
            to_core(i, r)(view).wait_recv()
        for way in range(2):
            view = one(views(2 * way, r, core))
            to_row(way, r)(view).wait_send()
            to_last(way, r)(view).wait_send()
            to_last(way, r)(view).wait_recv()
        line(r).wait_send()
        return carry

    lax.fori_loop(0, n - 1, finish, 0)


def gather_all(arrays, n, width):
    dma = pltpu.SemaphoreType.DMA
    return pl.pallas_call(
        functools.partial(gather_kernel, n, width),
        out_shape=[jax.ShapeDtypeStruct((n,) + a.shape, a.dtype) for a in arrays],
        in_specs=[pl.BlockSpec(memory_space=pltpu.VMEM)] * len(arrays),
        out_specs=[pl.BlockSpec(memory_space=pl.ANY)] * len(arrays),
        scratch_shapes=[dma((len(arrays),))]
        + [dma((4, n - 1))] * 4
        + [dma((2, n - 1))] * 4
        + [dma((n - 1,))] * 2,
        compiler_params=pltpu.CompilerParams(collective_id=0, has_side_effects=True),
        name="gather_all",
    )(*arrays)


def reduce_kernel(
    n,
    width,
    qkv_ref,
    out_ref,
    up_ref,
    down_ref,
    line_ref,
    sums,
    line_out,
    own,
    given,
    arrive,
    over,
    other,
    line_send,
    line_got,
    line_pair,
    own_sem,
    given_s,
    given_r,
    ring_s,
    ring_r,
    row_s,
    row_r,
    end_row_s,
    end_row_r,
    end_core_s,
    end_core_r,
    line_s,
    line_r,
    pair_s,
    pair_r,
):
    me, core, row, position, right, left, partner, across = places(n)
    refs = (qkv_ref, out_ref, up_ref, down_ref)
    f32 = jnp.float32

    def block(way, k):
        return ring_index((position + (1 if way else n - 1) * (k + 1)) % n, n)

    def source(i, k, whose):
        way, kind = i % 2, i // 2
        side, part = (
            (way, 2 * whose + row),
            (2, 2 * whose + way),
            (way, 2 * whose + 1 - row),
        )[kind]
        return window(refs, side, part, block(way, k), width)

    def load(i, k):
        return lambda v: pltpu.make_async_copy(v, own.at[i, k], own_sem.at[i, k])

    def give(i, k):
        return lambda v: remote(v, given.at[i, k], given_s.at[i, k], given_r.at[i, k], partner)

    def ring(i, k):
        peer = left if i % 2 else right
        return remote(own.at[i, k], arrive.at[i, k], ring_s.at[i, k], ring_r.at[i, k], peer)

    def to_row(way, k):
        return remote(
            own.at[4 + way, k], over.at[way, k], row_s.at[way, k], row_r.at[way, k], across
        )

    def line_ring(k):
        return remote(line_send.at[k], line_got.at[k], line_s.at[k], line_r.at[k], right)

    order = (4, 5, 2, 3, 0, 1)

    def loads(k, carry):
        for i in order:
            start_each(source(i, k, core), load(i, k))
        return carry

    lax.fori_loop(0, n, loads, 0)
    greet((right, left, partner, across))

    def gives(k, carry):
        for i in order:
            start_each(source(i, k, 1 - core), give(i, k))
        return carry

    lax.fori_loop(0, n, gives, 0)

    def take(i, k):
        view = source(i, k, core)[0][1]
        load(i, k)(view).wait()
        give(i, k)(view).wait_recv()
        return own[i, k].astype(f32) + given[i, k].astype(f32)

    def put(i, k, total):
        own[i, k] = total.astype(own.dtype)

    def ahead(k):
        for way in range(2):
            put(4 + way, k, take(4 + way, k))
            to_row(way, k).start()

    def partial(i, k, first):
        total = take(i, k)
        if i < 2:
            to_row(i, k).wait_recv()
            total = total + over[i, k].astype(f32)
        if not first:
            ring(i, k - 1).wait_recv()
            total = total + arrive[i, k - 1].astype(f32)
        return total

    ahead(0)
    line_send[0] = line_ref[block(0, 0)]
    line_ring(0).start()
    ahead(1)
    for i in (2, 3, 0, 1):
        put(i, 0, partial(i, 0, True))
        ring(i, 0).start()

    def step(k, carry):
        ahead(k + 1)
        for i in (2, 3, 0, 1):
            put(i, k, partial(i, k, False))
            ring(i, k).start()
        line_ring(k - 1).wait_recv()
        line_send[k] = line_ref[block(0, k)] + line_got[k - 1]
        line_ring(k).start()
        return carry

    lax.fori_loop(1, n - 1, step, 0)

    def end_row(i, k=None):
        if i < 2:
            view = sums.at[i, 2 * core + row]
            return remote(view, view, end_row_s.at[i], end_row_r.at[i], across)
        return remote(
            own.at[i, n - 1], other.at[i - 2], end_row_s.at[i], end_row_r.at[i], across
        )

    def end_core(j, side, part):
        view = sums.at[side, part]
        return remote(view, view, end_core_s.at[j], end_core_r.at[j], partner)

    for i in (2, 3):
        put(i, n - 1, partial(i, n - 1, False))
        end_row(i).start()
    line_ring(n - 2).wait_recv()
    line_pair[0] = line_ref[me] + line_got[n - 2]
    pair_row = remote(line_pair.at[0], line_pair.at[1], pair_s.at[0], pair_r.at[0], across)
    pair_row.start()
    for way in (0, 1):
        sums[way, 2 * core + row] = partial(way, n - 1, False).astype(sums.dtype)
        end_row(way).start()
        end_core(way, way, 2 * core + row).start()
    pair_row.wait()
    line_pair[2] = line_pair[0] + line_pair[1]
    pair_core = remote(line_pair.at[2], line_pair.at[3], pair_s.at[1], pair_r.at[1], partner)
    pair_core.start()
    for way in (0, 1):
        end_row(2 + way).wait_recv()
        total = own[2 + way, n - 1].astype(f32) + other[way].astype(f32)
        sums[2, 2 * core + way] = total.astype(sums.dtype)
        end_core(2 + way, 2, 2 * core + way).start()
    for way in (0, 1):
        end_row(way).wait_recv()
        end_core(4 + way, way, 2 * core + 1 - row).start()
    pair_core.wait()
    line_out[...] = line_pair[2] + line_pair[3]
    for i in range(4):
        end_row(i).wait_send()
    for j in range(6):
        copy = end_core(j, 0, 0)
        copy.wait_send()
        copy.wait_recv()

    def finish(k, carry):
        for i in range(6):
            give(i, k)(source(i, k, core)[0][1]).wait_send()
        for way in range(2):
            to_row(way, k).wait_send()
        return carry

    lax.fori_loop(0, n, finish, 0)

    def finish_ring(k, carry):
        for i in range(4):
            ring(i, k).wait_send()
        line_ring(k).wait_send()
        return carry

    lax.fori_loop(0, n - 1, finish_ring, 0)


def reduce_all(arrays, n, width):
    dma = pltpu.SemaphoreType.DMA
    vmem = pltpu.VMEM
    rows = arrays[0].shape[1]
    low = arrays[0].dtype
    line = arrays[-1].shape[1:]
    anywhere = pl.BlockSpec(memory_space=pl.ANY)
    near = pl.BlockSpec(memory_space=pltpu.VMEM)
    return pl.pallas_call(
        functools.partial(reduce_kernel, n, width),
        out_shape=[
            jax.ShapeDtypeStruct((3, 4, rows, width), low),
            jax.ShapeDtypeStruct(line, jnp.float32),
        ],
        in_specs=[anywhere] * 4 + [near],
        out_specs=[near, near],
        scratch_shapes=[
            vmem((6, n, rows, width), low),
            vmem((6, n, rows, width), low),
            vmem((4, n - 1, rows, width), low),
            vmem((2, n, rows, width), low),
            vmem((2, rows, width), low),
            vmem((n - 1,) + line, jnp.float32),
            vmem((n - 1,) + line, jnp.float32),
            vmem((4,) + line, jnp.float32),
            dma((6, n)),
            dma((6, n)),
            dma((6, n)),
            dma((4, n - 1)),
            dma((4, n - 1)),
            dma((2, n)),
            dma((2, n)),
            dma((4,)),
            dma((4,)),
            dma((6,)),
            dma((6,)),
            dma((n - 1,)),
            dma((n - 1,)),
            dma((2,)),
            dma((2,)),
        ],
        compiler_params=pltpu.CompilerParams(
            collective_id=1, has_side_effects=True, vmem_limit_bytes=56 * 1024 * 1024
        ),
        name="reduce_all",
    )(*arrays)


def per_device_in_parts(n, layer_input, cotangent, live, *params):
    width = params[0].shape[0] * n
    rows = params[0].shape[0]
    matrices = [i for i, p in enumerate(params) if p.ndim == 2]
    vectors = [i for i, p in enumerate(params) if p.ndim == 1]
    shapes = [params[i].shape for i in matrices]
    assert shapes == [(rows, 3 * width), (rows, width), (rows, 4 * width), (4 * rows, width)]
    lengths = [params[i].shape[0] for i in vectors]
    tall = -(-sum(lengths) // (16 * LANES)) * 16
    spare = tall * LANES - sum(lengths)

    line = jnp.concatenate([params[i] for i in vectors] + [jnp.zeros(spare, params[0].dtype)])
    sent = [params[i] for i in matrices]
    sent[3] = sent[3].reshape(4, rows, width)
    *full, lines = gather_all(sent + [line.reshape(tall, LANES)], n, width)
    gathered = [None] * len(params)
    for i, array in zip(matrices, full):
        gathered[i] = array.reshape(n * params[i].shape[0], params[i].shape[1])
    tail = lines.reshape(n, -1)
    at = 0
    for i, length in zip(vectors, lengths):
        gathered[i] = tail[:, at : at + length].reshape(-1)
        at += length

    output, saved = forward_pass(gathered, layer_input, live)
    input_grad, grads = backward_pass(gathered, saved, cotangent)

    low = jnp.bfloat16
    blocks = [grads[i].astype(low).reshape((n,) + a.shape) for i, a in zip(matrices, sent)]
    parts = [grads[i].reshape(n, -1) for i in vectors] + [jnp.zeros((n, spare), jnp.float32)]
    blocks.append(jnp.concatenate(parts, axis=1).reshape(n, tall, LANES))
    sums, tail = reduce_all(blocks, n, width)

    def joined(pieces):
        return jnp.swapaxes(pieces, 0, 1).reshape(rows, -1).astype(jnp.float32)

    results = [None] * len(params)
    whole = (
        joined(sums[0, :3]),
        sums[0, 3].astype(jnp.float32),
        joined(sums[1]),
        sums[2].reshape(4 * rows, width).astype(jnp.float32),
    )
    for i, array in zip(matrices, whole):
        results[i] = array
    tail = tail.reshape(-1)
    at = 0
    for i, length in zip(vectors, lengths):
        results[i] = tail[at : at + length]
        at += length
    return (output, input_grad, *results)


VECTOR_ROWS = (0, 1, 2, 3, 4, 5, 6, 8, 7)


def finish_kernel(rows, layout, packed, *refs):
    streams_out, wide_out, vectors_out, wide, streams, (low, in_sem, out_sem) = split(
        refs, (2, 4, 9, 4, 2, 3)
    )
    place = {}
    for i, (name, first, high, left, width) in enumerate(layout):
        view = pl.ds(first, high), pl.ds(0, width)
        copy = pltpu.make_async_copy(packed.at[view], low.at[view], in_sem.at[i])
        copy.start()
        place.setdefault(name, []).append((copy, first, high, left, width))
    store = [
        pltpu.make_async_copy(source, target, out_sem.at[i])
        for i, (source, target) in enumerate(zip((*wide, *streams), (*wide_out, *streams_out)))
    ]
    for m in (DOWN, UP, QKV, OUT):
        for copy, first, high, left, width in place[("FQ", "FO", "FU", "FD")[m]]:
            copy.wait()
            wide[m][:, left : left + width] = low[first : first + high, :].astype(F32)
        store[m].start()
    for i, name in enumerate(("c", "fn")):
        copy, first, high, _, _ = place[name][0]
        copy.wait()
        streams[i][0] = low[first : first + high, :][: streams[i].shape[1]]
        store[4 + i].start()
    copy, first, high, _, _ = place["tf"][0]
    copy.wait()
    line = low[first : first + high, :LANES].astype(F32)
    line = line + low[first : first + high, LANES : 2 * LANES].astype(F32)
    for i, ref in zip(VECTOR_ROWS, vectors_out):
        if i < 8:
            ref[...] = line[i, 0:rows]
        else:
            for e in range(4 * rows // LANES):
                ref[pl.ds(e * LANES, LANES)] = line[i + e, :]
    for copy in store:
        copy.wait()


def finish(packed, stream, matrices, vectors):
    rows, model = matrices[QKV].shape[0], stream.shape[2]
    layout = pack_layout(rows, -(-stream.shape[1] // 16) * 16, model)
    far = pl.BlockSpec(memory_space=pltpu.HBM)
    near = pl.BlockSpec(memory_space=pltpu.VMEM)
    shape = jax.ShapeDtypeStruct
    return pl.pallas_call(
        functools.partial(finish_kernel, rows, layout),
        out_shape=[shape(stream.shape, LOW)] * 2
        + [shape(a.shape, F32) for a in matrices]
        + [shape(a.shape, F32) for a in vectors],
        in_specs=[far],
        out_specs=[far] * 6 + [near] * 9,
        scratch_shapes=[pltpu.VMEM(a.shape, F32) for a in matrices]
        + [pltpu.VMEM(stream.shape, LOW)] * 2
        + [pltpu.VMEM(packed.shape, LOW)]
        + [pltpu.SemaphoreType.DMA((k,)) for k in (len(layout), 6)],
        compiler_params=pltpu.CompilerParams(vmem_limit_bytes=32 * 1024 * 1024),
        name="finish",
    )(packed)


def per_device(n, layer_input, cotangent, live, *params):
    rows = params[0].shape[0]
    if rows % 32 or rows > LANES or layer_input.shape[0] != 1:
        return per_device_in_parts(n, layer_input, cotangent, live, *params)
    matrices = [p for p in params if p.ndim == 2]
    vectors = [p for p in params if p.ndim == 1]
    packed = run_layer(layer_input, cotangent, live, matrices, vectors, n)
    done = finish(packed, layer_input, matrices, vectors)
    wide, tall = list(done[2:6]), list(done[6:])
    return (*done[:2], *((wide if p.ndim == 2 else tall).pop(0) for p in params))


def solution(mesh):
    whole = P(("rep", "shard"), None, None)
    vector, matrix = P("shard"), P("shard", None)
    ranks = (1, 1, 2, 1, 1, 2, 1, 1, 1, 2, 1, 2, 1)
    params = tuple(matrix if rank == 2 else vector for rank in ranks)
    return jax.shard_map(
        functools.partial(per_device, mesh.shape["shard"]),
        mesh=mesh,
        in_specs=(whole, whole, P(("rep", "shard"))) + params,
        out_specs=(whole, whole) + params,
        check_vma=False,
    )
```
